32 devices in a mesh: gx: 8 (over z, y), gy: 4 (over x, core).
Axes of the slice: x: 2, y: 2, z: 4, core: 2. Of those that a mesh axis runs over, the one named last changes fastest.
Arguments:
- level_set: float32 [16, 512, 512], P(None, 'gx', 'gy'), may hold values from -6 to 6
- speed_x: float32 [16, 512, 512], P(None, 'gx', 'gy'), may hold values from -1 to 1
- speed_y: float32 [16, 512, 512], P(None, 'gx', 'gy'), may hold values from -1 to 1
- cotangent: float32 [16, 512, 512], P(None, 'gx', 'gy'), may hold values from -6 to 6
- blocks: bfloat16 [8, 4, 36, 4096], P('gx', 'gy'), may hold values from -0.75 to 0.75
- tile_count: int32 [8, 4], P('gx', 'gy'), may hold values from 1 to 36, as said below
- source_tile: int32 [8, 4, 36], P('gx', 'gy'), may hold values from 0 to 127, as said below
- dest_offset: int32 [8, 4, 36], P('gx', 'gy'), may hold values from 0 to 8, as said below
- dest_tile: int32 [8, 4, 36], P('gx', 'gy'), may hold values from 0 to 127
Outputs:
- grad_level_set: float32 [16, 512, 512], P(None, 'gx', 'gy')
- grad_blocks: float32 [8, 4, 36, 4096], P('gx', 'gy')
The draws below stay inside these ranges and needn't reach their ends.
Inputs may be any that keep to these rules, and one draw needn't show every extreme that they name: `tile_count`: some device and its eight neighbours have all 36 slots live. `source_tile`: distinct within one device's list. `dest_offset`: each value occurs exactly 4 times among the 36 slots of one device.
All inputs are finite; a program needn't handle non-finite values.
Results may differ from the reference program's by a relative error of at most 0.0003.
Values sent between devices are 32-bit elements; how exact they have to be, the bound alone decides.
No kernel may reach another device: no remote copies, remote signals or barrier semaphores. Data moves between devices by JAX's collectives and lax.ppermute only.
A program may use at most 64 MiB of HBM per device.

```python
import jax
import jax.numpy as jnp
from jax import lax

TILE = 64
CX = 64
CY = 128
Z = 16
ROUTE_MOST = 4
NI = 36
TILES = 128
NX = 512
NY = 512
N_GX = 8
N_GY = 4


def draw_tile_count(key, part):
    base_key = jax.random.fold_in(key, 101)
    key_light, key_heavy, key_centre = jax.random.split(base_key, 3)
    lowest = max(NI // 8, 1)
    light_count = jax.random.randint(key_light, (N_GX, N_GY), lowest, NI // 2 + 1)
    heavy_device = jax.random.randint(key_heavy, (N_GX, N_GY), 0, 4) == 0
    centre = jax.random.randint(key_centre, (2,), 0, 1 << 20)
    row_gap = (jnp.arange(N_GX, dtype=jnp.int32) - centre[0] % N_GX) % N_GX
    col_gap = (jnp.arange(N_GY, dtype=jnp.int32) - centre[1] % N_GY) % N_GY
    near_row = (row_gap <= 1) | (row_gap >= N_GX - 1)
    near_col = (col_gap <= 1) | (col_gap >= N_GY - 1)
    near_centre = near_row[:, None] & near_col[None, :]
    return jnp.where(heavy_device | near_centre, NI, light_count).astype(jnp.int32)


def draw_source_tile(key, part):
    keys_all = jax.random.split(jax.random.fold_in(key, 202), N_GX * N_GY)
    orders = jax.vmap(lambda one_key: jax.random.permutation(one_key, TILES)[:NI])(keys_all)
    return orders.reshape(N_GX, N_GY, NI).astype(jnp.int32)


def draw_dest_offset(key, part):
    keys_all = jax.random.split(jax.random.fold_in(key, 303), N_GX * N_GY)
    labels = jnp.arange(9 * ROUTE_MOST, dtype=jnp.int32) // ROUTE_MOST
    orders = jax.vmap(lambda one_key: jax.random.permutation(one_key, labels))(keys_all)
    return orders.reshape(N_GX, N_GY, NI).astype(jnp.int32)


def set_ends(drawn, own_key, low, largest):
    shape = drawn.shape
    spot = [jax.random.randint(jax.random.fold_in(own_key, axis), (), 0, shape[axis]) for axis in range(len(shape))]
    drawn = drawn.at[tuple(spot)].set(low)
    longest = shape.index(max(shape))
    spot[longest] = (spot[longest] + 1) % shape[longest]
    return drawn.at[tuple(spot)].set(largest)


def level_of(key, extent, cuts, least, largest):
    def one(position, shards_of):
        steps = jax.random.uniform(jax.random.fold_in(jax.random.fold_in(key, 6), position), (shards_of,), jnp.float32, least / len(cuts), largest / len(cuts))
        return jnp.repeat(jnp.exp(steps), extent[position] // shards_of).reshape((-1,) + (1,) * (len(extent) - position - 1))

    loudness = one(*cuts[0])
    for cut in cuts[1:]:
        loudness = loudness * one(*cut)
    return loudness


def normal_values(rng, dims, scale, limit, cuts=(), kind=jnp.bfloat16):
    factor_of = level_of(rng, dims, cuts, -0.22, 0.18) if cuts else 1.0
    values = jax.random.normal(rng, dims, jnp.float32) * scale * factor_of
    return jnp.minimum(jnp.maximum(values, -limit), limit).astype(kind)


def setup_inputs(seed: int = 0) -> dict:
    seeds = jax.random.split(jax.random.key(seed), 10)
    level_set = normal_values(seeds[0], (Z, NX, NY), 1.0, 6.0, ((1, 8), (2, 4)), jnp.float32)
    speed_x = jnp.clip(jax.random.uniform(seeds[1], (Z, NX, NY), jnp.float32, -1.0, 1.0) * level_of(seeds[1], (Z, NX, NY), ((1, 8), (2, 4)), -0.4, 0.0), -1.0, 1.0)
    speed_y = jnp.clip(jax.random.uniform(seeds[2], (Z, NX, NY), jnp.float32, -1.0, 1.0) * level_of(seeds[2], (Z, NX, NY), ((1, 8), (2, 4)), -0.4, 0.0), -1.0, 1.0)
    cotangent = normal_values(seeds[3], (Z, NX, NY), 1.0, 6.0, ((1, 8), (2, 4)), jnp.float32)
    blocks = normal_values(seeds[4], (N_GX, N_GY, NI, TILE * TILE), TILE ** -0.5, 0.75, ((0, 8), (1, 4)))
    tile_count = draw_tile_count(jax.random.fold_in(seeds[9], 71), 0)
    source_tile = draw_source_tile(jax.random.fold_in(seeds[9], 71), 0)
    dest_offset = draw_dest_offset(jax.random.fold_in(seeds[9], 71), 0)
    dest_tile = set_ends(jax.random.randint(seeds[8], (N_GX, N_GY, NI), 0, TILES), jax.random.fold_in(seeds[8], 1), 0, TILES - 1).astype(jnp.int32)
    return {"level_set": level_set, "speed_x": speed_x, "speed_y": speed_y, "cotangent": cotangent, "blocks": blocks, "tile_count": tile_count, "source_tile": source_tile, "dest_offset": dest_offset, "dest_tile": dest_tile}


COEFFICIENTS = (2.0 / 60.0, -13.0 / 60.0, 47.0 / 60.0, 27.0 / 60.0, -3.0 / 60.0)
TIME_STEP = 0.3

def face_flux(field_in, face_speed, axis_dim):

    def neighbour(shift_by):
        return jnp.roll(field_in, -shift_by, axis=axis_dim)
    upwind_part = COEFFICIENTS[0] * neighbour(-2) + COEFFICIENTS[1] * neighbour(-1) + COEFFICIENTS[2] * neighbour(0) + COEFFICIENTS[3] * neighbour(1) + COEFFICIENTS[4] * neighbour(2)
    downwind_part = COEFFICIENTS[0] * neighbour(3) + COEFFICIENTS[1] * neighbour(2) + COEFFICIENTS[2] * neighbour(1) + COEFFICIENTS[3] * neighbour(0) + COEFFICIENTS[4] * neighbour(-1)
    return jnp.maximum(face_speed, 0.0) * upwind_part + jnp.minimum(face_speed, 0.0) * downwind_part

def advect(field_in, speed_x, speed_y):
    flux_x = face_flux(field_in, speed_x, 1)
    flux_y = face_flux(field_in, speed_y, 2)
    return -(flux_x - jnp.roll(flux_x, 1, axis=1)) - (flux_y - jnp.roll(flux_y, 1, axis=2))

def to_tiles(field_in):
    planes = field_in.shape[0]
    blocks_view = field_in.reshape(planes, N_GX, CX, N_GY, CY // TILE, TILE)
    return blocks_view.transpose(1, 3, 2, 4, 0, 5).reshape(N_GX, N_GY, TILES, planes, TILE)

def from_tiles(tile_array):
    planes = tile_array.shape[3]
    blocks_view = tile_array.reshape(N_GX, N_GY, CX, CY // TILE, planes, TILE)
    return blocks_view.transpose(4, 0, 2, 1, 3, 5).reshape(planes, NX, NY)

def extend(field_in, matrices, live_slots, source_tile, dest_offset, dest_tile):
    tile_array = to_tiles(field_in)
    grid_row = jnp.arange(N_GX, dtype=jnp.int32)[:, None, None]
    grid_col = jnp.arange(N_GY, dtype=jnp.int32)[None, :, None]
    picked = tile_array[grid_row, grid_col, source_tile]
    values = jnp.einsum('pqsab,pqszb->pqsza', matrices, picked, precision=lax.Precision.HIGHEST)
    values = values * live_slots[:, :, :, None, None]
    dest_row = (grid_row + dest_offset // 3 - 1) % N_GX
    dest_col = (grid_col + dest_offset % 3 - 1) % N_GY
    landed = jnp.zeros_like(tile_array).at[dest_row, dest_col, dest_tile].add(values)
    return from_tiles(landed)

def reference(level_set, speed_x, speed_y, cotangent, blocks, tile_count, source_tile, dest_offset, dest_tile):
    live_slots = (jnp.arange(NI, dtype=jnp.int32)[None, None, :] < tile_count[:, :, None]).astype(jnp.float32)

    def tendency(field_in, matrices):
        return advect(field_in, speed_x, speed_y) + extend(field_in, matrices, live_slots, source_tile, dest_offset, dest_tile)

    def final_state(field_in, flat_blocks):
        matrices = flat_blocks.reshape(N_GX, N_GY, NI, TILE, TILE)
        section = field_in + TIME_STEP * tendency(field_in, matrices)
        return 0.5 * field_in + 0.5 * (section + TIME_STEP * tendency(section, matrices))
    unused, pullback = jax.vjp(final_state, level_set, blocks.astype(jnp.float32))
    grad_level_set, grad_blocks = pullback(cotangent)
    return (grad_level_set, grad_blocks)
```

```python
import functools

import jax
import jax.numpy as jnp
from jax import lax
from jax.experimental import pallas as pl
from jax.experimental.pallas import tpu as pltpu
from jax.sharding import PartitionSpec as P

TILE = 64
ROUTE_MOST = 4
TIME_STEP = 0.3
WEIGHTS = (2.0 / 60.0, -13.0 / 60.0, 47.0 / 60.0, 27.0 / 60.0, -3.0 / 60.0)
PAD = 80
VMEM_LIMIT = 56 << 20

A, B, S = 0, 1, 2


def matching(count, which):
    return [(i, (i + (1 if (i % 2 == 0) == (which == B) else -1)) % count) for i in range(count)]


def exchange(block, axis, which):
    return lax.ppermute(block, axis, matching(lax.axis_size(axis), which))


def lanes(shape):
    return lax.broadcasted_iota(jnp.int32, shape, len(shape) - 1)


def roll(value, shift):
    return pltpu.roll(value, shift % 128 if isinstance(shift, int) else shift, axis=value.ndim - 1)


def split(value):
    high = value.astype(jnp.bfloat16)
    return high, (value - high.astype(jnp.float32)).astype(jnp.bfloat16)


def pair_dot(value, matrix, over):
    high, low = split(value)
    both = lax.dot_general(
        jnp.concatenate([high, low], axis=0),
        matrix,
        (((1,), (over,)), ((), ())),
        preferred_element_type=jnp.float32,
    )
    rows = value.shape[0]
    return both[:rows] + both[rows:]


def row_of(ref, x, planes, stride):
    return ref[pl.ds(x, planes, stride), :]


def tile_pair(ref, first, second, planes, extent_x):
    one = row_of(ref, first // 2, planes, extent_x)
    two = row_of(ref, second // 2, planes, extent_x)
    lane = lanes(one.shape)
    one = jnp.where(first % 2 == 0, one, roll(one, TILE))
    two = jnp.where(second % 2 == 1, two, roll(two, TILE))
    return jnp.where(lane < TILE, one, two)


def add_tile_pair(ref, first, second, value, planes, extent_x):
    lane = lanes(value.shape)
    turned = roll(value, TILE)
    for tile, half in ((first, 0), (second, 1)):
        spot = pl.ds(tile // 2, planes, extent_x)
        placed = jnp.where(tile % 2 == half, value, turned)
        keep = (lane // TILE) == tile % 2
        ref[spot, :] = ref[spot, :] + jnp.where(keep, placed, 0.0)


def edge_pack(ref, planes, extent_x):
    lane = lanes((extent_x, 128))
    packed = jnp.zeros((extent_x, 128), jnp.float32)
    for z in range(planes):
        plane = ref[z * extent_x : (z + 1) * extent_x, :]
        packed = jnp.where(lane // 8 == z, roll(plane, 8 * z + 3), packed)
    return packed


def edge_rows(ref, start, planes, extent_x):
    return jnp.concatenate([row_of(ref, start + j, planes, extent_x) for j in range(3)], axis=0)


def upwind(face_rate):
    return jnp.maximum(face_rate, 0.0), jnp.minimum(face_rate, 0.0)


UP = {2: WEIGHTS[0], 1: WEIGHTS[1], 0: WEIGHTS[2], -1: WEIGHTS[3], -2: WEIGHTS[4]}
DOWN = {1: WEIGHTS[4], 0: WEIGHTS[3], -1: WEIGHTS[2], -2: WEIGHTS[1], -3: WEIGHTS[0]}


def combine(up_part, down_part, k):
    total = 0.0
    if k in UP:
        total = total + UP[k] * up_part
    if k in DOWN:
        total = total + DOWN[k] * down_part
    return total


def fill_padded(pad_ref, field_ref, rows_a, rows_b, even, planes, extent_x):
    high = 8 + extent_x
    at_a = jnp.where(even, 5, high)
    at_b = jnp.where(even, high, 5)
    for z in range(planes):
        pad_ref[z * PAD + 8 : z * PAD + high, :] = field_ref[z * extent_x : (z + 1) * extent_x, :]
    for j in range(3):
        part = slice(j * planes, (j + 1) * planes)
        pad_ref[pl.ds(at_a + j, planes, PAD), :] = rows_a[part]
        pad_ref[pl.ds(at_b + j, planes, PAD), :] = rows_b[part]


def edge_join(from_a, from_b, even):
    low = jnp.where(even, from_a, from_b)
    high = jnp.where(even, from_b, from_a)
    return jnp.where(lanes(low.shape) % 8 < 3, low, high)


def adjoint_edges(own, halo, own_rate, halo_rate):
    lane = lanes(own.shape) % 8
    after = roll(jnp.where(lane == 3, own, halo), -1)
    before = roll(jnp.where(lane == 2, own, halo), 1)
    jump = jnp.where(lane < 3, after - halo, halo - before)
    rate = jnp.where(lane < 3, halo_rate, roll(jnp.where(lane == 2, own_rate, halo_rate), 1))
    rate_up, rate_down = upwind(rate)
    up_part, down_part = rate_up * jump, rate_down * jump
    low_side = 0.0
    high_side = 0.0
    for k in (-1, -2, -3):
        part = jnp.where(lane < 3, combine(up_part, down_part, k), 0.0)
        low_side = low_side + roll(part, -k)
    for k in (0, 1, 2):
        part = jnp.where((lane >= 3) & (lane < 6), combine(up_part, down_part, k), 0.0)
        high_side = high_side + roll(part, -(k + 1))
    return jnp.where(lane < 3, high_side, jnp.where(lane < 6, low_side, 0.0))


def adjoint_plane(z, pad_ref, pad_rate_ref, rate_y_ref, edges, up_ref, down_ref, extent_x):
    base = pl.multiple_of(z * PAD, 8)
    here = pad_ref[pl.ds(base, PAD), :]
    jump = pad_ref[pl.ds(base + 1, PAD), :] - here
    rate_up, rate_down = upwind(pad_rate_ref[pl.ds(base, PAD), :])
    up_ref[pl.ds(base, PAD), :] = rate_up * jump
    down_ref[pl.ds(base, PAD), :] = rate_down * jump
    total = 0.0
    for k in range(-3, 3):
        if k in UP:
            total = total + UP[k] * up_ref[pl.ds(base + 8 + k, extent_x), :]
        if k in DOWN:
            total = total + DOWN[k] * down_ref[pl.ds(base + 8 + k, extent_x), :]
    field = pad_ref[pl.ds(base + 8, extent_x), :]
    lane = lanes(field.shape)
    jump = jnp.where(lane == 127, 0.0, roll(field, -1) - field)
    rate_up, rate_down = upwind(rate_y_ref[pl.ds(pl.multiple_of(z * extent_x, 8), extent_x), :])
    up_part, down_part = rate_up * jump, rate_down * jump
    ahead = combine(up_part, down_part, 2)
    for k in (1, 0):
        ahead = jnp.where(lane == 127, 0.0, roll(ahead, -1)) + combine(up_part, down_part, k)
    behind = combine(up_part, down_part, -3)
    for k in (-2, -1):
        behind = jnp.where(lane == 0, 0.0, roll(behind, 1)) + combine(up_part, down_part, k)
    behind = jnp.where(lane == 0, 0.0, roll(behind, 1))
    rim = roll(edges, 125 - 8 * z)
    return total + ahead + behind + jnp.where((lane < 3) | (lane >= 125), rim, 0.0)


def dim(ref):
    return ref.shape[0]


def begin_body(info, count, heading, target, source, field, cotan, rate_x, rate_y, order, rows_a, rows_b, packs, used, *, planes, extent_x):
    slots = heading.shape[0]
    for label in range(9):
        used[label] = 0
    lane = lanes((8, 128))

    def place(slot, asked):
        toward = heading[slot]
        flip_x = 1 - 2 * info[0]
        flip_y = 1 - 2 * info[1]
        ex = (toward // 3 - 1) * flip_x
        ey = (lax.rem(toward, 3) - 1) * flip_y
        lx = jnp.where(ex == 0, 2, (ex + 1) // 2)
        ly = jnp.where(ey == 0, 2, (ey + 1) // 2)
        label = ly * 3 + lx
        spot = label * ROUTE_MOST + used[label]
        used[label] = used[label] + 1
        alive = slot < count[0]
        order[0, spot] = slot
        order[1, spot] = source[slot]
        order[2, spot] = alive.astype(jnp.int32)
        wanted = jnp.where(alive, target[slot], 0)
        return jnp.where(lane == spot, wanted, asked)

    asked = lax.fori_loop(0, slots, place, jnp.zeros((8, 128), jnp.int32))
    asked = asked.astype(jnp.float32)
    even = info[0] == 0
    high = extent_x - 3
    for rows, start in ((rows_a, jnp.where(even, 0, high)), (rows_b, jnp.where(even, high, 0))):
        rows[0:8, :] = asked
        for number, ref in enumerate((cotan, rate_x, field)):
            first = 8 + number * 3 * planes
            rows[first : first + 3 * planes, :] = edge_rows(ref, start, planes, extent_x)
    for number, ref in enumerate((cotan, rate_y, field)):
        packs[number * extent_x : (number + 1) * extent_x, :] = edge_pack(ref, planes, extent_x)


def extend_body(order, field, blocks, pairs, picked, values, *, planes, extent_x):
    def one(number, carry):
        first, second = order[0, 2 * number], order[0, 2 * number + 1]
        one_block, two_block = blocks[first], blocks[second]
        zero = jnp.zeros_like(one_block)
        joined = jnp.concatenate(
            [jnp.concatenate([one_block, zero], axis=1), jnp.concatenate([zero, two_block], axis=1)], axis=0
        )
        pairs[number] = joined
        tiles = tile_pair(field, order[1, 2 * number], order[1, 2 * number + 1], planes, extent_x)
        picked[number] = tiles
        lane = lanes(tiles.shape)
        alive = jnp.where(lane < TILE, order[2, 2 * number], order[2, 2 * number + 1])
        values[number] = pair_dot(jnp.where(alive == 1, tiles, 0.0), joined, 1)
        return carry

    lax.fori_loop(0, pairs.shape[0], one, 0)


def gather_tiles(asked, field, outs, planes, extent_x):
    for ly in range(3):
        for lx in range(3):
            label = ly * 3 + lx
            for half in range(2):
                first = asked[label, label * ROUTE_MOST + 2 * half]
                second = asked[label, label * ROUTE_MOST + 2 * half + 1]
                outs[ly](lx, half, tile_pair(field, first, second, planes, extent_x))


def serve_body(asked, field, values, out_a, out_b, out_s, *, planes, extent_x):
    outs = (out_a, out_b, out_s)

    def writer(out):
        def write(lx, half, tiles):
            out[lx, half * planes : (half + 1) * planes, :] = tiles

        return write

    gather_tiles(asked, field, [writer(out) for out in outs], planes, extent_x)
    for ly, out in enumerate(outs):
        for lx in range(3):
            for half in range(2):
                out[3 + lx, half * planes : (half + 1) * planes, :] = values[(ly * 3 + lx) * 2 + half]


def landed(lx, ly, half, planes, shift, x_a, x_b, y_a, y_b, own):
    rows = slice(half * planes, (half + 1) * planes)
    if lx == S:
        return (y_a, y_b, own)[ly][shift + S, rows, :]
    return (x_a, x_b)[lx][shift + (1, 2, 0)[ly], rows, :]


def middle_body(
    info, order, asked, cotan, rate_x, rate_y, rows_a, rows_b, packs, packs_a, packs_b, x_a, x_b, y_a, y_b, own, pairs,
    grad, pad_grad_rate, edge_rate, returned, send_a, send_b, send_s, send_rows_a, send_rows_b,
    pad, up_ref, down_ref, *, planes, extent_x,
):
    even_x, even_y = info[0] == 0, info[1] == 0
    rows = 3 * planes
    fill_padded(pad, cotan, rows_a[8 : 8 + rows], rows_b[8 : 8 + rows], even_x, planes, extent_x)
    fill_padded(
        pad_grad_rate, rate_x, rows_a[8 + rows : 8 + 2 * rows], rows_b[8 + rows : 8 + 2 * rows], even_x, planes, extent_x
    )
    part = lambda ref, number, first: ref[first + number * extent_x : first + (number + 1) * extent_x]
    halo = edge_join(part(packs_a, 0, 24), part(packs_b, 0, 24), even_y)
    halo_rate = edge_join(part(packs_a, 1, 24), part(packs_b, 1, 24), even_y)
    edge_rate[...] = halo_rate
    edges = adjoint_edges(part(packs, 0, 0), halo, part(packs, 1, 0), halo_rate)

    def plane(z, carry):
        spot = pl.ds(pl.multiple_of(z * extent_x, 8), extent_x)
        pulled = adjoint_plane(z, pad, pad_grad_rate, rate_y, edges, up_ref, down_ref, extent_x)
        grad[spot, :] = 0.5 * cotan[spot, :] + (0.5 * TIME_STEP) * pulled
        return carry

    lax.fori_loop(0, planes, plane, 0)
    for ly in range(3):
        for lx in range(3):
            for half in range(2):
                number = (ly * 3 + lx) * 2 + half
                back = landed(lx, ly, half, planes, 0, x_a, x_b, y_a, y_b, own)
                lane = lanes(back.shape)
                alive = jnp.where(lane < TILE, order[2, 2 * number], order[2, 2 * number + 1])
                back = jnp.where(alive == 1, back, 0.0)
                returned[number] = back
                pulled = (0.5 * TIME_STEP) * pair_dot(back, pairs[number], 0)
                add_tile_pair(grad, order[1, 2 * number], order[1, 2 * number + 1], pulled, planes, extent_x)
    packed = edge_pack(grad, planes, extent_x)
    outs = (send_a, send_b, send_s)

    def writer(out):
        def write(lx, half, tiles):
            first = extent_x + (lx * 2 + half) * planes
            out[first : first + planes, :] = tiles

        return write

    for out in outs:
        out[0:extent_x, :] = packed
    gather_tiles(asked, grad, [writer(out) for out in outs], planes, extent_x)
    high = extent_x - 3
    send_rows_a[...] = edge_rows(grad, jnp.where(even_x, 0, high), planes, extent_x)
    send_rows_b[...] = edge_rows(grad, jnp.where(even_x, high, 0), planes, extent_x)


def section_body(
    info, order, asked, field, pad_rate, rate_y, packs, packs_a, packs_b, rows_a, rows_b, x_a, x_b, y_a, y_b, own,
    picked, pad, section, flux_ref, *, planes, extent_x,
):
    even_x, even_y = info[0] == 0, info[1] == 0
    rows = 3 * planes
    first = 8 + 2 * rows
    fill_padded(pad, field, rows_a[first : first + rows], rows_b[first : first + rows], even_x, planes, extent_x)
    part = lambda ref, number, first: ref[first + number * extent_x : first + (number + 1) * extent_x]
    halo = edge_join(part(packs_a, 2, 24), part(packs_b, 2, 24), even_y)
    own_edge = part(packs, 2, 0)
    halo_rate = edge_join(part(packs_a, 1, 24), part(packs_b, 1, 24), even_y)
    lane8 = lanes(halo.shape) % 8
    line = jnp.where(lane8 < 3, halo, own_edge)
    moved = {k: roll(line, -k) for k in range(-2, 4)}
    rate_up, rate_down = upwind(halo_rate)
    flux_low = rate_up * sum(WEIGHTS[j] * moved[j - 2] for j in range(5)) + rate_down * sum(
        WEIGHTS[j] * moved[3 - j] for j in range(5)
    )

    def plane(z, carry):
        base = pl.multiple_of(z * PAD, 8)
        spot = pl.ds(pl.multiple_of(z * extent_x, 8), extent_x)
        window = extent_x + 8
        near = {k: pad[pl.ds(base + 7 + k, window), :] for k in range(-2, 4)}
        rate_up, rate_down = upwind(pad_rate[pl.ds(base + 7, window), :])
        flux_ref[pl.ds(base, window), :] = rate_up * sum(WEIGHTS[j] * near[j - 2] for j in range(5)) + rate_down * sum(
            WEIGHTS[j] * near[3 - j] for j in range(5)
        )
        change = flux_ref[pl.ds(base, extent_x), :] - flux_ref[pl.ds(base + 1, extent_x), :]
        here = field[spot, :]
        lane = lanes(here.shape)
        turn = 125 - 8 * z
        rim = roll(halo, turn)
        near = {0: here}
        for k in (1, 2, 3):
            near[k] = roll(jnp.where(lane < k, rim, here), -k)
        for k in (1, 2):
            near[-k] = roll(jnp.where(lane >= 128 - k, rim, here), k)
        rate_up, rate_down = upwind(rate_y[spot, :])
        flux = rate_up * sum(WEIGHTS[j] * near[j - 2] for j in range(5)) + rate_down * sum(
            WEIGHTS[j] * near[3 - j] for j in range(5)
        )
        change = change + roll(jnp.where(lane == 127, roll(flux_low, turn), flux), 1) - flux
        section[spot, :] = here + TIME_STEP * change
        return carry

    lax.fori_loop(0, planes, plane, 0)
    for ly in range(3):
        for lx in range(3):
            label = ly * 3 + lx
            for half in range(2):
                came = landed(lx, ly, half, planes, 3, x_a, x_b, y_a, y_b, own)
                at = label * ROUTE_MOST + 2 * half
                add_tile_pair(section, asked[label, at], asked[label, at + 1], TIME_STEP * came, planes, extent_x)

    def pick(number, carry):
        picked[number] = tile_pair(section, order[1, 2 * number], order[1, 2 * number + 1], planes, extent_x)
        return carry

    lax.fori_loop(0, picked.shape[0], pick, 0)


def last_body(
    info, order, cotan, grad, pad_rate, rate_y, edge_rate, packs, own, y_a, y_b, x_a, x_b, pairs, returned,
    picked_start, picked_section, out, out_blocks,
    pad, up_ref, down_ref, work, *, planes, extent_x,
):
    even_x, even_y = info[0] == 0, info[1] == 0
    rows = 3 * planes
    fill_padded(pad, grad, x_a[0:rows], x_b[0:rows], even_x, planes, extent_x)
    halo = edge_join(y_a[0:extent_x], y_b[0:extent_x], even_y)
    edges = adjoint_edges(own[0:extent_x], halo, packs[extent_x : 2 * extent_x], edge_rate[...])

    def plane(z, carry):
        spot = pl.ds(pl.multiple_of(z * extent_x, 8), extent_x)
        pulled = adjoint_plane(z, pad, pad_rate, rate_y, edges, up_ref, down_ref, extent_x)
        out[spot, :] = 0.5 * cotan[spot, :] + grad[spot, :] + TIME_STEP * pulled
        return carry

    lax.fori_loop(0, planes, plane, 0)
    half_lane = lanes((TILE // 2, 128)) < TILE
    for ly in range(3):
        for lx in range(3):
            for half in range(2):
                number = (ly * 3 + lx) * 2 + half
                if lx == S:
                    ref, first = (y_a, y_b, own)[ly], extent_x + (S * 2 + half) * planes
                else:
                    ref, first = (x_a, x_b)[lx], rows + ((1, 2, 0)[ly] * 2 + half) * planes
                back = ref[first : first + planes, :]
                lane = lanes(back.shape)
                alive = jnp.where(lane < TILE, order[2, 2 * number], order[2, 2 * number + 1])
                back = jnp.where(alive == 1, back, 0.0)
                pulled = TIME_STEP * pair_dot(back, pairs[number], 0)
                add_tile_pair(out, order[1, 2 * number], order[1, 2 * number + 1], pulled, planes, extent_x)
                left = jnp.concatenate([(0.5 * TIME_STEP) * returned[number], TIME_STEP * back], axis=0)
                right = jnp.concatenate([picked_section[number], picked_start[number]], axis=0)
                left_high, left_low = split(left)
                right_high, right_low = split(right)
                outer = lax.dot_general(
                    jnp.concatenate([left_high, left_high, left_low], axis=0),
                    jnp.concatenate([right_high, right_low, right_high], axis=0),
                    (((0,), (0,)), ((), ())),
                    preferred_element_type=jnp.float32,
                )
                work[number] = outer
                for which in range(2):
                    slot = order[0, 2 * number + which]
                    even_rows = work[number, pl.ds(which * TILE, TILE // 2, 2), :]
                    odd_rows = work[number, pl.ds(which * TILE + 1, TILE // 2, 2), :]
                    if which == 0:
                        merged = jnp.where(half_lane, even_rows, roll(odd_rows, TILE))
                    else:
                        merged = jnp.where(half_lane, roll(even_rows, TILE), odd_rows)
                    out_blocks[pl.ds((slot // 8) * 256 + slot % 8, TILE // 2, 8), :] = merged


def call(body, ins, outs, scratch=(), smem_in=0, smem_out=0, **sizes):
    vmem = pl.BlockSpec(memory_space=pltpu.VMEM)
    smem = pl.BlockSpec(memory_space=pltpu.SMEM)
    return pl.pallas_call(
        functools.partial(body, **sizes),
        out_shape=tuple(jax.ShapeDtypeStruct(shape, kind) for shape, kind in outs),
        in_specs=[smem] * smem_in + [vmem] * (len(ins) - smem_in),
        out_specs=tuple([smem] * smem_out + [vmem] * (len(outs) - smem_out)),
        scratch_shapes=list(scratch),
        compiler_params=pltpu.CompilerParams(vmem_limit_bytes=VMEM_LIMIT),
        name=body.__name__,
    )(*ins)


def shards(
    level_set, speed_x, speed_y, cotangent, blocks, tile_count, source_tile, dest_offset, dest_tile
):
    planes, extent_x, extent_y = level_set.shape
    slots = source_tile.shape[2]
    cells = planes * extent_x
    f32, i32 = jnp.float32, jnp.int32
    field, rate_x, rate_y, cotan = (v.reshape(cells, extent_y) for v in (level_set, speed_x, speed_y, cotangent))
    info = jnp.stack([lax.axis_index("gx") % 2, lax.axis_index("gy") % 2]).astype(i32)
    sizes = dict(planes=planes, extent_x=extent_x)
    rows = 3 * planes
    pair_total = slots // 2
    padded = pltpu.VMEM((planes * PAD + 8, extent_y), f32)

    order, rows_a, rows_b, packs = call(
        begin_body,
        (info, tile_count.reshape(1), dest_offset.reshape(slots), dest_tile.reshape(slots), source_tile.reshape(slots),
         field, cotan, rate_x, rate_y),
        [((3, slots), i32), ((8 + 3 * rows, extent_y), f32), ((8 + 3 * rows, extent_y), f32), ((3 * extent_x, extent_y), f32)],
        scratch=(pltpu.SMEM((9,), i32),), smem_in=5, smem_out=1, **sizes,
    )
    got_rows_a = exchange(rows_a, "gx", A)
    got_rows_b = exchange(rows_b, "gx", B)
    column = jnp.concatenate([rows_a[:8], got_rows_a[:8], got_rows_b[:8], packs], axis=0)
    got_packs_a = exchange(column, "gy", A)
    got_packs_b = exchange(column, "gy", B)

    pairs, picked_start, values = call(
        extend_body,
        (order, field, blocks.reshape(slots, TILE, TILE)),
        [((pair_total, 128, 128), jnp.bfloat16), ((pair_total, planes, 128), f32), ((pair_total, planes, 128), f32)],
        smem_in=1, **sizes,
    )

    asked = jnp.concatenate(
        [got_packs_a[8:9], got_packs_a[16:17], got_packs_a[0:1],
         got_packs_b[8:9], got_packs_b[16:17], got_packs_b[0:1],
         column[8:9], column[16:17], column[0:1]], axis=0,
    ).astype(i32)
    box = ((6, 2 * planes, 128), f32)
    out_a, out_b, own = call(serve_body, (asked, cotan, values), [box, box, box], smem_in=1, **sizes)
    y_a = exchange(out_a, "gy", A)
    y_b = exchange(out_b, "gy", B)
    forward = lambda m: jnp.stack([own[m], y_a[m], y_b[m], own[3 + m], y_a[3 + m], y_b[3 + m]])
    x_a = exchange(forward(A), "gx", A)
    x_b = exchange(forward(B), "gx", B)

    send = ((extent_x + 6 * planes, 128), f32)
    grad, pad_rate, edge_rate, returned, send_a, send_b, send_s, send_rows_a, send_rows_b = call(
        middle_body,
        (info, order, asked, cotan, rate_x, rate_y, got_rows_a, got_rows_b, packs, got_packs_a, got_packs_b,
         x_a, x_b, y_a, y_b, own, pairs),
        [((cells, 128), f32), ((planes * PAD + 8, 128), f32), ((extent_x, 128), f32), ((pair_total, planes, 128), f32),
         send, send, send, ((rows, 128), f32), ((rows, 128), f32)],
        scratch=(padded, padded, padded), smem_in=3, **sizes,
    )
    last_y_a = exchange(send_a, "gy", A)
    last_y_b = exchange(send_b, "gy", B)

    def onward(edge, m):
        first = extent_x + m * 2 * planes
        part = slice(first, first + 2 * planes)
        return jnp.concatenate([edge, send_s[part], last_y_a[part], last_y_b[part]], axis=0)

    last_x_a = exchange(onward(send_rows_a, A), "gx", A)
    last_x_b = exchange(onward(send_rows_b, B), "gx", B)

    (picked_section,) = call(
        section_body,
        (info, order, asked, field, pad_rate, rate_y, packs, got_packs_a, got_packs_b, got_rows_a, got_rows_b,
         x_a, x_b, y_a, y_b, own),
        [((pair_total, planes, 128), f32)],
        scratch=(padded, pltpu.VMEM((cells, 128), f32), padded), smem_in=3, **sizes,
    )
    row_tiles = -(-slots // 8)
    grad_level_set, grad_blocks = call(
        last_body,
        (info, order, cotan, grad, pad_rate, rate_y, edge_rate, packs, send_s, last_y_a, last_y_b, last_x_a, last_x_b,
         pairs, returned, picked_start, picked_section),
        [((cells, 128), f32), ((row_tiles * 256, 128), f32)],
        scratch=(padded, padded, padded, pltpu.VMEM((pair_total, 128, 128), f32)), smem_in=2, **sizes,
    )
    grad_blocks = grad_blocks.reshape(row_tiles, TILE // 2, 8, 128).transpose(0, 2, 1, 3)
    grad_blocks = grad_blocks.reshape(row_tiles * 8, TILE * TILE)[:slots]
    return (grad_level_set.reshape(planes, extent_x, extent_y), grad_blocks.reshape(1, 1, slots, TILE * TILE))


def solution(mesh):
    return jax.shard_map(
        shards,
        mesh=mesh,
        in_specs=(
            P(None, "gx", "gy"),
            P(None, "gx", "gy"),
            P(None, "gx", "gy"),
            P(None, "gx", "gy"),
            P("gx", "gy", None, None),
            P("gx", "gy"),
            P("gx", "gy", None),
            P("gx", "gy", None),
            P("gx", "gy", None),
        ),
        out_specs=(P(None, "gx", "gy"), P("gx", "gy", None, None)),
        check_vma=False,
    )
```

```python
import functools

import jax
import jax.numpy as jnp
from jax import lax
from jax.experimental import pallas as pl
from jax.experimental.pallas import tpu as pltpu
from jax.sharding import PartitionSpec as P

TILE = 64
ROUTE_MOST = 4
TIME_STEP = 0.3
WEIGHTS = (2.0 / 60.0, -13.0 / 60.0, 47.0 / 60.0, 27.0 / 60.0, -3.0 / 60.0)
PAD = 80
VMEM_LIMIT = 16 << 20
UNROLL = 2

A, B, S = 0, 1, 2


def matching(count, which):
    return [(i, (i + (1 if (i % 2 == 0) == (which == B) else -1)) % count) for i in range(count)]


def exchange(block, axis, which):
    return lax.ppermute(block, axis, matching(lax.axis_size(axis), which))


def lanes(shape):
    return lax.broadcasted_iota(jnp.int32, shape, len(shape) - 1)


def roll(value, shift):
    return pltpu.roll(value, shift % 128 if isinstance(shift, int) else shift, axis=value.ndim - 1)


def split(value):
    high = value.astype(jnp.bfloat16)
    return high, (value - high.astype(jnp.float32)).astype(jnp.bfloat16)


def pair_dot(value, matrix, over):
    high, low = split(value)
    both = lax.dot_general(
        jnp.concatenate([high, low], axis=0),
        matrix,
        (((1,), (over,)), ((), ())),
        preferred_element_type=jnp.float32,
    )
    rows = value.shape[0]
    return both[:rows] + both[rows:]


def row_of(ref, x, planes, stride):
    return ref[pl.ds(x, planes, stride), :]


def tile_pair(ref, first, second, planes, extent_x):
    one = row_of(ref, first // 2, planes, extent_x)
    two = row_of(ref, second // 2, planes, extent_x)
    lane = lanes(one.shape)
    one = jnp.where(first % 2 == 0, one, roll(one, TILE))
    two = jnp.where(second % 2 == 1, two, roll(two, TILE))
    return jnp.where(lane < TILE, one, two)


def add_tile_pair(ref, first, second, value, planes, extent_x):
    lane = lanes(value.shape)
    turned = roll(value, TILE)
    for tile, half in ((first, 0), (second, 1)):
        spot = pl.ds(tile // 2, planes, extent_x)
        placed = jnp.where(tile % 2 == half, value, turned)
        keep = (lane // TILE) == tile % 2
        ref[spot, :] = ref[spot, :] + jnp.where(keep, placed, 0.0)


def edge_pack(ref, planes, extent_x):
    lane = lanes((extent_x, 128))
    packed = jnp.zeros((extent_x, 128), jnp.float32)
    for z in range(planes):
        plane = ref[z * extent_x : (z + 1) * extent_x, :]
        packed = jnp.where(lane // 8 == z, roll(plane, 8 * z + 3), packed)
    return packed


def edge_rows(ref, start, planes, extent_x):
    return jnp.concatenate([row_of(ref, start + j, planes, extent_x) for j in range(3)], axis=0)


def upwind(face_rate):
    return jnp.maximum(face_rate, 0.0), jnp.minimum(face_rate, 0.0)


UP = {2: WEIGHTS[0], 1: WEIGHTS[1], 0: WEIGHTS[2], -1: WEIGHTS[3], -2: WEIGHTS[4]}
DOWN = {1: WEIGHTS[4], 0: WEIGHTS[3], -1: WEIGHTS[2], -2: WEIGHTS[1], -3: WEIGHTS[0]}


def combine(up_part, down_part, k):
    total = 0.0
    if k in UP:
        total = total + UP[k] * up_part
    if k in DOWN:
        total = total + DOWN[k] * down_part
    return total


def fill_padded(pad_ref, field_ref, rows_a, rows_b, even, planes, extent_x):
    high = 8 + extent_x
    at_a = jnp.where(even, 5, high)
    at_b = jnp.where(even, high, 5)
    for z in range(planes):
        pad_ref[z * PAD + 8 : z * PAD + high, :] = field_ref[z * extent_x : (z + 1) * extent_x, :]
    for j in range(3):
        part = slice(j * planes, (j + 1) * planes)
        pad_ref[pl.ds(at_a + j, planes, PAD), :] = rows_a[part]
        pad_ref[pl.ds(at_b + j, planes, PAD), :] = rows_b[part]


def edge_join(from_a, from_b, even):
    low = jnp.where(even, from_a, from_b)
    high = jnp.where(even, from_b, from_a)
    return jnp.where(lanes(low.shape) % 8 < 3, low, high)


def adjoint_edges(own, halo, own_rate, halo_rate):
    lane = lanes(own.shape) % 8
    after = roll(jnp.where(lane == 3, own, halo), -1)
    before = roll(jnp.where(lane == 2, own, halo), 1)
    jump = jnp.where(lane < 3, after - halo, halo - before)
    rate = jnp.where(lane < 3, halo_rate, roll(jnp.where(lane == 2, own_rate, halo_rate), 1))
    rate_up, rate_down = upwind(rate)
    up_part, down_part = rate_up * jump, rate_down * jump
    low_side = 0.0
    high_side = 0.0
    for k in (-1, -2, -3):
        part = jnp.where(lane < 3, combine(up_part, down_part, k), 0.0)
        low_side = low_side + roll(part, -k)
    for k in (0, 1, 2):
        part = jnp.where((lane >= 3) & (lane < 6), combine(up_part, down_part, k), 0.0)
        high_side = high_side + roll(part, -(k + 1))
    return jnp.where(lane < 3, high_side, jnp.where(lane < 6, low_side, 0.0))


def adjoint_plane(z, pad_ref, pad_rate_ref, rate_y_ref, up_ref, down_ref, extent_x):
    base = pl.multiple_of(z * PAD, 8)
    here = pad_ref[pl.ds(base, PAD), :]
    jump = pad_ref[pl.ds(base + 1, PAD), :] - here
    rate_up, rate_down = upwind(pad_rate_ref[pl.ds(base, PAD), :])
    up_ref[pl.ds(base, PAD), :] = rate_up * jump
    down_ref[pl.ds(base, PAD), :] = rate_down * jump
    total = 0.0
    for k in range(-3, 3):
        if k in UP:
            total = total + UP[k] * up_ref[pl.ds(base + 8 + k, extent_x), :]
        if k in DOWN:
            total = total + DOWN[k] * down_ref[pl.ds(base + 8 + k, extent_x), :]
    field = pad_ref[pl.ds(base + 8, extent_x), :]
    lane = lanes(field.shape)
    jump = jnp.where(lane == 127, 0.0, roll(field, -1) - field)
    rate_up, rate_down = upwind(rate_y_ref[pl.ds(pl.multiple_of(z * extent_x, 8), extent_x), :])
    up_part, down_part = rate_up * jump, rate_down * jump
    ahead = combine(up_part, down_part, 2)
    for k in (1, 0):
        ahead = jnp.where(lane == 127, 0.0, roll(ahead, -1)) + combine(up_part, down_part, k)
    behind = combine(up_part, down_part, -3)
    for k in (-2, -1):
        behind = jnp.where(lane == 0, 0.0, roll(behind, 1)) + combine(up_part, down_part, k)
    behind = jnp.where(lane == 0, 0.0, roll(behind, 1))
    return total + ahead + behind


def parities():
    return lax.rem(lax.axis_index("gx"), 2), lax.rem(lax.axis_index("gy"), 2)


def alive_lanes(value, order, number):
    lane = lanes(value.shape)
    alive = jnp.where(lane < TILE, order[2, 2 * number], order[2, 2 * number + 1])
    return jnp.where(alive == 1, value, 0.0)


def part(ref, number, extent_x):
    return ref[number * extent_x : (number + 1) * extent_x]


def lists_body(count, heading, target, source, order, request, used, *, planes, extent_x):
    parity_x, parity_y = parities()
    for label in range(9):
        used[label] = 0
    lane = lanes((8, 128))

    def place(slot, asked):
        toward = heading[slot]
        ex = (toward // 3 - 1) * (1 - 2 * parity_x)
        ey = (lax.rem(toward, 3) - 1) * (1 - 2 * parity_y)
        lx = jnp.where(ex == 0, 2, (ex + 1) // 2)
        ly = jnp.where(ey == 0, 2, (ey + 1) // 2)
        label = ly * 3 + lx
        spot = label * ROUTE_MOST + used[label]
        used[label] = used[label] + 1
        alive = slot < count[0]
        order[0, spot] = slot
        order[1, spot] = source[slot]
        order[2, spot] = alive.astype(jnp.int32)
        wanted = jnp.where(alive, target[slot], 0)
        return jnp.where(lane == spot, wanted, asked)

    asked = lax.fori_loop(0, heading.shape[0], place, jnp.zeros((8, 128), jnp.int32), unroll=4)
    request[...] = asked.astype(jnp.float32)


def edges_body(field, cotan, rate_x, rate_y, rows_a, rows_b, late_a, late_b, packs, *, planes, extent_x):
    even = parities()[0] == 0
    high = extent_x - 3
    size = 3 * planes
    for rows, late, start in (
        (rows_a, late_a, jnp.where(even, 0, high)),
        (rows_b, late_b, jnp.where(even, high, 0)),
    ):
        rows[0:size, :] = edge_rows(cotan, start, planes, extent_x)
        rows[size : 2 * size, :] = edge_rows(rate_x, start, planes, extent_x)
        late[...] = edge_rows(field, start, planes, extent_x)
    for number, ref in enumerate((cotan, rate_y, field)):
        packs[number * extent_x : (number + 1) * extent_x, :] = edge_pack(ref, planes, extent_x)


def extend_body(order, field, blocks, pairs, picked, value_a, value_b, value_s, *, planes, extent_x):
    for ly, value in enumerate((value_a, value_b, value_s)):

        def one(inner, carry):
            number = ly * 6 + inner
            one_block, two_block = blocks[order[0, 2 * number]], blocks[order[0, 2 * number + 1]]
            zero = jnp.zeros_like(one_block)
            joined = jnp.concatenate(
                [jnp.concatenate([one_block, zero], axis=1), jnp.concatenate([zero, two_block], axis=1)], axis=0
            )
            pairs[number] = joined
            tiles = tile_pair(field, order[1, 2 * number], order[1, 2 * number + 1], planes, extent_x)
            picked[number] = tiles
            spot = pl.ds(pl.multiple_of(inner * planes, 8), planes)
            value[spot, :] = pair_dot(alive_lanes(tiles, order, number), joined, 1)
            return carry

        lax.fori_loop(0, 6, one, 0, unroll=UNROLL)


def gather_tiles(asked, field, outs, first, planes, extent_x):
    for ly in range(3):

        def one(inner, carry):
            at = ly * 12 + 2 * inner
            tiles = tile_pair(field, asked[ly, at], asked[ly, at + 1], planes, extent_x)
            outs[ly][pl.ds(pl.multiple_of(first + inner * planes, 8), planes), :] = tiles
            return carry

        lax.fori_loop(0, 6, one, 0, unroll=UNROLL)


def serve_body(request, got_a, got_b, from_a, from_b, cotan, asked, out_a, out_b, out_s, list_ref, sem, *, planes, extent_x):
    row = lax.broadcasted_iota(jnp.int32, (8, 128), 0)
    group = lax.rem(lanes((8, 128)), 12) // ROUTE_MOST
    merged = []
    for a, b, s in (
        (from_a[8:16], from_a[16:24], from_a[0:8]),
        (from_b[8:16], from_b[16:24], from_b[0:8]),
        (got_a[...], got_b[...], request[...]),
    ):
        merged.append(jnp.where(group == 0, a, jnp.where(group == 1, b, s))[0:1])
    spread = [jnp.broadcast_to(one, (8, 128)) for one in merged]
    joined = jnp.where(row == 0, spread[0], jnp.where(row == 1, spread[1], spread[2]))
    list_ref[...] = joined.astype(jnp.int32)
    copy = pltpu.make_async_copy(list_ref, asked, sem)
    copy.start()
    copy.wait()
    gather_tiles(asked, cotan, (out_a, out_b, out_s), 0, planes, extent_x)


def landed(lx, ly, half, planes, x_first, y_first, x_a, x_b, y_a, y_b, own):
    if lx == S:
        ref, first = (y_a, y_b, own)[ly], (0 if ly == S and own.shape[0] == 6 * planes else y_first) + (S * 2 + half) * planes
    else:
        ref, first = (x_a, x_b)[lx], x_first + ((1, 2, 0)[ly] * 2 + half) * planes
    return ref[first : first + planes, :]


LABELS = [(lx, ly, half) for ly in range(3) for lx in range(3) for half in range(2)]


def pull_body(cotan, rate_x, rate_y, rows_a, rows_b, packs, packs_a, packs_b, grad, pad_rate, edge_rate, pad, up_ref, down_ref, *, planes, extent_x):
    parity_x, parity_y = parities()
    even_x, even_y = parity_x == 0, parity_y == 0
    size = 3 * planes
    fill_padded(pad, cotan, rows_a[0:size], rows_b[0:size], even_x, planes, extent_x)
    fill_padded(pad_rate, rate_x, rows_a[size : 2 * size], rows_b[size : 2 * size], even_x, planes, extent_x)
    halo = edge_join(part(packs_a, 0, extent_x), part(packs_b, 0, extent_x), even_y)
    halo_rate = edge_join(part(packs_a, 1, extent_x), part(packs_b, 1, extent_x), even_y)
    edge_rate[...] = halo_rate
    edges = adjoint_edges(part(packs, 0, extent_x), halo, part(packs, 1, extent_x), halo_rate)

    def plane(z, carry):
        spot = pl.ds(pl.multiple_of(z * extent_x, 8), extent_x)
        pulled = adjoint_plane(z, pad, pad_rate, rate_y, up_ref, down_ref, extent_x)
        rim = roll(edges, 125 - 8 * z)
        lane = lanes(rim.shape)
        pulled = pulled + jnp.where((lane < 3) | (lane >= 125), rim, 0.0)
        grad[spot, :] = 0.5 * cotan[spot, :] + (0.5 * TIME_STEP) * pulled
        return carry

    lax.fori_loop(0, planes, plane, 0)


def push_body(field, pad_rate, rate_y, edge_rate, late_a, late_b, packs, packs_a, packs_b, section, pad, flux_ref, *, planes, extent_x):
    parity_x, parity_y = parities()
    even_x, even_y = parity_x == 0, parity_y == 0
    fill_padded(pad, field, late_a[...], late_b[...], even_x, planes, extent_x)
    halo = edge_join(part(packs_a, 2, extent_x), part(packs_b, 2, extent_x), even_y)
    line = jnp.where(lanes(halo.shape) % 8 < 3, halo, part(packs, 2, extent_x))
    moved = {k: roll(line, -k) for k in range(-2, 4)}
    rate_up, rate_down = upwind(edge_rate[...])
    flux_low = rate_up * sum(WEIGHTS[j] * moved[j - 2] for j in range(5)) + rate_down * sum(
        WEIGHTS[j] * moved[3 - j] for j in range(5)
    )

    def plane(z, carry):
        base = pl.multiple_of(z * PAD, 8)
        spot = pl.ds(pl.multiple_of(z * extent_x, 8), extent_x)
        window = extent_x + 8
        near = {k: pad[pl.ds(base + 7 + k, window), :] for k in range(-2, 4)}
        rate_up, rate_down = upwind(pad_rate[pl.ds(base + 7, window), :])
        flux_ref[pl.ds(base, window), :] = rate_up * sum(WEIGHTS[j] * near[j - 2] for j in range(5)) + rate_down * sum(
            WEIGHTS[j] * near[3 - j] for j in range(5)
        )
        change = flux_ref[pl.ds(base, extent_x), :] - flux_ref[pl.ds(base + 1, extent_x), :]
        here = field[spot, :]
        lane = lanes(here.shape)
        turn = 125 - 8 * z
        rim = roll(halo, turn)
        near = {0: here}
        for k in (1, 2, 3):
            near[k] = roll(jnp.where(lane < k, rim, here), -k)
        for k in (1, 2):
            near[-k] = roll(jnp.where(lane >= 128 - k, rim, here), k)
        rate_up, rate_down = upwind(rate_y[spot, :])
        flux = rate_up * sum(WEIGHTS[j] * near[j - 2] for j in range(5)) + rate_down * sum(
            WEIGHTS[j] * near[3 - j] for j in range(5)
        )
        change = change + roll(jnp.where(lane == 127, roll(flux_low, turn), flux), 1) - flux
        section[spot, :] = here + TIME_STEP * change
        return carry

    lax.fori_loop(0, planes, plane, 0)


def middle_body(order, asked, early, pairs, x_a, x_b, y_a, y_b, own, grad, returned, send_a, send_b, send_s, rows_a, rows_b, *, planes, extent_x):
    even_x = parities()[0] == 0
    for number, label in enumerate(LABELS):
        back = alive_lanes(landed(*label, planes, 0, 0, x_a, x_b, y_a, y_b, own), order, number)
        returned[number] = back
        pulled = (0.5 * TIME_STEP) * pair_dot(back, pairs[number], 0)
        add_tile_pair(grad, order[1, 2 * number], order[1, 2 * number + 1], pulled, planes, extent_x)
    packed = edge_pack(grad, planes, extent_x)
    for out in (send_a, send_b, send_s):
        out[0:extent_x, :] = packed
    gather_tiles(asked, grad, (send_a, send_b, send_s), extent_x, planes, extent_x)
    high = extent_x - 3
    rows_a[...] = edge_rows(grad, jnp.where(even_x, 0, high), planes, extent_x)
    rows_b[...] = edge_rows(grad, jnp.where(even_x, high, 0), planes, extent_x)


def inner_body(cotan, grad, pad_rate, rate_y, out, pad, up_ref, down_ref, *, planes, extent_x):
    high = 8 + extent_x
    for z in range(planes):
        pad[z * PAD + 8 : z * PAD + high, :] = grad[z * extent_x : (z + 1) * extent_x, :]
    for j in range(3):
        pad[pl.ds(5 + j, planes, PAD), :] = row_of(grad, 0, planes, extent_x)
        pad[pl.ds(high + j, planes, PAD), :] = row_of(grad, extent_x - 1, planes, extent_x)

    def plane(z, carry):
        spot = pl.ds(pl.multiple_of(z * extent_x, 8), extent_x)
        pulled = adjoint_plane(z, pad, pad_rate, rate_y, up_ref, down_ref, extent_x)
        out[spot, :] = 0.5 * cotan[spot, :] + grad[spot, :] + TIME_STEP * pulled
        return carry

    lax.fori_loop(0, planes, plane, 0)


def outer(left, right):
    left_high, left_low = split(left)
    right_high, right_low = split(right)
    return lax.dot_general(
        jnp.concatenate([left_high, left_high, left_low], axis=0),
        jnp.concatenate([right_high, right_low, right_high], axis=0),
        (((0,), (0,)), ((), ())),
        preferred_element_type=jnp.float32,
    )


def section_body(order, asked, early, returned, x_a, x_b, y_a, y_b, own, section, first_outer, *, planes, extent_x):
    for number, (lx, ly, half) in enumerate(LABELS):
        came = TIME_STEP * landed(lx, ly, half, planes, 0, 3 * extent_x, x_a, x_b, y_a, y_b, own)
        at = ly * 12 + lx * ROUTE_MOST + 2 * half
        add_tile_pair(section, asked[ly, at], asked[ly, at + 1], came, planes, extent_x)

    def pick(number, carry):
        picked = tile_pair(section, order[1, 2 * number], order[1, 2 * number + 1], planes, extent_x)
        first_outer[number] = outer((0.5 * TIME_STEP) * returned[number], picked)
        return carry

    lax.fori_loop(0, first_outer.shape[0], pick, 0, unroll=UNROLL)


def last_body(
    order, early, grad, pad_rate, edge_rate, packs, own, y_a, y_b, x_a, x_b, pairs, first_outer, picked, out, out_blocks, work, total,
    *, planes, extent_x,
):
    parity_x, parity_y = parities()
    even_x, even_y = parity_x == 0, parity_y == 0
    size = 3 * planes
    halo = edge_join(y_a[0:extent_x], y_b[0:extent_x], even_y)
    edges = adjoint_edges(own[0:extent_x], halo, part(packs, 1, extent_x), edge_rate[...])

    def plane(z, carry):
        spot = pl.ds(pl.multiple_of(z * extent_x, 8), extent_x)
        rim = roll(edges, 125 - 8 * z)
        lane = lanes(rim.shape)
        total[spot, :] = early[spot, :] + TIME_STEP * jnp.where((lane < 3) | (lane >= 125), rim, 0.0)
        return carry

    lax.fori_loop(0, planes, plane, 0, unroll=2)
    low_rows = [jnp.where(even_x, x_a[j * planes : (j + 1) * planes], x_b[j * planes : (j + 1) * planes]) for j in range(3)]
    high_rows = [jnp.where(even_x, x_b[j * planes : (j + 1) * planes], x_a[j * planes : (j + 1) * planes]) for j in range(3)]
    first_cell = row_of(grad, 0, planes, extent_x)
    last_cell = row_of(grad, extent_x - 1, planes, extent_x)
    for line, low_face in ((low_rows + [first_cell], -3), ([last_cell] + high_rows, extent_x - 1)):
        faces = []
        for j in range(3):
            rate_up, rate_down = upwind(row_of(pad_rate, 8 + low_face + j, planes, PAD))
            jump = line[j + 1] - line[j]
            faces.append((rate_up * jump, rate_down * jump))
        cells = range(0, 3) if low_face < 0 else range(extent_x - 3, extent_x)
        for cell in cells:
            added = 0.0
            for j in range(3):
                k = low_face + j - cell
                if -3 <= k <= 2:
                    added = added + combine(*faces[j], k)
            spot = pl.ds(cell, planes, extent_x)
            total[spot, :] = total[spot, :] + TIME_STEP * added
    half_lane = lanes((TILE // 2, 128)) < TILE
    for number, label in enumerate(LABELS):
        back = alive_lanes(landed(*label, planes, size, extent_x, x_a, x_b, y_a, y_b, own), order, number)
        pulled = TIME_STEP * pair_dot(back, pairs[number], 0)
        add_tile_pair(total, order[1, 2 * number], order[1, 2 * number + 1], pulled, planes, extent_x)
        work[number] = first_outer[number] + outer(TIME_STEP * back, picked[number])
        for which in range(2):
            slot = order[0, 2 * number + which]
            even_rows = work[number, pl.ds(which * TILE, TILE // 2, 2), :]
            odd_rows = work[number, pl.ds(which * TILE + 1, TILE // 2, 2), :]
            if which == 0:
                merged = jnp.where(half_lane, even_rows, roll(odd_rows, TILE))
            else:
                merged = jnp.where(half_lane, roll(even_rows, TILE), odd_rows)
            out_blocks[pl.ds(pl.multiple_of(slot * (TILE // 2), 8), TILE // 2), :] = merged
    out[...] = total[...]


SPACE = {"v": pltpu.VMEM, "s": pltpu.SMEM}


def call(body, smem, vmem, outs, scratch=(), alias=None, **sizes):
    ins, specs, shapes, out_specs = [], [], [], []
    for value, kind in [(v, "s") for v in smem] + [(v, "v") for v in vmem]:
        if isinstance(value, tuple):
            value = value[0]
        else:
            value = pltpu.with_memory_space_constraint(value, SPACE[kind])
        ins.append(value)
        specs.append(pl.BlockSpec(memory_space=SPACE[kind]))
    for shape, dtype, kind in outs:
        shapes.append(jax.ShapeDtypeStruct(shape, dtype) if kind == "h" else SPACE[kind](shape, dtype))
        out_specs.append(pl.BlockSpec(memory_space=SPACE["s" if kind == "s" else "v"]))
    return pl.pallas_call(
        functools.partial(body, **sizes),
        out_shape=tuple(shapes),
        in_specs=specs,
        out_specs=tuple(out_specs),
        scratch_shapes=list(scratch),
        input_output_aliases=alias or {},
        compiler_params=pltpu.CompilerParams(vmem_limit_bytes=VMEM_LIMIT),
        name=body.__name__,
    )(*ins)


def shards(
    level_set, speed_x, speed_y, cotangent, blocks, tile_count, source_tile, dest_offset, dest_tile
):
    planes, extent_x, extent_y = level_set.shape
    slots = source_tile.shape[2]
    cells = planes * extent_x
    f32, i32 = jnp.float32, jnp.int32
    field, rate_x, rate_y, cotan = (v.reshape(cells, extent_y) for v in (level_set, speed_x, speed_y, cotangent))
    sizes = dict(planes=planes, extent_x=extent_x)
    size = 3 * planes
    pair_total = slots // 2
    box = ((2 * size, 128), f32, "v")
    padded = ((planes * PAD + 8, extent_y), f32)
    pad_scratch = pltpu.VMEM(*padded)
    whole = ((cells, 128), f32, "v")

    order, request = call(
        lists_body,
        [(tile_count.reshape(1),), (dest_offset.reshape(slots),), (dest_tile.reshape(slots),), (source_tile.reshape(slots),)], [],
        [((3, slots), i32, "s"), ((8, 128), f32, "v")],
        scratch=(pltpu.SMEM((9,), i32),), **sizes,
    )
    got_b = exchange(request, "gx", B)
    got_a = exchange(request, "gx", A)
    rows_a, rows_b, late_a, late_b, packs = call(
        edges_body, [], [field, cotan, rate_x, rate_y],
        [box, box, ((size, 128), f32, "v"), ((size, 128), f32, "v"), ((3 * extent_x, 128), f32, "v")], **sizes,
    )
    rows_b = exchange(rows_b, "gx", B)
    rows_a = exchange(rows_a, "gx", A)
    column = jnp.concatenate([request, got_a, got_b], axis=0)
    from_b = exchange(column, "gy", B)
    from_a = exchange(column, "gy", A)
    pairs, picked, value_a, value_b, value_s = call(
        extend_body, [order], [field, blocks.reshape(slots, TILE, TILE)],
        [((pair_total, 128, 128), jnp.bfloat16, "v"), ((pair_total, planes, 128), f32, "v"), box, box, box], **sizes,
    )
    packs_b = exchange(jnp.concatenate([packs, value_b], axis=0), "gy", B)
    packs_a = exchange(jnp.concatenate([packs, value_a], axis=0), "gy", A)

    asked, tiles_a, tiles_b, tiles_s = call(
        serve_body, [], [request, got_a, got_b, from_a, from_b, cotan],
        [((8, 128), i32, "s"), box, box, box], scratch=(pltpu.VMEM((8, 128), i32), pltpu.SemaphoreType.DMA(())), **sizes,
    )
    y_b = exchange(tiles_b, "gy", B)
    y_a = exchange(tiles_a, "gy", A)

    def onward(own, a, b, own_first, first, m):
        cut = lambda v, start: v[start + m * 2 * planes : start + (m + 1) * 2 * planes]
        return [cut(own, own_first), cut(a, first), cut(b, first)]

    x_b = exchange(jnp.concatenate(onward(tiles_s, y_a, y_b, 0, 0, B), axis=0), "gx", B)
    x_a = exchange(jnp.concatenate(onward(tiles_s, y_a, y_b, 0, 0, A), axis=0), "gx", A)
    early, pad_rate, edge_rate = call(
        pull_body, [], [cotan, rate_x, rate_y, rows_a, rows_b, packs, packs_a, packs_b],
        [whole, padded + ("v",), ((extent_x, 128), f32, "v")], scratch=(pad_scratch,) * 3, **sizes,
    )
    extra = 3 * extent_x
    z_b = exchange(jnp.concatenate(onward(value_s, packs_a, packs_b, 0, extra, B) + [late_b], axis=0), "gx", B)
    z_a = exchange(jnp.concatenate(onward(value_s, packs_a, packs_b, 0, extra, A) + [late_a], axis=0), "gx", A)
    grad, returned, send_a, send_b, send_s, edge_a, edge_b = call(
        middle_body, [order, asked], [early, pairs, x_a, x_b, y_a, y_b, tiles_s],
        [whole, ((pair_total, planes, 128), f32, "v")] + [((extent_x + 2 * size, 128), f32, "v")] * 3 + [((size, 128), f32, "v")] * 2,
        alias={2: 0}, **sizes,
    )
    last_y_b = exchange(send_b, "gy", B)
    last_y_a = exchange(send_a, "gy", A)
    last_x_b = exchange(jnp.concatenate([edge_b] + onward(send_s, last_y_a, last_y_b, extent_x, extent_x, B), axis=0), "gx", B)
    last_x_a = exchange(jnp.concatenate([edge_a] + onward(send_s, last_y_a, last_y_b, extent_x, extent_x, A), axis=0), "gx", A)
    (pushed,) = call(
        push_body, [], [field, pad_rate, rate_y, edge_rate, z_a[2 * size :], z_b[2 * size :], packs, packs_a, packs_b],
        [whole], scratch=(pad_scratch,) * 2, **sizes,
    )
    (inner,) = call(
        inner_body, [], [cotan, grad, pad_rate, rate_y], [whole], scratch=(pad_scratch,) * 3, **sizes,
    )
    section, first_outer = call(
        section_body, [order, asked], [pushed, returned, z_a, z_b, packs_a, packs_b, value_s],
        [whole, ((pair_total, 128, 128), f32, "v")], alias={2: 0}, **sizes,
    )
    grad_level_set, grad_blocks = call(
        last_body, [order],
        [inner, grad, pad_rate, edge_rate, packs, send_s, last_y_a, last_y_b, last_x_a, last_x_b, pairs, first_outer, picked],
        [((cells, 128), f32, "h"), ((slots * TILE // 2, 128), f32, "h")],
        scratch=(pltpu.VMEM((pair_total, 128, 128), f32), pltpu.VMEM((cells, 128), f32)), **sizes,
    )
    return (grad_level_set.reshape(planes, extent_x, extent_y), grad_blocks.reshape(1, 1, slots, TILE * TILE))


def solution(mesh):
    return jax.shard_map(
        shards,
        mesh=mesh,
        in_specs=(
            P(None, "gx", "gy"),
            P(None, "gx", "gy"),
            P(None, "gx", "gy"),
            P(None, "gx", "gy"),
            P("gx", "gy", None, None),
            P("gx", "gy"),
            P("gx", "gy", None),
            P("gx", "gy", None),
            P("gx", "gy", None),
        ),
        out_specs=(P(None, "gx", "gy"), P("gx", "gy", None, None)),
        check_vma=False,
    )
```

```python
import functools

import jax
import jax.numpy as jnp
from jax import lax
from jax.experimental import pallas as pl
from jax.experimental.pallas import tpu as pltpu
from jax.sharding import PartitionSpec as P

TILE = 64
ROUTE_MOST = 4
TIME_STEP = 0.3
WEIGHTS = (2.0 / 60.0, -13.0 / 60.0, 47.0 / 60.0, 27.0 / 60.0, -3.0 / 60.0)
PAD = 80
VMEM_LIMIT = 16 << 20

A, B, S = 0, 1, 2


def matching(count, which):
    return [(i, (i + (1 if (i % 2 == 0) == (which == B) else -1)) % count) for i in range(count)]


def exchange(block, axis, which):
    return lax.ppermute(block, axis, matching(lax.axis_size(axis), which))


def lanes(shape):
    return lax.broadcasted_iota(jnp.int32, shape, len(shape) - 1)


def roll(value, shift):
    return pltpu.roll(value, shift % 128 if isinstance(shift, int) else shift, axis=value.ndim - 1)


def split(value):
    high = value.astype(jnp.bfloat16)
    return high, (value - high.astype(jnp.float32)).astype(jnp.bfloat16)


def pair_dot(value, matrix, over):
    high, low = split(value)
    both = lax.dot_general(
        jnp.concatenate([high, low], axis=0),
        matrix,
        (((1,), (over,)), ((), ())),
        preferred_element_type=jnp.float32,
    )
    rows = value.shape[0]
    return both[:rows] + both[rows:]


def row_of(ref, x, planes, stride):
    return ref[pl.ds(x, planes, stride), :]


def tile_pair(ref, first, second, planes, extent_x):
    one = row_of(ref, first // 2, planes, extent_x)
    two = row_of(ref, second // 2, planes, extent_x)
    lane = lanes(one.shape)
    one = jnp.where(first % 2 == 0, one, roll(one, TILE))
    two = jnp.where(second % 2 == 1, two, roll(two, TILE))
    return jnp.where(lane < TILE, one, two)


def add_tile_pair(ref, first, second, value, planes, extent_x):
    lane = lanes(value.shape)
    turned = roll(value, TILE)
    for tile, half in ((first, 0), (second, 1)):
        spot = pl.ds(tile // 2, planes, extent_x)
        placed = jnp.where(tile % 2 == half, value, turned)
        keep = (lane // TILE) == tile % 2
        ref[spot, :] = ref[spot, :] + jnp.where(keep, placed, 0.0)


def edge_pack(ref, planes, extent_x):
    lane = lanes((extent_x, 128))
    packed = jnp.zeros((extent_x, 128), jnp.float32)
    for z in range(planes):
        plane = ref[z * extent_x : (z + 1) * extent_x, :]
        packed = jnp.where(lane // 8 == z, roll(plane, 8 * z + 3), packed)
    return packed


def edge_rows(ref, start, planes, extent_x):
    return jnp.concatenate([row_of(ref, start + j, planes, extent_x) for j in range(3)], axis=0)


def upwind(face_rate):
    return jnp.maximum(face_rate, 0.0), jnp.minimum(face_rate, 0.0)


UP = {2: WEIGHTS[0], 1: WEIGHTS[1], 0: WEIGHTS[2], -1: WEIGHTS[3], -2: WEIGHTS[4]}
DOWN = {1: WEIGHTS[4], 0: WEIGHTS[3], -1: WEIGHTS[2], -2: WEIGHTS[1], -3: WEIGHTS[0]}


def combine(up_part, down_part, k):
    total = 0.0
    if k in UP:
        total = total + UP[k] * up_part
    if k in DOWN:
        total = total + DOWN[k] * down_part
    return total


def fill_padded(pad_ref, field_ref, rows_a, rows_b, even, planes, extent_x):
    high = 8 + extent_x
    at_a = jnp.where(even, 5, high)
    at_b = jnp.where(even, high, 5)
    for z in range(planes):
        pad_ref[z * PAD + 8 : z * PAD + high, :] = field_ref[z * extent_x : (z + 1) * extent_x, :]
    for j in range(3):
        part = slice(j * planes, (j + 1) * planes)
        pad_ref[pl.ds(at_a + j, planes, PAD), :] = rows_a[part]
        pad_ref[pl.ds(at_b + j, planes, PAD), :] = rows_b[part]


def edge_join(from_a, from_b, even):
    low = jnp.where(even, from_a, from_b)
    high = jnp.where(even, from_b, from_a)
    return jnp.where(lanes(low.shape) % 8 < 3, low, high)


def adjoint_edges(own, halo, own_rate, halo_rate):
    lane = lanes(own.shape) % 8
    after = roll(jnp.where(lane == 3, own, halo), -1)
    before = roll(jnp.where(lane == 2, own, halo), 1)
    jump = jnp.where(lane < 3, after - halo, halo - before)
    rate = jnp.where(lane < 3, halo_rate, roll(jnp.where(lane == 2, own_rate, halo_rate), 1))
    rate_up, rate_down = upwind(rate)
    up_part, down_part = rate_up * jump, rate_down * jump
    low_side = 0.0
    high_side = 0.0
    for k in (-1, -2, -3):
        part = jnp.where(lane < 3, combine(up_part, down_part, k), 0.0)
        low_side = low_side + roll(part, -k)
    for k in (0, 1, 2):
        part = jnp.where((lane >= 3) & (lane < 6), combine(up_part, down_part, k), 0.0)
        high_side = high_side + roll(part, -(k + 1))
    return jnp.where(lane < 3, high_side, jnp.where(lane < 6, low_side, 0.0))


def adjoint_plane(z, pad_ref, pad_rate_ref, rate_y_ref, up_ref, down_ref, extent_x):
    base = z * PAD
    here = pad_ref[pl.ds(base, PAD), :]
    jump = pad_ref[pl.ds(base + 1, PAD), :] - here
    rate_up, rate_down = upwind(pad_rate_ref[pl.ds(base, PAD), :])
    up_ref[pl.ds(base, PAD), :] = rate_up * jump
    down_ref[pl.ds(base, PAD), :] = rate_down * jump
    total = 0.0
    for k in range(-3, 3):
        if k in UP:
            total = total + UP[k] * up_ref[pl.ds(base + 8 + k, extent_x), :]
        if k in DOWN:
            total = total + DOWN[k] * down_ref[pl.ds(base + 8 + k, extent_x), :]
    field = pad_ref[pl.ds(base + 8, extent_x), :]
    lane = lanes(field.shape)
    jump = jnp.where(lane == 127, 0.0, roll(field, -1) - field)
    rate_up, rate_down = upwind(rate_y_ref[pl.ds(z * extent_x, extent_x), :])
    up_part, down_part = rate_up * jump, rate_down * jump
    ahead = combine(up_part, down_part, 2)
    for k in (1, 0):
        ahead = jnp.where(lane == 127, 0.0, roll(ahead, -1)) + combine(up_part, down_part, k)
    behind = combine(up_part, down_part, -3)
    for k in (-2, -1):
        behind = jnp.where(lane == 0, 0.0, roll(behind, 1)) + combine(up_part, down_part, k)
    behind = jnp.where(lane == 0, 0.0, roll(behind, 1))
    return total + ahead + behind


def parities():
    return lax.rem(lax.axis_index("gx"), 2), lax.rem(lax.axis_index("gy"), 2)


def alive_lanes(value, order, number):
    lane = lanes(value.shape)
    alive = jnp.where(lane < TILE, order[2, 2 * number], order[2, 2 * number + 1])
    return jnp.where(alive == 1, value, 0.0)


def part(ref, number, extent_x):
    return ref[number * extent_x : (number + 1) * extent_x]


def begin_body(
    count, heading, target, source, field, cotan, rate_x, rate_y,
    order, send_a, send_b, field_out, cotan_out, rate_x_out, rate_y_out,
    heading_in, target_in, source_in, used, sems, *, planes, extent_x,
):
    pairs = (
        (heading, heading_in), (target, target_in), (source, source_in),
        (cotan, cotan_out), (rate_x, rate_x_out), (field, field_out), (rate_y, rate_y_out),
    )
    copies = [pltpu.make_async_copy(a, b, sems.at[number]) for number, (a, b) in enumerate(pairs)]
    for copy in copies:
        copy.start()
    parity_x, parity_y = parities()
    for label in range(9):
        used[label] = 0
    lane = lanes((8, 128))
    for copy in copies[:3]:
        copy.wait()
    total = count[0, 0]
    asked = jnp.zeros((8, 128), jnp.int32)
    for slot in range(heading.shape[0]):
        toward = heading_in[slot]
        across = (toward >= 3).astype(jnp.int32) + (toward >= 6).astype(jnp.int32)
        ex = (across - 1) * (1 - 2 * parity_x)
        ey = (toward - 3 * across - 1) * (1 - 2 * parity_y)
        lx = jnp.where(ex == 0, 2, (ex + 1) // 2)
        ly = jnp.where(ey == 0, 2, (ey + 1) // 2)
        label = ly * 3 + lx
        spot = label * ROUTE_MOST + used[label]
        used[label] = used[label] + 1
        order[0, spot] = slot
        order[1, spot] = source_in[slot]
        order[2, spot] = (slot < total).astype(jnp.int32)
        wanted = jnp.where(slot < total, target_in[slot], 0)
        asked = jnp.where(lane == spot, wanted, asked)
    even = parity_x == 0
    high = extent_x - 3
    size = 3 * planes
    for out in (send_a, send_b):
        out[0:8, :] = asked.astype(jnp.float32)
    for number, ref in enumerate((cotan_out, rate_x_out, field_out)):
        copies[3 + number].wait()
        first = 8 + number * size
        send_a[first : first + size, :] = edge_rows(ref, jnp.where(even, 0, high), planes, extent_x)
        send_b[first : first + size, :] = edge_rows(ref, jnp.where(even, high, 0), planes, extent_x)
    copies[6].wait()


def extend_body(order, field, cotan, rate_y, blocks, pairs, picked, send_a, send_b, value_s, *, planes, extent_x):
    extra = 3 * extent_x
    for number, ref in enumerate((cotan, rate_y, field)):
        packed = edge_pack(ref, planes, extent_x)
        for out in (send_a, send_b):
            out[number * extent_x : (number + 1) * extent_x, :] = packed
    for number in range(18):
        one_block, two_block = blocks[order[0, 2 * number]], blocks[order[0, 2 * number + 1]]
        zero = jnp.zeros_like(one_block)
        joined = jnp.concatenate(
            [jnp.concatenate([one_block, zero], axis=1), jnp.concatenate([zero, two_block], axis=1)], axis=0
        )
        pairs[number] = joined
        tiles = tile_pair(field, order[1, 2 * number], order[1, 2 * number + 1], planes, extent_x)
        picked[number] = tiles
        value = pair_dot(alive_lanes(tiles, order, number), joined, 1)
        out, first = ((send_a, extra), (send_b, extra), (value_s, 0))[number // 6]
        first = first + number % 6 * planes
        out[first : first + planes, :] = value


def gather_tiles(asked, field, outs, first, planes, extent_x):
    for ly in range(3):

        for inner in range(6):
            at = ly * 12 + 2 * inner
            tiles = tile_pair(field, asked[ly, at], asked[ly, at + 1], planes, extent_x)
            outs[ly][first + inner * planes : first + (inner + 1) * planes, :] = tiles


def serve_body(request, got_a, got_b, from_a, from_b, cotan, asked, out_a, out_b, out_s, list_ref, sem, *, planes, extent_x):
    row = lax.broadcasted_iota(jnp.int32, (8, 128), 0)
    group = lax.rem(lanes((8, 128)), 12) // ROUTE_MOST
    merged = []
    for a, b, s in (
        (from_a[8:16], from_a[16:24], from_a[0:8]),
        (from_b[8:16], from_b[16:24], from_b[0:8]),
        (got_a[0:8], got_b[0:8], request[0:8]),
    ):
        merged.append(jnp.where(group == 0, a, jnp.where(group == 1, b, s))[0:1])
    spread = [jnp.broadcast_to(one, (8, 128)) for one in merged]
    joined = jnp.where(row == 0, spread[0], jnp.where(row == 1, spread[1], spread[2]))
    list_ref[...] = joined.astype(jnp.int32)
    copy = pltpu.make_async_copy(list_ref, asked, sem)
    copy.start()
    copy.wait()
    gather_tiles(asked, cotan, (out_a, out_b, out_s), 0, planes, extent_x)


def landed(lx, ly, half, planes, x_first, y_first, x_a, x_b, y_a, y_b, own):
    if lx == S:
        ref, first = (y_a, y_b, own)[ly], (0 if ly == S and own.shape[0] == 6 * planes else y_first) + (S * 2 + half) * planes
    else:
        ref, first = (x_a, x_b)[lx], x_first + ((1, 2, 0)[ly] * 2 + half) * planes
    return ref[first : first + planes, :]


LABELS = [(lx, ly, half) for ly in range(3) for lx in range(3) for half in range(2)]


def pull_body(cotan, rate_x, rate_y, rows_a, rows_b, packs, packs_a, packs_b, grad, pad_rate, edge_rate, pad, up_ref, down_ref, *, planes, extent_x):
    parity_x, parity_y = parities()
    even_x, even_y = parity_x == 0, parity_y == 0
    size = 3 * planes
    fill_padded(pad, cotan, rows_a[8 : 8 + size], rows_b[8 : 8 + size], even_x, planes, extent_x)
    fill_padded(pad_rate, rate_x, rows_a[8 + size : 8 + 2 * size], rows_b[8 + size : 8 + 2 * size], even_x, planes, extent_x)
    halo = edge_join(part(packs_a, 0, extent_x), part(packs_b, 0, extent_x), even_y)
    halo_rate = edge_join(part(packs_a, 1, extent_x), part(packs_b, 1, extent_x), even_y)
    edge_rate[...] = halo_rate
    edges = adjoint_edges(part(packs, 0, extent_x), halo, part(packs, 1, extent_x), halo_rate)

    for z in range(planes):
        spot = pl.ds(z * extent_x, extent_x)
        pulled = adjoint_plane(z, pad, pad_rate, rate_y, up_ref, down_ref, extent_x)
        rim = roll(edges, 125 - 8 * z)
        lane = lanes(rim.shape)
        pulled = pulled + jnp.where((lane < 3) | (lane >= 125), rim, 0.0)
        grad[spot, :] = 0.5 * cotan[spot, :] + (0.5 * TIME_STEP) * pulled


def push_body(field, pad_rate, rate_y, edge_rate, rows_a, rows_b, packs, packs_a, packs_b, section, pad, flux_ref, *, planes, extent_x):
    parity_x, parity_y = parities()
    even_x, even_y = parity_x == 0, parity_y == 0
    first = 8 + 6 * planes
    fill_padded(pad, field, rows_a[first : first + 3 * planes], rows_b[first : first + 3 * planes], even_x, planes, extent_x)
    halo = edge_join(part(packs_a, 2, extent_x), part(packs_b, 2, extent_x), even_y)
    line = jnp.where(lanes(halo.shape) % 8 < 3, halo, part(packs, 2, extent_x))
    moved = {k: roll(line, -k) for k in range(-2, 4)}
    rate_up, rate_down = upwind(edge_rate[...])
    flux_low = rate_up * sum(WEIGHTS[j] * moved[j - 2] for j in range(5)) + rate_down * sum(
        WEIGHTS[j] * moved[3 - j] for j in range(5)
    )

    for z in range(planes):
        base = z * PAD
        spot = pl.ds(z * extent_x, extent_x)
        window = extent_x + 8
        near = {k: pad[pl.ds(base + 7 + k, window), :] for k in range(-2, 4)}
        rate_up, rate_down = upwind(pad_rate[pl.ds(base + 7, window), :])
        flux_ref[pl.ds(base, window), :] = rate_up * sum(WEIGHTS[j] * near[j - 2] for j in range(5)) + rate_down * sum(
            WEIGHTS[j] * near[3 - j] for j in range(5)
        )
        change = flux_ref[pl.ds(base, extent_x), :] - flux_ref[pl.ds(base + 1, extent_x), :]
        here = field[spot, :]
        lane = lanes(here.shape)
        turn = 125 - 8 * z
        rim = roll(halo, turn)
        near = {0: here}
        for k in (1, 2, 3):
            near[k] = roll(jnp.where(lane < k, rim, here), -k)
        for k in (1, 2):
            near[-k] = roll(jnp.where(lane >= 128 - k, rim, here), k)
        rate_up, rate_down = upwind(rate_y[spot, :])
        flux = rate_up * sum(WEIGHTS[j] * near[j - 2] for j in range(5)) + rate_down * sum(
            WEIGHTS[j] * near[3 - j] for j in range(5)
        )
        change = change + roll(jnp.where(lane == 127, roll(flux_low, turn), flux), 1) - flux
        section[spot, :] = here + TIME_STEP * change


def middle_body(order, asked, early, pairs, x_a, x_b, y_a, y_b, own, grad, returned, send_a, send_b, send_s, rows_a, rows_b, *, planes, extent_x):
    even_x = parities()[0] == 0
    for number, label in enumerate(LABELS):
        back = alive_lanes(landed(*label, planes, 0, 0, x_a, x_b, y_a, y_b, own), order, number)
        returned[number] = back
        pulled = (0.5 * TIME_STEP) * pair_dot(back, pairs[number], 0)
        add_tile_pair(grad, order[1, 2 * number], order[1, 2 * number + 1], pulled, planes, extent_x)
    packed = edge_pack(grad, planes, extent_x)
    for out in (send_a, send_b, send_s):
        out[0:extent_x, :] = packed
    gather_tiles(asked, grad, (send_a, send_b, send_s), extent_x, planes, extent_x)
    high = extent_x - 3
    rows_a[...] = edge_rows(grad, jnp.where(even_x, 0, high), planes, extent_x)
    rows_b[...] = edge_rows(grad, jnp.where(even_x, high, 0), planes, extent_x)


def inner_body(cotan, grad, pad_rate, rate_y, out, pad, up_ref, down_ref, *, planes, extent_x):
    high = 8 + extent_x
    for z in range(planes):
        pad[z * PAD + 8 : z * PAD + high, :] = grad[z * extent_x : (z + 1) * extent_x, :]
    for j in range(3):
        pad[pl.ds(5 + j, planes, PAD), :] = row_of(grad, 0, planes, extent_x)
        pad[pl.ds(high + j, planes, PAD), :] = row_of(grad, extent_x - 1, planes, extent_x)

    for z in range(planes):
        spot = pl.ds(z * extent_x, extent_x)
        pulled = adjoint_plane(z, pad, pad_rate, rate_y, up_ref, down_ref, extent_x)
        out[spot, :] = 0.5 * cotan[spot, :] + grad[spot, :] + TIME_STEP * pulled


def outer(left, right):
    left_high, left_low = split(left)
    right_high, right_low = split(right)
    return lax.dot_general(
        jnp.concatenate([left_high, left_high, left_low], axis=0),
        jnp.concatenate([right_high, right_low, right_high], axis=0),
        (((0,), (0,)), ((), ())),
        preferred_element_type=jnp.float32,
    )


def section_body(order, asked, early, returned, x_a, x_b, y_a, y_b, own, section, first_outer, *, planes, extent_x):
    for number, (lx, ly, half) in enumerate(LABELS):
        came = TIME_STEP * landed(lx, ly, half, planes, 0, 3 * extent_x, x_a, x_b, y_a, y_b, own)
        at = ly * 12 + lx * ROUTE_MOST + 2 * half
        add_tile_pair(section, asked[ly, at], asked[ly, at + 1], came, planes, extent_x)

    for number in range(first_outer.shape[0]):
        picked = tile_pair(section, order[1, 2 * number], order[1, 2 * number + 1], planes, extent_x)
        first_outer[number] = outer((0.5 * TIME_STEP) * returned[number], picked)


def last_body(
    order, early, grad, pad_rate, edge_rate, packs, own, y_a, y_b, x_a, x_b, pairs, first_outer, picked, out, out_blocks, work, total,
    *, planes, extent_x,
):
    parity_x, parity_y = parities()
    even_x, even_y = parity_x == 0, parity_y == 0
    size = 3 * planes
    halo = edge_join(y_a[0:extent_x], y_b[0:extent_x], even_y)
    edges = adjoint_edges(own[0:extent_x], halo, part(packs, 1, extent_x), edge_rate[...])

    for z in range(planes):
        spot = pl.ds(z * extent_x, extent_x)
        rim = roll(edges, 125 - 8 * z)
        lane = lanes(rim.shape)
        total[spot, :] = early[spot, :] + TIME_STEP * jnp.where((lane < 3) | (lane >= 125), rim, 0.0)
    low_rows = [jnp.where(even_x, x_a[j * planes : (j + 1) * planes], x_b[j * planes : (j + 1) * planes]) for j in range(3)]
    high_rows = [jnp.where(even_x, x_b[j * planes : (j + 1) * planes], x_a[j * planes : (j + 1) * planes]) for j in range(3)]
    first_cell = row_of(grad, 0, planes, extent_x)
    last_cell = row_of(grad, extent_x - 1, planes, extent_x)
    for line, low_face in ((low_rows + [first_cell], -3), ([last_cell] + high_rows, extent_x - 1)):
        faces = []
        for j in range(3):
            rate_up, rate_down = upwind(row_of(pad_rate, 8 + low_face + j, planes, PAD))
            jump = line[j + 1] - line[j]
            faces.append((rate_up * jump, rate_down * jump))
        cells = range(0, 3) if low_face < 0 else range(extent_x - 3, extent_x)
        for cell in cells:
            added = 0.0
            for j in range(3):
                k = low_face + j - cell
                if -3 <= k <= 2:
                    added = added + combine(*faces[j], k)
            spot = pl.ds(cell, planes, extent_x)
            total[spot, :] = total[spot, :] + TIME_STEP * added
    half_lane = lanes((TILE // 2, 128)) < TILE
    for number, label in enumerate(LABELS):
        back = alive_lanes(landed(*label, planes, size, extent_x, x_a, x_b, y_a, y_b, own), order, number)
        pulled = TIME_STEP * pair_dot(back, pairs[number], 0)
        add_tile_pair(total, order[1, 2 * number], order[1, 2 * number + 1], pulled, planes, extent_x)
        work[number] = first_outer[number] + outer(TIME_STEP * back, picked[number])
        for which in range(2):
            slot = order[0, 2 * number + which]
            even_rows = work[number, pl.ds(which * TILE, TILE // 2, 2), :]
            odd_rows = work[number, pl.ds(which * TILE + 1, TILE // 2, 2), :]
            if which == 0:
                merged = jnp.where(half_lane, even_rows, roll(odd_rows, TILE))
            else:
                merged = jnp.where(half_lane, roll(even_rows, TILE), odd_rows)
            out_blocks[pl.ds(pl.multiple_of(slot * (TILE // 2), 8), TILE // 2), :] = merged
    out[...] = total[...]


SPACE = {"v": pltpu.VMEM, "s": pltpu.SMEM, "h": pltpu.HBM}


def call(body, ins, outs, scratch=(), alias=None, **sizes):
    values, specs, shapes, out_specs = [], [], [], []
    for kind, group in ins:
        for value in group:
            values.append(value if kind == "r" else pltpu.with_memory_space_constraint(value, SPACE[kind]))
            specs.append(pl.BlockSpec(memory_space=SPACE["s" if kind == "r" else kind]))
    for shape, dtype, kind in outs:
        shapes.append(jax.ShapeDtypeStruct(shape, dtype) if kind == "h" else SPACE[kind](shape, dtype))
        out_specs.append(pl.BlockSpec(memory_space=SPACE["s" if kind == "s" else "v"]))
    return pl.pallas_call(
        functools.partial(body, **sizes),
        out_shape=tuple(shapes),
        in_specs=specs,
        out_specs=tuple(out_specs),
        scratch_shapes=list(scratch),
        input_output_aliases=alias or {},
        compiler_params=pltpu.CompilerParams(vmem_limit_bytes=VMEM_LIMIT),
        name=body.__name__,
    )(*values)


def shards(
    level_set, speed_x, speed_y, cotangent, blocks, tile_count, source_tile, dest_offset, dest_tile
):
    planes, extent_x, extent_y = level_set.shape
    slots = source_tile.shape[2]
    cells = planes * extent_x
    f32, i32 = jnp.float32, jnp.int32
    field, rate_x, rate_y, cotan = (v.reshape(cells, extent_y) for v in (level_set, speed_x, speed_y, cotangent))
    sizes = dict(planes=planes, extent_x=extent_x)
    size = 3 * planes
    pair_total = slots // 2
    box = ((2 * size, 128), f32, "v")
    padded = ((planes * PAD + 8, extent_y), f32)
    pad_scratch = pltpu.VMEM(*padded)
    whole = ((cells, 128), f32, "v")

    order, send_a, send_b, field, cotan, rate_x, rate_y = call(
        begin_body,
        [("r", [tile_count]), ("h", [v.reshape(slots) for v in (dest_offset, dest_tile, source_tile)] + [field, cotan, rate_x, rate_y])],
        [((3, slots), i32, "s")] + [((8 + 3 * size, 128), f32, "v")] * 2 + [whole] * 4,
        scratch=[pltpu.SMEM((slots,), i32)] * 3 + [pltpu.SMEM((9,), i32), pltpu.SemaphoreType.DMA((7,))],
        **sizes,
    )
    rows_b = exchange(send_b, "gx", B)
    rows_a = exchange(send_a, "gx", A)
    column = jnp.concatenate([send_a[:8], rows_a[:8], rows_b[:8]], axis=0)
    extra = 3 * extent_x
    pairs, picked, wide_a, wide_b, value_s = call(
        extend_body, [("s", [order]), ("v", [field, cotan, rate_y, blocks.reshape(slots, TILE, TILE)])],
        [((pair_total, 128, 128), jnp.bfloat16, "v"), ((pair_total, planes, 128), f32, "v")]
        + [((extra + 2 * size, 128), f32, "v")] * 2 + [box], **sizes,
    )
    column, wide_a, wide_b = lax.optimization_barrier((column, wide_a, wide_b))
    from_b = exchange(column, "gy", B)
    from_a = exchange(column, "gy", A)
    packs_b = exchange(wide_b, "gy", B)
    packs_a = exchange(wide_a, "gy", A)

    asked, tiles_a, tiles_b, tiles_s = call(
        serve_body, [("v", [send_a, rows_a, rows_b, from_a, from_b, cotan])],
        [((8, 128), i32, "s"), box, box, box], scratch=(pltpu.VMEM((8, 128), i32), pltpu.SemaphoreType.DMA(())), **sizes,
    )
    y_b = exchange(tiles_b, "gy", B)
    y_a = exchange(tiles_a, "gy", A)
    early, pad_rate, edge_rate = call(
        pull_body, [("v", [cotan, rate_x, rate_y, rows_a, rows_b, wide_a, packs_a, packs_b])],
        [whole, padded + ("v",), ((extent_x, 128), f32, "v")], scratch=(pad_scratch,) * 3, **sizes,
    )
    y_a, y_b, early = lax.optimization_barrier((y_a, y_b, early))

    def onward(own, a, b, own_first, first, m):
        cut = lambda v, start: v[start + m * 2 * planes : start + (m + 1) * 2 * planes]
        return [cut(own, own_first), cut(a, first), cut(b, first)]

    x_b = exchange(jnp.concatenate(onward(tiles_s, y_a, y_b, 0, 0, B), axis=0), "gx", B)
    x_a = exchange(jnp.concatenate(onward(tiles_s, y_a, y_b, 0, 0, A), axis=0), "gx", A)
    z_b = exchange(jnp.concatenate(onward(value_s, packs_a, packs_b, 0, extra, B), axis=0), "gx", B)
    z_a = exchange(jnp.concatenate(onward(value_s, packs_a, packs_b, 0, extra, A), axis=0), "gx", A)
    grad, returned, send_a, send_b, send_s, edge_a, edge_b = call(
        middle_body, [("s", [order, asked]), ("v", [early, pairs, x_a, x_b, y_a, y_b, tiles_s])],
        [whole, ((pair_total, planes, 128), f32, "v")] + [((extent_x + 2 * size, 128), f32, "v")] * 3 + [((size, 128), f32, "v")] * 2,
        alias={2: 0}, **sizes,
    )
    last_y_b = exchange(send_b, "gy", B)
    last_y_a = exchange(send_a, "gy", A)
    (pushed,) = call(
        push_body, [("v", [field, pad_rate, rate_y, edge_rate, rows_a, rows_b, wide_a, packs_a, packs_b])],
        [whole], scratch=(pad_scratch,) * 2, **sizes,
    )
    last_y_a, last_y_b, pushed = lax.optimization_barrier((last_y_a, last_y_b, pushed))
    last_x_b = exchange(jnp.concatenate([edge_b] + onward(send_s, last_y_a, last_y_b, extent_x, extent_x, B), axis=0), "gx", B)
    last_x_a = exchange(jnp.concatenate([edge_a] + onward(send_s, last_y_a, last_y_b, extent_x, extent_x, A), axis=0), "gx", A)
    (inner,) = call(
        inner_body, [("v", [cotan, grad, pad_rate, rate_y])], [whole], scratch=(pad_scratch,) * 3, **sizes,
    )
    section, first_outer = call(
        section_body, [("s", [order, asked]), ("v", [pushed, returned, z_a, z_b, packs_a, packs_b, value_s])],
        [whole, ((pair_total, 128, 128), f32, "v")], alias={2: 0}, **sizes,
    )
    grad_level_set, grad_blocks = call(
        last_body,
        [("s", [order]), ("v", [inner, grad, pad_rate, edge_rate, wide_a, send_s, last_y_a, last_y_b, last_x_a, last_x_b, pairs, first_outer, picked])],
        [((cells, 128), f32, "h"), ((slots * TILE // 2, 128), f32, "h")],
        scratch=(pltpu.VMEM((pair_total, 128, 128), f32), pltpu.VMEM((cells, 128), f32)), **sizes,
    )
    return (grad_level_set.reshape(planes, extent_x, extent_y), grad_blocks.reshape(1, 1, slots, TILE * TILE))


def solution(mesh):
    return jax.shard_map(
        shards,
        mesh=mesh,
        in_specs=(
            P(None, "gx", "gy"),
            P(None, "gx", "gy"),
            P(None, "gx", "gy"),
            P(None, "gx", "gy"),
            P("gx", "gy", None, None),
            P("gx", "gy"),
            P("gx", "gy", None),
            P("gx", "gy", None),
            P("gx", "gy", None),
        ),
        out_specs=(P(None, "gx", "gy"), P("gx", "gy", None, None)),
        check_vma=False,
    )
```

```python
import functools

import jax
import jax.numpy as jnp
from jax import lax
from jax.experimental import pallas as pl
from jax.experimental.pallas import tpu as pltpu
from jax.sharding import PartitionSpec as P

TILE = 64
ROUTE_MOST = 4
TIME_STEP = 0.3
WEIGHTS = (2.0 / 60.0, -13.0 / 60.0, 47.0 / 60.0, 27.0 / 60.0, -3.0 / 60.0)
PAD = 80
VMEM_LIMIT = 16 << 20

A, B, S = 0, 1, 2


def matching(count, which):
    return [(i, (i + (1 if (i % 2 == 0) == (which == B) else -1)) % count) for i in range(count)]


def exchange(block, axis, which):
    return lax.ppermute(block, axis, matching(lax.axis_size(axis), which))


def lanes(shape):
    return lax.broadcasted_iota(jnp.int32, shape, len(shape) - 1)


def roll(value, shift):
    return pltpu.roll(value, shift % 128 if isinstance(shift, int) else shift, axis=value.ndim - 1)


def split(value):
    high = value.astype(jnp.bfloat16)
    return high, (value - high.astype(jnp.float32)).astype(jnp.bfloat16)


def pair_dot(value, matrix, over):
    high, low = split(value)
    both = lax.dot_general(
        jnp.concatenate([high, low], axis=0),
        matrix,
        (((1,), (over,)), ((), ())),
        preferred_element_type=jnp.float32,
    )
    rows = value.shape[0]
    return both[:rows] + both[rows:]


def row_of(ref, x, planes, stride):
    return ref[pl.ds(x, planes, stride), :]


def tile_pair(ref, first, second, planes, extent_x):
    one = row_of(ref, first // 2, planes, extent_x)
    two = row_of(ref, second // 2, planes, extent_x)
    lane = lanes(one.shape)
    one = jnp.where(first % 2 == 0, one, roll(one, TILE))
    two = jnp.where(second % 2 == 1, two, roll(two, TILE))
    return jnp.where(lane < TILE, one, two)


def add_tile_pair(ref, first, second, value, planes, extent_x):
    lane = lanes(value.shape)
    turned = roll(value, TILE)
    for tile, half in ((first, 0), (second, 1)):
        spot = pl.ds(tile // 2, planes, extent_x)
        placed = jnp.where(tile % 2 == half, value, turned)
        keep = (lane // TILE) == tile % 2
        ref[spot, :] = ref[spot, :] + jnp.where(keep, placed, 0.0)


def edge_pack(ref, planes, extent_x):
    lane = lanes((extent_x, 128))
    packed = jnp.zeros((extent_x, 128), jnp.float32)
    for z in range(planes):
        plane = ref[z * extent_x : (z + 1) * extent_x, :]
        packed = jnp.where(lane // 8 == z, roll(plane, 8 * z + 3), packed)
    return packed


def edge_rows(ref, start, planes, extent_x):
    return jnp.concatenate([row_of(ref, start + j, planes, extent_x) for j in range(3)], axis=0)


def upwind(face_rate):
    return jnp.maximum(face_rate, 0.0), jnp.minimum(face_rate, 0.0)


UP = {2: WEIGHTS[0], 1: WEIGHTS[1], 0: WEIGHTS[2], -1: WEIGHTS[3], -2: WEIGHTS[4]}
DOWN = {1: WEIGHTS[4], 0: WEIGHTS[3], -1: WEIGHTS[2], -2: WEIGHTS[1], -3: WEIGHTS[0]}


def combine(up_part, down_part, k):
    total = 0.0
    if k in UP:
        total = total + UP[k] * up_part
    if k in DOWN:
        total = total + DOWN[k] * down_part
    return total


def fill_padded(pad_ref, field_ref, rows_a, rows_b, even, planes, extent_x):
    high = 8 + extent_x
    at_a = jnp.where(even, 5, high)
    at_b = jnp.where(even, high, 5)
    for z in range(planes):
        pad_ref[z * PAD + 8 : z * PAD + high, :] = field_ref[z * extent_x : (z + 1) * extent_x, :]
    for j in range(3):
        part = slice(j * planes, (j + 1) * planes)
        pad_ref[pl.ds(at_a + j, planes, PAD), :] = rows_a[part]
        pad_ref[pl.ds(at_b + j, planes, PAD), :] = rows_b[part]


def edge_join(from_a, from_b, even):
    low = jnp.where(even, from_a, from_b)
    high = jnp.where(even, from_b, from_a)
    return jnp.where(lanes(low.shape) % 8 < 3, low, high)


def adjoint_edges(own, halo, own_rate, halo_rate):
    lane = lanes(own.shape) % 8
    after = roll(jnp.where(lane == 3, own, halo), -1)
    before = roll(jnp.where(lane == 2, own, halo), 1)
    jump = jnp.where(lane < 3, after - halo, halo - before)
    rate = jnp.where(lane < 3, halo_rate, roll(jnp.where(lane == 2, own_rate, halo_rate), 1))
    rate_up, rate_down = upwind(rate)
    up_part, down_part = rate_up * jump, rate_down * jump
    low_side = 0.0
    high_side = 0.0
    for k in (-1, -2, -3):
        part = jnp.where(lane < 3, combine(up_part, down_part, k), 0.0)
        low_side = low_side + roll(part, -k)
    for k in (0, 1, 2):
        part = jnp.where((lane >= 3) & (lane < 6), combine(up_part, down_part, k), 0.0)
        high_side = high_side + roll(part, -(k + 1))
    return jnp.where(lane < 3, high_side, jnp.where(lane < 6, low_side, 0.0))


def adjoint_x(z, pad_ref, pad_rate_ref, up_ref, down_ref, extent_x):
    base = z * PAD
    here = pad_ref[pl.ds(base, PAD), :]
    jump = pad_ref[pl.ds(base + 1, PAD), :] - here
    rate_up, rate_down = upwind(pad_rate_ref[pl.ds(base, PAD), :])
    up_ref[pl.ds(base, PAD), :] = rate_up * jump
    down_ref[pl.ds(base, PAD), :] = rate_down * jump
    total = 0.0
    for k in range(-3, 3):
        if k in UP:
            total = total + UP[k] * up_ref[pl.ds(base + 8 + k, extent_x), :]
        if k in DOWN:
            total = total + DOWN[k] * down_ref[pl.ds(base + 8 + k, extent_x), :]
    return total


def band(weights, first_lost):
    row = lax.broadcasted_iota(jnp.int32, (128, 128), 0)
    gap = row - lax.broadcasted_iota(jnp.int32, (128, 128), 1)
    matrix = jnp.zeros((128, 128), jnp.float32)
    for k, weight in weights.items():
        matrix = jnp.where(gap == k, float(round(60.0 * weight)), matrix)
    return jnp.where(row >= first_lost, 0.0, matrix).astype(jnp.bfloat16)


def mix(left, matrix):
    return lax.dot_general(left, matrix, (((1,), (0,)), ((), ())), preferred_element_type=jnp.float32)


def adjoint_y(field_ref, rate_y_ref, planes, extent_x):
    up_matrix, down_matrix = band(UP, 127), band(DOWN, 127)
    matrix = jnp.concatenate([up_matrix, up_matrix, down_matrix, down_matrix], axis=0)
    rows = 4 * extent_x
    results = []
    for chunk in range(planes // 4):
        field = field_ref[chunk * rows : (chunk + 1) * rows, :]
        jump = roll(field, -1) - field
        rate_up, rate_down = upwind(rate_y_ref[chunk * rows : (chunk + 1) * rows, :])
        left = jnp.concatenate(split(rate_up * jump) + split(rate_down * jump), axis=1)
        results.append(mix(left, matrix))
    return results


def parities():
    return lax.rem(lax.axis_index("gx"), 2), lax.rem(lax.axis_index("gy"), 2)


def alive_lanes(value, order, number):
    lane = lanes(value.shape)
    alive = jnp.where(lane < TILE, order[2, 2 * number], order[2, 2 * number + 1])
    return jnp.where(alive == 1, value, 0.0)


def part(ref, number, extent_x):
    return ref[number * extent_x : (number + 1) * extent_x]


def begin_body(
    count, heading, target, source, field, cotan, rate_x, rate_y,
    order, send_a, send_b, field_out, cotan_out, rate_x_out, rate_y_out,
    heading_in, target_in, source_in, used, sems, *, planes, extent_x,
):
    pairs = (
        (heading, heading_in), (target, target_in), (source, source_in),
        (cotan, cotan_out), (rate_x, rate_x_out), (field, field_out), (rate_y, rate_y_out),
    )
    copies = [pltpu.make_async_copy(a, b, sems.at[number]) for number, (a, b) in enumerate(pairs)]
    for copy in copies:
        copy.start()
    parity_x, parity_y = parities()
    for label in range(9):
        used[label] = 0
    lane = lanes((8, 128))
    for copy in copies[:3]:
        copy.wait()
    total = jnp.max(count[...]).astype(jnp.int32)
    asked = jnp.zeros((8, 128), jnp.int32)
    for slot in range(heading.shape[0]):
        toward = heading_in[slot]
        across = (toward >= 3).astype(jnp.int32) + (toward >= 6).astype(jnp.int32)
        ex = (across - 1) * (1 - 2 * parity_x)
        ey = (toward - 3 * across - 1) * (1 - 2 * parity_y)
        lx = jnp.where(ex == 0, 2, (ex + 1) // 2)
        ly = jnp.where(ey == 0, 2, (ey + 1) // 2)
        label = ly * 3 + lx
        spot = label * ROUTE_MOST + used[label]
        used[label] = used[label] + 1
        order[0, spot] = slot
        order[1, spot] = source_in[slot]
        order[2, spot] = (slot < total).astype(jnp.int32)
        wanted = jnp.where(slot < total, target_in[slot], 0)
        asked = jnp.where(lane == spot, wanted, asked)
    even = parity_x == 0
    high = extent_x - 3
    size = 3 * planes
    for out in (send_a, send_b):
        out[0:8, :] = asked.astype(jnp.float32)
    for number, ref in enumerate((cotan_out, rate_x_out, field_out)):
        copies[3 + number].wait()
        first = 8 + number * size
        send_a[first : first + size, :] = edge_rows(ref, jnp.where(even, 0, high), planes, extent_x)
        send_b[first : first + size, :] = edge_rows(ref, jnp.where(even, high, 0), planes, extent_x)
    copies[6].wait()


def extend_body(order, field, cotan, rate_y, blocks, pairs, picked, send_a, send_b, value_s, *, planes, extent_x):
    extra = 3 * extent_x
    for number, ref in enumerate((cotan, rate_y, field)):
        packed = edge_pack(ref, planes, extent_x)
        for out in (send_a, send_b):
            out[number * extent_x : (number + 1) * extent_x, :] = packed
    for number in range(18):
        one_block, two_block = blocks[order[0, 2 * number]], blocks[order[0, 2 * number + 1]]
        zero = jnp.zeros_like(one_block)
        joined = jnp.concatenate(
            [jnp.concatenate([one_block, zero], axis=1), jnp.concatenate([zero, two_block], axis=1)], axis=0
        )
        pairs[number] = joined
        tiles = tile_pair(field, order[1, 2 * number], order[1, 2 * number + 1], planes, extent_x)
        picked[number] = tiles
        value = pair_dot(alive_lanes(tiles, order, number), joined, 1)
        out, first = ((send_a, extra), (send_b, extra), (value_s, 0))[number // 6]
        first = first + number % 6 * planes
        out[first : first + planes, :] = value


def gather_tiles(asked, field, outs, first, planes, extent_x):
    for ly in range(3):

        for inner in range(6):
            at = ly * 12 + 2 * inner
            tiles = tile_pair(field, asked[ly, at], asked[ly, at + 1], planes, extent_x)
            outs[ly][first + inner * planes : first + (inner + 1) * planes, :] = tiles


def serve_body(request, got_a, got_b, from_a, from_b, cotan, asked, out_a, out_b, out_s, list_ref, sem, *, planes, extent_x):
    row = lax.broadcasted_iota(jnp.int32, (8, 128), 0)
    group = lax.rem(lanes((8, 128)), 12) // ROUTE_MOST
    merged = []
    for a, b, s in (
        (from_a[8:16], from_a[16:24], from_a[0:8]),
        (from_b[8:16], from_b[16:24], from_b[0:8]),
        (got_a[0:8], got_b[0:8], request[0:8]),
    ):
        merged.append(jnp.where(group == 0, a, jnp.where(group == 1, b, s))[0:1])
    spread = [jnp.broadcast_to(one, (8, 128)) for one in merged]
    joined = jnp.where(row == 0, spread[0], jnp.where(row == 1, spread[1], spread[2]))
    list_ref[...] = joined.astype(jnp.int32)
    copy = pltpu.make_async_copy(list_ref, asked, sem)
    copy.start()
    copy.wait()
    gather_tiles(asked, cotan, (out_a, out_b, out_s), 0, planes, extent_x)


def landed(lx, ly, half, planes, x_first, y_first, x_a, x_b, y_a, y_b, own):
    if lx == S:
        ref, first = (y_a, y_b, own)[ly], (0 if ly == S and own.shape[0] == 6 * planes else y_first) + (S * 2 + half) * planes
    else:
        ref, first = (x_a, x_b)[lx], x_first + ((1, 2, 0)[ly] * 2 + half) * planes
    return ref[first : first + planes, :]


LABELS = [(lx, ly, half) for ly in range(3) for lx in range(3) for half in range(2)]


def pull_y_body(cotan, rate_y, packs, packs_a, packs_b, grad, edge_rate, *, planes, extent_x):
    even_y = parities()[1] == 0
    halo = edge_join(part(packs_a, 0, extent_x), part(packs_b, 0, extent_x), even_y)
    halo_rate = edge_join(part(packs_a, 1, extent_x), part(packs_b, 1, extent_x), even_y)
    edge_rate[...] = halo_rate
    edges = adjoint_edges(part(packs, 0, extent_x), halo, part(packs, 1, extent_x), halo_rate)
    pulled = adjoint_y(cotan, rate_y, planes, extent_x)
    for z in range(planes):
        spot = pl.ds(z * extent_x, extent_x)
        rim = roll(edges, 125 - 8 * z)
        lane = lanes(rim.shape)
        rim = jnp.where((lane < 3) | (lane >= 125), rim, 0.0)
        main = pulled[z // 4][z % 4 * extent_x : (z % 4 + 1) * extent_x]
        grad[spot, :] = 0.5 * cotan[spot, :] + (0.5 * TIME_STEP) * (main * (1.0 / 60.0) + rim)


def pull_x_body(early, cotan, rate_x, rows_a, rows_b, grad, pad_rate, pad, up_ref, down_ref, *, planes, extent_x):
    even_x = parities()[0] == 0
    size = 3 * planes
    fill_padded(pad, cotan, rows_a[8 : 8 + size], rows_b[8 : 8 + size], even_x, planes, extent_x)
    fill_padded(pad_rate, rate_x, rows_a[8 + size : 8 + 2 * size], rows_b[8 + size : 8 + 2 * size], even_x, planes, extent_x)
    for z in range(planes):
        spot = pl.ds(z * extent_x, extent_x)
        grad[spot, :] = early[spot, :] + (0.5 * TIME_STEP) * adjoint_x(z, pad, pad_rate, up_ref, down_ref, extent_x)


def push_body(field, pad_rate, rate_y, edge_rate, rows_a, rows_b, packs, packs_a, packs_b, section, pad, flux_ref, *, planes, extent_x):
    parity_x, parity_y = parities()
    even_x, even_y = parity_x == 0, parity_y == 0
    first = 8 + 6 * planes
    fill_padded(pad, field, rows_a[first : first + 3 * planes], rows_b[first : first + 3 * planes], even_x, planes, extent_x)
    halo = edge_join(part(packs_a, 2, extent_x), part(packs_b, 2, extent_x), even_y)
    own_rate = part(packs, 1, extent_x)
    lane8 = lanes(halo.shape) % 8

    def shifted_by(value, k):
        return roll(value, -k) if k else value

    def stencils(value):
        up_part = sum(WEIGHTS[j] * shifted_by(value, j - 2) for j in range(5))
        down_part = sum(WEIGHTS[j] * shifted_by(value, 3 - j) for j in range(5))
        return up_part, down_part

    up_part, down_part = stencils(jnp.where(lane8 < 3, halo, jnp.where(lane8 < 6, part(packs, 2, extent_x), 0.0)))
    rate_up, rate_down = upwind(edge_rate[...])
    flux_low = roll(rate_up * up_part + rate_down * down_part, 1)
    rate_up, rate_down = upwind(own_rate)
    up_part, down_part = stencils(jnp.where((lane8 >= 3) & (lane8 < 6), halo, 0.0))
    flux_high = jnp.where(lane8 < 3, rate_up * up_part + rate_down * down_part, 0.0)
    up_part, down_part = stencils(jnp.where(lane8 < 3, halo, 0.0))
    flux_first = jnp.where((lane8 >= 3) & (lane8 < 5), rate_up * up_part + rate_down * down_part, 0.0)
    change_edge = roll(flux_high, 1) - flux_high
    before = jnp.where(lane8 == 3, flux_low, roll(flux_first, 1))
    change_edge = jnp.where(lane8 < 3, change_edge, jnp.where(lane8 < 6, before - flux_first, 0.0))
    both = jnp.concatenate([band({k: WEIGHTS[k + 2] for k in range(-2, 3)}, 128), band({k: WEIGHTS[3 - k] for k in range(-1, 4)}, 128)], axis=1)
    both = jnp.concatenate([both, both], axis=0)
    chunk_rows = 4 * extent_x
    fluxes = []
    for chunk in range(planes // 4):
        rows = slice(chunk * chunk_rows, (chunk + 1) * chunk_rows)
        parts = mix(jnp.concatenate(split(field[rows, :]), axis=1), both) * (1.0 / 60.0)
        rate_up, rate_down = upwind(rate_y[rows, :])
        fluxes.append(rate_up * parts[:, :128] + rate_down * parts[:, 128:])
    for z in range(planes):
        base = z * PAD
        spot = pl.ds(z * extent_x, extent_x)
        window = extent_x + 8
        near = {k: pad[pl.ds(base + 7 + k, window), :] for k in range(-2, 4)}
        rate_up, rate_down = upwind(pad_rate[pl.ds(base + 7, window), :])
        flux_ref[pl.ds(base, window), :] = rate_up * sum(WEIGHTS[j] * near[j - 2] for j in range(5)) + rate_down * sum(
            WEIGHTS[j] * near[3 - j] for j in range(5)
        )
        change = flux_ref[pl.ds(base, extent_x), :] - flux_ref[pl.ds(base + 1, extent_x), :]
        flux = fluxes[z // 4][z % 4 * extent_x : (z % 4 + 1) * extent_x]
        lane = lanes(flux.shape)
        rim = roll(change_edge, 125 - 8 * z)
        rim = jnp.where((lane < 3) | (lane >= 125), rim, 0.0)
        change = change + jnp.where(lane == 0, 0.0, roll(flux, 1)) - flux + rim
        section[spot, :] = field[spot, :] + TIME_STEP * change


def middle_body(order, asked, early, pairs, x_a, x_b, y_a, y_b, own, grad, returned, send_a, send_b, send_s, rows_a, rows_b, *, planes, extent_x):
    even_x = parities()[0] == 0
    for number, label in enumerate(LABELS):
        back = alive_lanes(landed(*label, planes, 0, 0, x_a, x_b, y_a, y_b, own), order, number)
        returned[number] = back
        pulled = (0.5 * TIME_STEP) * pair_dot(back, pairs[number], 0)
        add_tile_pair(grad, order[1, 2 * number], order[1, 2 * number + 1], pulled, planes, extent_x)
    packed = edge_pack(grad, planes, extent_x)
    for out in (send_a, send_b, send_s):
        out[0:extent_x, :] = packed
    gather_tiles(asked, grad, (send_a, send_b, send_s), extent_x, planes, extent_x)
    high = extent_x - 3
    rows_a[...] = edge_rows(grad, jnp.where(even_x, 0, high), planes, extent_x)
    rows_b[...] = edge_rows(grad, jnp.where(even_x, high, 0), planes, extent_x)


def inner_body(cotan, grad, pad_rate, rate_y, out, pad, up_ref, down_ref, *, planes, extent_x):
    high = 8 + extent_x
    for z in range(planes):
        pad[z * PAD + 8 : z * PAD + high, :] = grad[z * extent_x : (z + 1) * extent_x, :]
    for j in range(3):
        pad[pl.ds(5 + j, planes, PAD), :] = row_of(grad, 0, planes, extent_x)
        pad[pl.ds(high + j, planes, PAD), :] = row_of(grad, extent_x - 1, planes, extent_x)

    along_y = adjoint_y(grad, rate_y, planes, extent_x)
    for z in range(planes):
        spot = pl.ds(z * extent_x, extent_x)
        pulled = along_y[z // 4][z % 4 * extent_x : (z % 4 + 1) * extent_x] * (1.0 / 60.0)
        pulled = pulled + adjoint_x(z, pad, pad_rate, up_ref, down_ref, extent_x)
        out[spot, :] = 0.5 * cotan[spot, :] + grad[spot, :] + TIME_STEP * pulled


def outer(left, right):
    left_high, left_low = split(left)
    right_high, right_low = split(right)
    return lax.dot_general(
        jnp.concatenate([left_high, left_high, left_low], axis=0),
        jnp.concatenate([right_high, right_low, right_high], axis=0),
        (((0,), (0,)), ((), ())),
        preferred_element_type=jnp.float32,
    )


def section_body(order, asked, early, returned, x_a, x_b, y_a, y_b, own, section, first_outer, *, planes, extent_x):
    for number, (lx, ly, half) in enumerate(LABELS):
        came = TIME_STEP * landed(lx, ly, half, planes, 6 * planes, 3 * extent_x, x_a, x_b, y_a, y_b, own)
        at = ly * 12 + lx * ROUTE_MOST + 2 * half
        add_tile_pair(section, asked[ly, at], asked[ly, at + 1], came, planes, extent_x)

    for number in range(first_outer.shape[0]):
        picked = tile_pair(section, order[1, 2 * number], order[1, 2 * number + 1], planes, extent_x)
        first_outer[number] = outer((0.5 * TIME_STEP) * returned[number], picked)


def last_body(
    order, early, grad, pad_rate, edge_rate, packs, own, y_a, y_b, x_a, x_b, pairs, first_outer, picked, out, out_blocks, work, total, blocks, sems,
    *, planes, extent_x,
):
    parity_x, parity_y = parities()
    even_x, even_y = parity_x == 0, parity_y == 0
    size = 3 * planes
    halo = edge_join(y_a[0:extent_x], y_b[0:extent_x], even_y)
    edges = adjoint_edges(own[0:extent_x], halo, part(packs, 1, extent_x), edge_rate[...])

    for z in range(planes):
        spot = pl.ds(z * extent_x, extent_x)
        rim = roll(edges, 125 - 8 * z)
        lane = lanes(rim.shape)
        total[spot, :] = early[spot, :] + TIME_STEP * jnp.where((lane < 3) | (lane >= 125), rim, 0.0)
    low_rows = [jnp.where(even_x, x_a[j * planes : (j + 1) * planes], x_b[j * planes : (j + 1) * planes]) for j in range(3)]
    high_rows = [jnp.where(even_x, x_b[j * planes : (j + 1) * planes], x_a[j * planes : (j + 1) * planes]) for j in range(3)]
    first_cell = row_of(grad, 0, planes, extent_x)
    last_cell = row_of(grad, extent_x - 1, planes, extent_x)
    for line, low_face in ((low_rows + [first_cell], -3), ([last_cell] + high_rows, extent_x - 1)):
        faces = []
        for j in range(3):
            rate_up, rate_down = upwind(row_of(pad_rate, 8 + low_face + j, planes, PAD))
            jump = line[j + 1] - line[j]
            faces.append((rate_up * jump, rate_down * jump))
        cells = range(0, 3) if low_face < 0 else range(extent_x - 3, extent_x)
        for cell in cells:
            added = 0.0
            for j in range(3):
                k = low_face + j - cell
                if -3 <= k <= 2:
                    added = added + combine(*faces[j], k)
            spot = pl.ds(cell, planes, extent_x)
            total[spot, :] = total[spot, :] + TIME_STEP * added
    backs = []
    for number, label in enumerate(LABELS):
        back = alive_lanes(landed(*label, planes, size, extent_x, x_a, x_b, y_a, y_b, own), order, number)
        backs.append(back)
        pulled = TIME_STEP * pair_dot(back, pairs[number], 0)
        add_tile_pair(total, order[1, 2 * number], order[1, 2 * number + 1], pulled, planes, extent_x)
    copies = [pltpu.make_async_copy(total, out, sems.at[0]), pltpu.make_async_copy(blocks, out_blocks, sems.at[1])]
    copies[0].start()
    half_lane = lanes((TILE // 2, 128)) < TILE
    for number, back in enumerate(backs):
        work[number] = first_outer[number] + outer(TIME_STEP * back, picked[number])
        for which in range(2):
            slot = order[0, 2 * number + which]
            even_rows = work[number, pl.ds(which * TILE, TILE // 2, 2), :]
            odd_rows = work[number, pl.ds(which * TILE + 1, TILE // 2, 2), :]
            if which == 0:
                merged = jnp.where(half_lane, even_rows, roll(odd_rows, TILE))
            else:
                merged = jnp.where(half_lane, roll(even_rows, TILE), odd_rows)
            blocks[pl.ds(pl.multiple_of(slot * (TILE // 2), 8), TILE // 2), :] = merged
    copies[1].start()
    for copy in copies:
        copy.wait()


SPACE = {"v": pltpu.VMEM, "s": pltpu.SMEM, "h": pltpu.HBM}


def call(body, ins, outs, scratch=(), alias=None, **sizes):
    values, specs, shapes, out_specs = [], [], [], []
    for kind, group in ins:
        for value in group:
            values.append(value if kind == "r" else pltpu.with_memory_space_constraint(value, SPACE[kind]))
            specs.append(pl.BlockSpec(memory_space=SPACE["s" if kind == "r" else kind]))
    for shape, dtype, kind in outs:
        shapes.append(SPACE[kind](shape, dtype))
        out_specs.append(pl.BlockSpec(memory_space=SPACE[kind]))
    return pl.pallas_call(
        functools.partial(body, **sizes),
        out_shape=tuple(shapes),
        in_specs=specs,
        out_specs=tuple(out_specs),
        scratch_shapes=list(scratch),
        input_output_aliases=alias or {},
        compiler_params=pltpu.CompilerParams(vmem_limit_bytes=VMEM_LIMIT),
        name=body.__name__,
    )(*values)


def shards(
    level_set, speed_x, speed_y, cotangent, blocks, tile_count, source_tile, dest_offset, dest_tile
):
    planes, extent_x, extent_y = level_set.shape
    slots = source_tile.shape[2]
    cells = planes * extent_x
    f32, i32 = jnp.float32, jnp.int32
    field, rate_x, rate_y, cotan = (v.reshape(cells, extent_y) for v in (level_set, speed_x, speed_y, cotangent))
    sizes = dict(planes=planes, extent_x=extent_x)
    size = 3 * planes
    pair_total = slots // 2
    box = ((2 * size, 128), f32, "v")
    padded = ((planes * PAD + 8, extent_y), f32)
    pad_scratch = pltpu.VMEM(*padded)
    whole = ((cells, 128), f32, "v")

    order, send_a, send_b, field, cotan, rate_x, rate_y = call(
        begin_body,
        [("v", [jnp.broadcast_to(tile_count.reshape(1, 1), (8, 128)).astype(f32)]), ("h", [v.reshape(slots) for v in (dest_offset, dest_tile, source_tile)] + [field, cotan, rate_x, rate_y])],
        [((3, slots), i32, "s")] + [((8 + 3 * size, 128), f32, "v")] * 2 + [whole] * 4,
        scratch=[pltpu.SMEM((slots,), i32)] * 3 + [pltpu.SMEM((9,), i32), pltpu.SemaphoreType.DMA((7,))],
        **sizes,
    )
    rows_a = exchange(send_a, "gx", A)
    rows_b = exchange(send_b, "gx", B)
    column = jnp.concatenate([send_a[:8], rows_a[:8], rows_b[:8]], axis=0)
    extra = 3 * extent_x
    pairs, picked, wide_a, wide_b, value_s = call(
        extend_body, [("s", [order]), ("v", [field, cotan, rate_y, blocks.reshape(slots, TILE, TILE)])],
        [((pair_total, 128, 128), jnp.bfloat16, "v"), ((pair_total, planes, 128), f32, "v")]
        + [((extra + 2 * size, 128), f32, "v")] * 2 + [box], **sizes,
    )
    column, wide_a, wide_b = lax.optimization_barrier((column, wide_a, wide_b))
    from_b = exchange(column, "gy", B)
    from_a = exchange(column, "gy", A)
    packs_b = exchange(wide_b, "gy", B)
    packs_a = exchange(wide_a, "gy", A)

    asked, tiles_a, tiles_b, tiles_s = call(
        serve_body, [("v", [send_a, rows_a, rows_b, from_a, from_b, cotan])],
        [((8, 128), i32, "s"), box, box, box], scratch=(pltpu.VMEM((8, 128), i32), pltpu.SemaphoreType.DMA(())), **sizes,
    )
    y_b = exchange(tiles_b, "gy", B)
    y_a = exchange(tiles_a, "gy", A)
    early, edge_rate = call(
        pull_y_body, [("v", [cotan, rate_y, wide_a, packs_a, packs_b])], [whole, ((extent_x, 128), f32, "v")], **sizes,
    )
    y_a, y_b, early = lax.optimization_barrier((y_a, y_b, early))

    def onward(own, a, b, own_first, first, m):
        cut = lambda v, start: v[start + m * 2 * planes : start + (m + 1) * 2 * planes]
        return [cut(own, own_first), cut(a, first), cut(b, first)]

    both = lambda m: jnp.concatenate(onward(tiles_s, y_a, y_b, 0, 0, m) + onward(value_s, packs_a, packs_b, 0, extra, m), axis=0)
    x_b = exchange(both(B), "gx", B)
    x_a = exchange(both(A), "gx", A)
    early, pad_rate = call(
        pull_x_body, [("v", [early, cotan, rate_x, rows_a, rows_b])], [whole, padded + ("v",)],
        scratch=(pad_scratch,) * 3, alias={0: 0}, **sizes,
    )
    grad, returned, send_a, send_b, send_s, edge_a, edge_b = call(
        middle_body, [("s", [order, asked]), ("v", [early, pairs, x_a, x_b, y_a, y_b, tiles_s])],
        [whole, ((pair_total, planes, 128), f32, "v")] + [((extent_x + 2 * size, 128), f32, "v")] * 3 + [((size, 128), f32, "v")] * 2,
        alias={2: 0}, **sizes,
    )
    send_a, send_b, field = lax.optimization_barrier((send_a, send_b, field))
    last_y_b = exchange(send_b, "gy", B)
    last_y_a = exchange(send_a, "gy", A)
    (pushed,) = call(
        push_body, [("v", [field, pad_rate, rate_y, edge_rate, rows_a, rows_b, wide_a, packs_a, packs_b])],
        [whole], scratch=(pad_scratch,) * 2, **sizes,
    )
    last_y_a, last_y_b, pushed = lax.optimization_barrier((last_y_a, last_y_b, pushed))
    last_x_b = exchange(jnp.concatenate([edge_b] + onward(send_s, last_y_a, last_y_b, extent_x, extent_x, B), axis=0), "gx", B)
    last_x_a = exchange(jnp.concatenate([edge_a] + onward(send_s, last_y_a, last_y_b, extent_x, extent_x, A), axis=0), "gx", A)
    (inner,) = call(
        inner_body, [("v", [cotan, grad, pad_rate, rate_y])], [whole], scratch=(pad_scratch,) * 3, **sizes,
    )
    section, first_outer = call(
        section_body, [("s", [order, asked]), ("v", [pushed, returned, x_a, x_b, packs_a, packs_b, value_s])],
        [whole, ((pair_total, 128, 128), f32, "v")], alias={2: 0}, **sizes,
    )
    grad_level_set, grad_blocks = call(
        last_body,
        [("s", [order]), ("v", [inner, grad, pad_rate, edge_rate, wide_a, send_s, last_y_a, last_y_b, last_x_a, last_x_b, pairs, first_outer, picked])],
        [((cells, 128), f32, "h"), ((slots * TILE // 2, 128), f32, "h")],
        scratch=(pltpu.VMEM((pair_total, 128, 128), f32), pltpu.VMEM((cells, 128), f32),
                 pltpu.VMEM((slots * TILE // 2, 128), f32), pltpu.SemaphoreType.DMA((2,))), **sizes,
    )
    return (grad_level_set.reshape(planes, extent_x, extent_y), grad_blocks.reshape(1, 1, slots, TILE * TILE))


def solution(mesh):
    return jax.shard_map(
        shards,
        mesh=mesh,
        in_specs=(
            P(None, "gx", "gy"),
            P(None, "gx", "gy"),
            P(None, "gx", "gy"),
            P(None, "gx", "gy"),
            P("gx", "gy", None, None),
            P("gx", "gy"),
            P("gx", "gy", None),
            P("gx", "gy", None),
            P("gx", "gy", None),
        ),
        out_specs=(P(None, "gx", "gy"), P("gx", "gy", None, None)),
        check_vma=False,
    )
```

```python
import functools

import jax
import jax.numpy as jnp
from jax import lax
from jax.experimental import pallas as pl
from jax.experimental.pallas import tpu as pltpu
from jax.sharding import PartitionSpec as P

TILE = 64
ROUTE_MOST = 4
TIME_STEP = 0.3
WEIGHTS = (2.0 / 60.0, -13.0 / 60.0, 47.0 / 60.0, 27.0 / 60.0, -3.0 / 60.0)
PAD = 80
VMEM_LIMIT = 16 << 20

A, B, S = 0, 1, 2


def matching(count, which):
    return [(i, (i + (1 if (i % 2 == 0) == (which == B) else -1)) % count) for i in range(count)]


def exchange(block, axis, which):
    return lax.ppermute(block, axis, matching(lax.axis_size(axis), which))


def lanes(shape):
    return lax.broadcasted_iota(jnp.int32, shape, len(shape) - 1)


def roll(value, shift):
    return pltpu.roll(value, shift % 128 if isinstance(shift, int) else shift, axis=value.ndim - 1)


def split(value):
    high = value.astype(jnp.bfloat16)
    return high, (value - high.astype(jnp.float32)).astype(jnp.bfloat16)


def pair_dot(value, matrix, over):
    high, low = split(value)
    both = lax.dot_general(
        jnp.concatenate([high, low], axis=0),
        matrix,
        (((1,), (over,)), ((), ())),
        preferred_element_type=jnp.float32,
    )
    rows = value.shape[0]
    return both[:rows] + both[rows:]


def row_of(ref, x, planes, stride):
    return ref[pl.ds(x, planes, stride), :]


def tile_pair(ref, first, second, planes, extent_x):
    one = row_of(ref, first // 2, planes, extent_x)
    two = row_of(ref, second // 2, planes, extent_x)
    lane = lanes(one.shape)
    one = jnp.where(first % 2 == 0, one, roll(one, TILE))
    two = jnp.where(second % 2 == 1, two, roll(two, TILE))
    return jnp.where(lane < TILE, one, two)


def add_tile_pair(ref, first, second, value, planes, extent_x):
    lane = lanes(value.shape)
    turned = roll(value, TILE)
    for tile, half in ((first, 0), (second, 1)):
        spot = pl.ds(tile // 2, planes, extent_x)
        placed = jnp.where(tile % 2 == half, value, turned)
        keep = (lane // TILE) == tile % 2
        ref[spot, :] = ref[spot, :] + jnp.where(keep, placed, 0.0)


def edge_pack(ref, planes, extent_x):
    lane = lanes((extent_x, 128))
    packed = jnp.zeros((extent_x, 128), jnp.float32)
    for z in range(planes):
        plane = ref[z * extent_x : (z + 1) * extent_x, :]
        packed = jnp.where(lane // 8 == z, roll(plane, 8 * z + 3), packed)
    return packed


def edge_rows(ref, start, planes, extent_x):
    return jnp.concatenate([row_of(ref, start + j, planes, extent_x) for j in range(3)], axis=0)


def upwind(face_rate):
    return jnp.maximum(face_rate, 0.0), jnp.minimum(face_rate, 0.0)


UP = {2: WEIGHTS[0], 1: WEIGHTS[1], 0: WEIGHTS[2], -1: WEIGHTS[3], -2: WEIGHTS[4]}
DOWN = {1: WEIGHTS[4], 0: WEIGHTS[3], -1: WEIGHTS[2], -2: WEIGHTS[1], -3: WEIGHTS[0]}


def combine(up_part, down_part, k):
    total = 0.0
    if k in UP:
        total = total + UP[k] * up_part
    if k in DOWN:
        total = total + DOWN[k] * down_part
    return total


def fill_padded(pad_ref, field_ref, rows_a, rows_b, even, planes, extent_x):
    high = 8 + extent_x
    at_a = jnp.where(even, 5, high)
    at_b = jnp.where(even, high, 5)
    for z in range(planes):
        pad_ref[z * PAD + 8 : z * PAD + high, :] = field_ref[z * extent_x : (z + 1) * extent_x, :]
    for j in range(3):
        part = slice(j * planes, (j + 1) * planes)
        pad_ref[pl.ds(at_a + j, planes, PAD), :] = rows_a[part]
        pad_ref[pl.ds(at_b + j, planes, PAD), :] = rows_b[part]


def edge_join(from_a, from_b, even):
    low = jnp.where(even, from_a, from_b)
    high = jnp.where(even, from_b, from_a)
    return jnp.where(lanes(low.shape) % 8 < 3, low, high)


def adjoint_edges(own, halo, own_rate, halo_rate):
    lane = lanes(own.shape) % 8
    after = roll(jnp.where(lane == 3, own, halo), -1)
    before = roll(jnp.where(lane == 2, own, halo), 1)
    jump = jnp.where(lane < 3, after - halo, halo - before)
    rate = jnp.where(lane < 3, halo_rate, roll(jnp.where(lane == 2, own_rate, halo_rate), 1))
    rate_up, rate_down = upwind(rate)
    up_part, down_part = rate_up * jump, rate_down * jump
    low_side = 0.0
    high_side = 0.0
    for k in (-1, -2, -3):
        part = jnp.where(lane < 3, combine(up_part, down_part, k), 0.0)
        low_side = low_side + roll(part, -k)
    for k in (0, 1, 2):
        part = jnp.where((lane >= 3) & (lane < 6), combine(up_part, down_part, k), 0.0)
        high_side = high_side + roll(part, -(k + 1))
    return jnp.where(lane < 3, high_side, jnp.where(lane < 6, low_side, 0.0))


def adjoint_x(z, pad_ref, pad_rate_ref, up_ref, down_ref, extent_x):
    base = z * PAD
    here = pad_ref[pl.ds(base, PAD), :]
    jump = pad_ref[pl.ds(base + 1, PAD), :] - here
    rate_up, rate_down = upwind(pad_rate_ref[pl.ds(base, PAD), :])
    up_ref[pl.ds(base, PAD), :] = rate_up * jump
    down_ref[pl.ds(base, PAD), :] = rate_down * jump
    total = 0.0
    for k in range(-3, 3):
        if k in UP:
            total = total + UP[k] * up_ref[pl.ds(base + 8 + k, extent_x), :]
        if k in DOWN:
            total = total + DOWN[k] * down_ref[pl.ds(base + 8 + k, extent_x), :]
    return total


def band(weights, first_lost):
    row = lax.broadcasted_iota(jnp.int32, (128, 128), 0)
    gap = row - lax.broadcasted_iota(jnp.int32, (128, 128), 1)
    matrix = jnp.zeros((128, 128), jnp.float32)
    for k, weight in weights.items():
        matrix = jnp.where(gap == k, float(round(60.0 * weight)), matrix)
    return jnp.where(row >= first_lost, 0.0, matrix).astype(jnp.bfloat16)


def mix(left, matrix):
    return lax.dot_general(left, matrix, (((1,), (0,)), ((), ())), preferred_element_type=jnp.float32)


def adjoint_y(field_ref, rate_y_ref, planes, extent_x):
    up_matrix, down_matrix = band(UP, 127), band(DOWN, 127)
    matrix = jnp.concatenate([up_matrix, up_matrix, down_matrix, down_matrix], axis=0)
    rows = 4 * extent_x
    results = []
    for chunk in range(planes // 4):
        field = field_ref[chunk * rows : (chunk + 1) * rows, :]
        jump = roll(field, -1) - field
        rate_up, rate_down = upwind(rate_y_ref[chunk * rows : (chunk + 1) * rows, :])
        left = jnp.concatenate(split(rate_up * jump) + split(rate_down * jump), axis=1)
        results.append(mix(left, matrix))
    return results


LABELS = [(lx, ly, half) for ly in range(3) for lx in range(3) for half in range(2)]


def parities():
    return lax.rem(lax.axis_index("gx"), 2), lax.rem(lax.axis_index("gy"), 2)


def alive_lanes(value, order, number, total):
    lane = lanes(value.shape)
    return jnp.where(jnp.where(lane < TILE, order[0, 2 * number], order[0, 2 * number + 1]) < total, value, 0.0)


def part(ref, number, extent_x):
    return ref[number * extent_x : (number + 1) * extent_x]


def begin_body(
    heading, target, source, field, cotan, rate_x, rate_y,
    order, send_a, send_b, field_out, cotan_out, rate_x_out, rate_y_out,
    heading_in, target_in, source_in, used, sems, *, planes, extent_x,
):
    pairs = (
        (heading, heading_in), (target, target_in), (source, source_in),
        (cotan, cotan_out), (rate_x, rate_x_out), (field, field_out), (rate_y, rate_y_out),
    )
    copies = [pltpu.make_async_copy(a, b, sems.at[number]) for number, (a, b) in enumerate(pairs)]
    for copy in copies:
        copy.start()
    parity_x, parity_y = parities()
    for label in range(9):
        used[label] = 0
    lane = lanes((8, 128))
    for copy in copies[:3]:
        copy.wait()
    asked = jnp.zeros((8, 128), jnp.int32)
    for slot in range(heading.shape[0]):
        toward = heading_in[slot]
        across = (toward >= 3).astype(jnp.int32) + (toward >= 6).astype(jnp.int32)
        ex = (across - 1) * (1 - 2 * parity_x)
        ey = (toward - 3 * across - 1) * (1 - 2 * parity_y)
        lx = jnp.where(ex == 0, 2, (ex + 1) // 2)
        ly = jnp.where(ey == 0, 2, (ey + 1) // 2)
        label = ly * 3 + lx
        spot = label * ROUTE_MOST + used[label]
        used[label] = used[label] + 1
        order[0, spot] = slot
        order[1, spot] = source_in[slot]
        asked = jnp.where(lane == spot, target_in[slot], asked)
    even = parity_x == 0
    high = extent_x - 3
    size = 3 * planes
    for out in (send_a, send_b):
        out[0:8, :] = asked.astype(jnp.float32)
    for number, ref in enumerate((cotan_out, rate_x_out, field_out)):
        copies[3 + number].wait()
        first = 8 + number * size
        send_a[first : first + size, :] = edge_rows(ref, jnp.where(even, 0, high), planes, extent_x)
        send_b[first : first + size, :] = edge_rows(ref, jnp.where(even, high, 0), planes, extent_x)
    copies[6].wait()


def extend_body(order, count, field, cotan, rate_y, blocks, pairs, picked, packs, value_a, value_b, value_s, *, planes, extent_x):
    for number, ref in enumerate((rate_y, field, cotan)):
        packs[number * extent_x : (number + 1) * extent_x, :] = edge_pack(ref, planes, extent_x)
    total = count[0, 0]
    for number, (lx, ly, half) in enumerate(LABELS):
        one_block, two_block = blocks[order[0, 2 * number]], blocks[order[0, 2 * number + 1]]
        zero = jnp.zeros_like(one_block)
        joined = jnp.concatenate(
            [jnp.concatenate([one_block, zero], axis=1), jnp.concatenate([zero, two_block], axis=1)], axis=0
        )
        pairs[number] = joined
        tiles = tile_pair(field, order[1, 2 * number], order[1, 2 * number + 1], planes, extent_x)
        picked[number] = tiles
        first = (ly * 2 + half) * planes
        value = pair_dot(alive_lanes(tiles, order, number, total), joined, 1)
        (value_a, value_b, value_s)[lx][first : first + planes, :] = value


def merge_lists(a, b, s):
    group = lax.rem(lanes((8, 128)), 12) // ROUTE_MOST
    return jnp.where(group == 0, a, jnp.where(group == 1, b, s)).astype(jnp.int32)


def to_scalars(value, list_ref, asked, sem):
    list_ref[...] = value
    copy = pltpu.make_async_copy(list_ref, asked, sem)
    copy.start()
    copy.wait()


def serve_body(request, got_a, got_b, cotan_a, cotan_b, cotan, out_a, out_b, out_s, list_ref, asked, sem, *, planes, extent_x):
    to_scalars(merge_lists(got_a[0:8], got_b[0:8], request[0:8]), list_ref, asked, sem)
    for lx, ly, half in LABELS:
        at = ly * 12 + lx * ROUTE_MOST + 2 * half
        tiles = tile_pair((cotan_a, cotan_b, cotan)[ly], asked[0, at], asked[0, at + 1], planes, extent_x)
        first = (ly * 2 + half) * planes
        (out_a, out_b, out_s)[lx][first : first + planes, :] = tiles


def gather_tiles(asked, field, outs, first, planes, extent_x):
    for ly in range(3):
        for inner in range(6):
            at = ly * 12 + 2 * inner
            tiles = tile_pair(field, asked[ly, at], asked[ly, at + 1], planes, extent_x)
            outs[ly][first + inner * planes : first + (inner + 1) * planes, :] = tiles


def rows_at(ref, first, planes):
    return ref[first : first + planes, :]


def pull_y_body(
    cotan, cotan_a, cotan_b, rate_y, packs, request, got_a, got_b, from_a, from_b, grad, edge_rate, asked, list_ref, joined, sem,
    *, planes, extent_x,
):
    row = lax.broadcasted_iota(jnp.int32, (8, 128), 0)
    spread = [
        jnp.broadcast_to(merge_lists(a, b, c)[0:1], (8, 128))
        for a, b, c in (
            (from_a[8:16], from_a[16:24], from_a[0:8]),
            (from_b[8:16], from_b[16:24], from_b[0:8]),
            (got_a[0:8], got_b[0:8], request[0:8]),
        )
    ]
    list_ref[...] = jnp.where(row == 0, spread[0], jnp.where(row == 1, spread[1], spread[2]))
    copy = pltpu.make_async_copy(list_ref, asked, sem)
    copy.start()
    even_y = parities()[1] == 0
    lane = lanes((extent_x, 128))
    upper = jnp.where(even_y, lane, 127 - lane) >= TILE
    for z in range(planes):
        plane = slice(z * extent_x, (z + 1) * extent_x)
        joined[plane, :] = jnp.where(upper, cotan_a[plane, :], cotan_b[plane, :])
    halo = edge_pack(joined, planes, extent_x)
    halo_rate = edge_join(from_a[24 : 24 + extent_x], from_b[24 : 24 + extent_x], even_y)
    edge_rate[...] = halo_rate
    edges = adjoint_edges(part(packs, 2, extent_x), halo, part(packs, 0, extent_x), halo_rate)
    pulled = adjoint_y(cotan, rate_y, planes, extent_x)
    for z in range(planes):
        spot = pl.ds(z * extent_x, extent_x)
        rim = roll(edges, 125 - 8 * z)
        rim = jnp.where((lane < 3) | (lane >= 125), rim, 0.0)
        main = pulled[z // 4][z % 4 * extent_x : (z % 4 + 1) * extent_x]
        grad[spot, :] = 0.5 * cotan[spot, :] + (0.5 * TIME_STEP) * (main * (1.0 / 60.0) + rim)
    copy.wait()


def pull_x_body(early, cotan, rate_x, rows_a, rows_b, grad, pad_rate, pad, up_ref, down_ref, *, planes, extent_x):
    even_x = parities()[0] == 0
    size = 3 * planes
    fill_padded(pad, cotan, rows_a[8 : 8 + size], rows_b[8 : 8 + size], even_x, planes, extent_x)
    fill_padded(pad_rate, rate_x, rows_a[8 + size : 8 + 2 * size], rows_b[8 + size : 8 + 2 * size], even_x, planes, extent_x)
    for z in range(planes):
        spot = pl.ds(z * extent_x, extent_x)
        grad[spot, :] = early[spot, :] + (0.5 * TIME_STEP) * adjoint_x(z, pad, pad_rate, up_ref, down_ref, extent_x)


def push_body(field, pad_rate, rate_y, edge_rate, rows_a, rows_b, packs, packs_a, packs_b, section, pad, flux_ref, *, planes, extent_x):
    parity_x, parity_y = parities()
    even_x, even_y = parity_x == 0, parity_y == 0
    first = 8 + 6 * planes
    fill_padded(pad, field, rows_a[first : first + 3 * planes], rows_b[first : first + 3 * planes], even_x, planes, extent_x)
    second = slice(24 + extent_x, 24 + 2 * extent_x)
    halo = edge_join(packs_a[second], packs_b[second], even_y)
    own_rate = part(packs, 0, extent_x)
    lane8 = lanes(halo.shape) % 8

    def shifted_by(value, k):
        return roll(value, -k) if k else value

    def stencils(value):
        up_part = sum(WEIGHTS[j] * shifted_by(value, j - 2) for j in range(5))
        down_part = sum(WEIGHTS[j] * shifted_by(value, 3 - j) for j in range(5))
        return up_part, down_part

    up_part, down_part = stencils(jnp.where(lane8 < 3, halo, jnp.where(lane8 < 6, part(packs, 1, extent_x), 0.0)))
    rate_up, rate_down = upwind(edge_rate[...])
    flux_low = roll(rate_up * up_part + rate_down * down_part, 1)
    rate_up, rate_down = upwind(own_rate)
    up_part, down_part = stencils(jnp.where((lane8 >= 3) & (lane8 < 6), halo, 0.0))
    flux_high = jnp.where(lane8 < 3, rate_up * up_part + rate_down * down_part, 0.0)
    up_part, down_part = stencils(jnp.where(lane8 < 3, halo, 0.0))
    flux_first = jnp.where((lane8 >= 3) & (lane8 < 5), rate_up * up_part + rate_down * down_part, 0.0)
    change_edge = roll(flux_high, 1) - flux_high
    before = jnp.where(lane8 == 3, flux_low, roll(flux_first, 1))
    change_edge = jnp.where(lane8 < 3, change_edge, jnp.where(lane8 < 6, before - flux_first, 0.0))
    both = jnp.concatenate([band({k: WEIGHTS[k + 2] for k in range(-2, 3)}, 128), band({k: WEIGHTS[3 - k] for k in range(-1, 4)}, 128)], axis=1)
    both = jnp.concatenate([both, both], axis=0)
    chunk_rows = 4 * extent_x
    fluxes = []
    for chunk in range(planes // 4):
        rows = slice(chunk * chunk_rows, (chunk + 1) * chunk_rows)
        parts = mix(jnp.concatenate(split(field[rows, :]), axis=1), both) * (1.0 / 60.0)
        rate_up, rate_down = upwind(rate_y[rows, :])
        fluxes.append(rate_up * parts[:, :128] + rate_down * parts[:, 128:])
    for z in range(planes):
        base = z * PAD
        spot = pl.ds(z * extent_x, extent_x)
        window = extent_x + 8
        near = {k: pad[pl.ds(base + 7 + k, window), :] for k in range(-2, 4)}
        rate_up, rate_down = upwind(pad_rate[pl.ds(base + 7, window), :])
        flux_ref[pl.ds(base, window), :] = rate_up * sum(WEIGHTS[j] * near[j - 2] for j in range(5)) + rate_down * sum(
            WEIGHTS[j] * near[3 - j] for j in range(5)
        )
        change = flux_ref[pl.ds(base, extent_x), :] - flux_ref[pl.ds(base + 1, extent_x), :]
        flux = fluxes[z // 4][z % 4 * extent_x : (z % 4 + 1) * extent_x]
        lane = lanes(flux.shape)
        rim = roll(change_edge, 125 - 8 * z)
        rim = jnp.where((lane < 3) | (lane >= 125), rim, 0.0)
        change = change + jnp.where(lane == 0, 0.0, roll(flux, 1)) - flux + rim
        section[spot, :] = field[spot, :] + TIME_STEP * change


def middle_body(order, asked, count, early, pairs, x_a, x_b, own, grad, returned, send_a, send_b, send_s, rows_a, rows_b, *, planes, extent_x):
    even_x = parities()[0] == 0
    alive = count[0, 0]
    for number, (lx, ly, half) in enumerate(LABELS):
        back = rows_at((x_a, x_b, own)[lx], (ly * 2 + half) * planes, planes)
        back = alive_lanes(back, order, number, alive)
        returned[number] = back
        pulled = (0.5 * TIME_STEP) * pair_dot(back, pairs[number], 0)
        add_tile_pair(grad, order[1, 2 * number], order[1, 2 * number + 1], pulled, planes, extent_x)
    packed = edge_pack(grad, planes, extent_x)
    for out in (send_a, send_b, send_s):
        out[0:extent_x, :] = packed
    gather_tiles(asked, grad, (send_a, send_b, send_s), extent_x, planes, extent_x)
    high = extent_x - 3
    rows_a[...] = edge_rows(grad, jnp.where(even_x, 0, high), planes, extent_x)
    rows_b[...] = edge_rows(grad, jnp.where(even_x, high, 0), planes, extent_x)


def inner_body(cotan, grad, pad_rate, rate_y, out, pad, up_ref, down_ref, *, planes, extent_x):
    high = 8 + extent_x
    for z in range(planes):
        pad[z * PAD + 8 : z * PAD + high, :] = grad[z * extent_x : (z + 1) * extent_x, :]
    for j in range(3):
        pad[pl.ds(5 + j, planes, PAD), :] = row_of(grad, 0, planes, extent_x)
        pad[pl.ds(high + j, planes, PAD), :] = row_of(grad, extent_x - 1, planes, extent_x)

    along_y = adjoint_y(grad, rate_y, planes, extent_x)
    for z in range(planes):
        spot = pl.ds(z * extent_x, extent_x)
        pulled = along_y[z // 4][z % 4 * extent_x : (z % 4 + 1) * extent_x] * (1.0 / 60.0)
        pulled = pulled + adjoint_x(z, pad, pad_rate, up_ref, down_ref, extent_x)
        out[spot, :] = 0.5 * cotan[spot, :] + grad[spot, :] + TIME_STEP * pulled


def outer(left, right):
    left_high, left_low = split(left)
    right_high, right_low = split(right)
    return lax.dot_general(
        jnp.concatenate([left_high, left_high, left_low], axis=0),
        jnp.concatenate([right_high, right_low, right_high], axis=0),
        (((0,), (0,)), ((), ())),
        preferred_element_type=jnp.float32,
    )


def section_body(order, asked, early, returned, x_a, x_b, y_a, y_b, own, section, first_outer, *, planes, extent_x):
    for number, (lx, ly, half) in enumerate(LABELS):
        if ly == S:
            came = rows_at((x_a, x_b, own)[lx], (0 if lx == S else 6 * planes) + (S * 2 + half) * planes, planes)
        else:
            came = rows_at((y_a, y_b)[ly], ((1, 2, 0)[lx] * 2 + half) * planes, planes)
        came = TIME_STEP * came
        at = ly * 12 + lx * ROUTE_MOST + 2 * half
        add_tile_pair(section, asked[ly, at], asked[ly, at + 1], came, planes, extent_x)

    for number in range(first_outer.shape[0]):
        picked = tile_pair(section, order[1, 2 * number], order[1, 2 * number + 1], planes, extent_x)
        first_outer[number] = outer((0.5 * TIME_STEP) * returned[number], picked)


def last_body(
    order, count, early, grad, pad_rate, edge_rate, packs, own, y_a, y_b, x_a, x_b, pairs, first_outer, picked, out, out_blocks, work, total, blocks, sems,
    *, planes, extent_x,
):
    parity_x, parity_y = parities()
    even_x, even_y = parity_x == 0, parity_y == 0
    size = 3 * planes
    halo = edge_join(y_a[0:extent_x], y_b[0:extent_x], even_y)
    edges = adjoint_edges(own[0:extent_x], halo, part(packs, 0, extent_x), edge_rate[...])

    for z in range(planes):
        spot = pl.ds(z * extent_x, extent_x)
        rim = roll(edges, 125 - 8 * z)
        lane = lanes(rim.shape)
        total[spot, :] = early[spot, :] + TIME_STEP * jnp.where((lane < 3) | (lane >= 125), rim, 0.0)
    low_rows = [jnp.where(even_x, x_a[j * planes : (j + 1) * planes], x_b[j * planes : (j + 1) * planes]) for j in range(3)]
    high_rows = [jnp.where(even_x, x_b[j * planes : (j + 1) * planes], x_a[j * planes : (j + 1) * planes]) for j in range(3)]
    first_cell = row_of(grad, 0, planes, extent_x)
    last_cell = row_of(grad, extent_x - 1, planes, extent_x)
    for line, low_face in ((low_rows + [first_cell], -3), ([last_cell] + high_rows, extent_x - 1)):
        faces = []
        for j in range(3):
            rate_up, rate_down = upwind(row_of(pad_rate, 8 + low_face + j, planes, PAD))
            jump = line[j + 1] - line[j]
            faces.append((rate_up * jump, rate_down * jump))
        cells = range(0, 3) if low_face < 0 else range(extent_x - 3, extent_x)
        for cell in cells:
            added = 0.0
            for j in range(3):
                k = low_face + j - cell
                if -3 <= k <= 2:
                    added = added + combine(*faces[j], k)
            spot = pl.ds(cell, planes, extent_x)
            total[spot, :] = total[spot, :] + TIME_STEP * added
    backs = []
    for number, label in enumerate(LABELS):
        lx, ly, half = label
        if lx == S:
            back = rows_at((y_a, y_b, own)[ly], extent_x + (S * 2 + half) * planes, planes)
        else:
            back = rows_at((x_a, x_b)[lx], size + ((1, 2, 0)[ly] * 2 + half) * planes, planes)
        back = alive_lanes(back, order, number, count[0, 0])
        backs.append(back)
        pulled = TIME_STEP * pair_dot(back, pairs[number], 0)
        add_tile_pair(total, order[1, 2 * number], order[1, 2 * number + 1], pulled, planes, extent_x)
    copies = [pltpu.make_async_copy(total, out, sems.at[0]), pltpu.make_async_copy(blocks, out_blocks, sems.at[1])]
    copies[0].start()
    half_lane = lanes((TILE // 2, 128)) < TILE
    for number, back in enumerate(backs):
        work[number] = first_outer[number] + outer(TIME_STEP * back, picked[number])
        for which in range(2):
            slot = order[0, 2 * number + which]
            even_rows = work[number, pl.ds(which * TILE, TILE // 2, 2), :]
            odd_rows = work[number, pl.ds(which * TILE + 1, TILE // 2, 2), :]
            if which == 0:
                merged = jnp.where(half_lane, even_rows, roll(odd_rows, TILE))
            else:
                merged = jnp.where(half_lane, roll(even_rows, TILE), odd_rows)
            blocks[pl.ds(pl.multiple_of(slot * (TILE // 2), 8), TILE // 2), :] = merged
    copies[1].start()
    for copy in copies:
        copy.wait()


SPACE = {"v": pltpu.VMEM, "s": pltpu.SMEM, "h": pltpu.HBM}


def call(body, ins, outs, scratch=(), alias=None, **sizes):
    values, specs, shapes, out_specs = [], [], [], []
    for kind, group in ins:
        for value in group:
            values.append(value if kind == "r" else pltpu.with_memory_space_constraint(value, SPACE[kind]))
            specs.append(pl.BlockSpec(memory_space=SPACE["s" if kind == "r" else kind]))
    for shape, dtype, kind in outs:
        shapes.append(SPACE[kind](shape, dtype))
        out_specs.append(pl.BlockSpec(memory_space=SPACE[kind]))
    return pl.pallas_call(
        functools.partial(body, **sizes),
        out_shape=tuple(shapes),
        in_specs=specs,
        out_specs=tuple(out_specs),
        scratch_shapes=list(scratch),
        input_output_aliases=alias or {},
        compiler_params=pltpu.CompilerParams(vmem_limit_bytes=VMEM_LIMIT),
        name=body.__name__,
    )(*values)


def shards(
    level_set, speed_x, speed_y, cotangent, blocks, tile_count, source_tile, dest_offset, dest_tile
):
    planes, extent_x, extent_y = level_set.shape
    slots = source_tile.shape[2]
    cells = planes * extent_x
    f32, i32 = jnp.float32, jnp.int32
    field, rate_x, rate_y, cotan = (v.reshape(cells, extent_y) for v in (level_set, speed_x, speed_y, cotangent))
    sizes = dict(planes=planes, extent_x=extent_x)
    size = 3 * planes
    pair_total = slots // 2
    box = ((2 * size, 128), f32, "v")
    padded = ((planes * PAD + 8, extent_y), f32)
    pad_scratch = pltpu.VMEM(*padded)
    whole = ((cells, 128), f32, "v")

    cotan_b = exchange(cotan, "gy", B)
    cotan_a = exchange(cotan, "gy", A)
    order, send_a, send_b, field, cotan, rate_x, rate_y = call(
        begin_body,
        [("h", [v.reshape(slots) for v in (dest_offset, dest_tile, source_tile)] + [field, cotan, rate_x, rate_y])],
        [((2, slots), i32, "s")] + [((8 + 3 * size, 128), f32, "v")] * 2 + [whole] * 4,
        scratch=[pltpu.SMEM((slots,), i32)] * 3 + [pltpu.SMEM((9,), i32), pltpu.SemaphoreType.DMA((7,))],
        **sizes,
    )
    request = send_a
    rows_a = exchange(send_a, "gx", A)
    rows_b = exchange(send_b, "gx", B)
    pairs, picked, packs, value_a, value_b, value_s = call(
        extend_body, [("s", [order]), ("r", [tile_count]), ("v", [field, cotan, rate_y, blocks.reshape(slots, TILE, TILE)])],
        [((pair_total, 128, 128), jnp.bfloat16, "v"), ((pair_total, planes, 128), f32, "v"), ((3 * extent_x, 128), f32, "v")]
        + [box] * 3, **sizes,
    )
    tiles_a, tiles_b, tiles_s = call(
        serve_body, [("v", [request, rows_a, rows_b, cotan_a, cotan_b, cotan])], [box, box, box],
        scratch=(pltpu.VMEM((8, 128), i32), pltpu.SMEM((8, 128), i32), pltpu.SemaphoreType.DMA(())), **sizes,
    )
    wide = jnp.concatenate([request[:8], rows_a[:8], rows_b[:8], packs[: 2 * extent_x]], axis=0)
    wide, tiles_a, tiles_b = lax.optimization_barrier((wide, tiles_a, tiles_b))
    x_b = exchange(jnp.concatenate([tiles_b, value_b], axis=0), "gx", B)
    x_a = exchange(jnp.concatenate([tiles_a, value_a], axis=0), "gx", A)
    packs_b = exchange(wide, "gy", B)
    packs_a = exchange(wide, "gy", A)
    early, edge_rate, asked = call(
        pull_y_body, [("v", [cotan, cotan_a, cotan_b, rate_y, packs, request, rows_a, rows_b, packs_a, packs_b])],
        [whole, ((extent_x, 128), f32, "v"), ((8, 128), i32, "s")],
        scratch=(pltpu.VMEM((8, 128), i32), pltpu.VMEM((cells, 128), f32), pltpu.SemaphoreType.DMA(())), **sizes,
    )
    early, pad_rate = call(
        pull_x_body, [("v", [early, cotan, rate_x, rows_a, rows_b])], [whole, padded + ("v",)],
        scratch=(pad_scratch,) * 3, alias={0: 0}, **sizes,
    )
    grad, returned, send_a, send_b, send_s, edge_a, edge_b = call(
        middle_body, [("s", [order, asked]), ("r", [tile_count]), ("v", [early, pairs, x_a, x_b, tiles_s])],
        [whole, ((pair_total, planes, 128), f32, "v")] + [((extent_x + 2 * size, 128), f32, "v")] * 3 + [((size, 128), f32, "v")] * 2,
        alias={3: 0}, **sizes,
    )

    def onward(own, a, b, own_first, first, m):
        cut = lambda v, start: v[start + m * 2 * planes : start + (m + 1) * 2 * planes]
        return [cut(own, own_first), cut(a, first), cut(b, first)]

    ext_a = jnp.concatenate(onward(value_s, x_a, x_b, 0, 2 * size, A), axis=0)
    ext_b = jnp.concatenate(onward(value_s, x_a, x_b, 0, 2 * size, B), axis=0)
    send_a, send_b, field, ext_a, ext_b = lax.optimization_barrier((send_a, send_b, field, ext_a, ext_b))
    last_y_b = exchange(send_b, "gy", B)
    last_y_a = exchange(send_a, "gy", A)
    ext_b = exchange(ext_b, "gy", B)
    ext_a = exchange(ext_a, "gy", A)
    (pushed,) = call(
        push_body, [("v", [field, pad_rate, rate_y, edge_rate, rows_a, rows_b, packs, packs_a, packs_b])],
        [whole], scratch=(pad_scratch,) * 2, **sizes,
    )
    last_y_a, last_y_b, pushed = lax.optimization_barrier((last_y_a, last_y_b, pushed))
    last_x_b = exchange(jnp.concatenate([edge_b] + onward(send_s, last_y_a, last_y_b, extent_x, extent_x, B), axis=0), "gx", B)
    last_x_a = exchange(jnp.concatenate([edge_a] + onward(send_s, last_y_a, last_y_b, extent_x, extent_x, A), axis=0), "gx", A)
    (inner,) = call(
        inner_body, [("v", [cotan, grad, pad_rate, rate_y])], [whole], scratch=(pad_scratch,) * 3, **sizes,
    )
    section, first_outer = call(
        section_body, [("s", [order, asked]), ("v", [pushed, returned, x_a, x_b, ext_a, ext_b, value_s])],
        [whole, ((pair_total, 128, 128), f32, "v")], alias={2: 0}, **sizes,
    )
    grad_level_set, grad_blocks = call(
        last_body,
        [("s", [order]), ("r", [tile_count]), ("v", [inner, grad, pad_rate, edge_rate, packs, send_s, last_y_a, last_y_b, last_x_a, last_x_b, pairs, first_outer, picked])],
        [((cells, 128), f32, "h"), ((slots * TILE // 2, 128), f32, "h")],
        scratch=(pltpu.VMEM((pair_total, 128, 128), f32), pltpu.VMEM((cells, 128), f32),
                 pltpu.VMEM((slots * TILE // 2, 128), f32), pltpu.SemaphoreType.DMA((2,))), **sizes,
    )
    return (grad_level_set.reshape(planes, extent_x, extent_y), grad_blocks.reshape(1, 1, slots, TILE * TILE))


def solution(mesh):
    return jax.shard_map(
        shards,
        mesh=mesh,
        in_specs=(
            P(None, "gx", "gy"),
            P(None, "gx", "gy"),
            P(None, "gx", "gy"),
            P(None, "gx", "gy"),
            P("gx", "gy", None, None),
            P("gx", "gy"),
            P("gx", "gy", None),
            P("gx", "gy", None),
            P("gx", "gy", None),
        ),
        out_specs=(P(None, "gx", "gy"), P("gx", "gy", None, None)),
        check_vma=False,
    )
```

```python
import functools

import jax
import jax.numpy as jnp
from jax import lax
from jax.experimental import pallas as pl
from jax.experimental.pallas import tpu as pltpu
from jax.sharding import PartitionSpec as P

TILE = 64
ROUTE_MOST = 4
TIME_STEP = 0.3
WEIGHTS = (2.0 / 60.0, -13.0 / 60.0, 47.0 / 60.0, 27.0 / 60.0, -3.0 / 60.0)
PAD = 80
VMEM_LIMIT = 16 << 20

A, B, S = 0, 1, 2


def matching(count, which):
    return [(i, (i + (1 if (i % 2 == 0) == (which == B) else -1)) % count) for i in range(count)]


def exchange(block, axis, which):
    return lax.ppermute(block, axis, matching(lax.axis_size(axis), which))


def lanes(shape):
    return lax.broadcasted_iota(jnp.int32, shape, len(shape) - 1)


def roll(value, shift):
    return pltpu.roll(value, shift % 128 if isinstance(shift, int) else shift, axis=value.ndim - 1)


def split(value):
    high = value.astype(jnp.bfloat16)
    return high, (value - high.astype(jnp.float32)).astype(jnp.bfloat16)


def pair_dot(value, matrix, over):
    high, low = split(value)
    both = lax.dot_general(
        jnp.concatenate([high, low], axis=0),
        matrix,
        (((1,), (over,)), ((), ())),
        preferred_element_type=jnp.float32,
    )
    rows = value.shape[0]
    return both[:rows] + both[rows:]


def row_of(ref, x, planes, stride):
    return ref[pl.ds(x, planes, stride), :]


def tile_pair(ref, first, second, planes, extent_x):
    one = row_of(ref, first // 2, planes, extent_x)
    two = row_of(ref, second // 2, planes, extent_x)
    lane = lanes(one.shape)
    one = jnp.where(first % 2 == 0, one, roll(one, TILE))
    two = jnp.where(second % 2 == 1, two, roll(two, TILE))
    return jnp.where(lane < TILE, one, two)


def add_tile_pair(ref, first, second, value, planes, extent_x):
    lane = lanes(value.shape)
    turned = roll(value, TILE)
    for tile, half in ((first, 0), (second, 1)):
        spot = pl.ds(tile // 2, planes, extent_x)
        placed = jnp.where(tile % 2 == half, value, turned)
        keep = (lane // TILE) == tile % 2
        ref[spot, :] = ref[spot, :] + jnp.where(keep, placed, 0.0)


def edge_pack(ref, planes, extent_x):
    lane = lanes((extent_x, 128))
    packed = jnp.zeros((extent_x, 128), jnp.float32)
    for z in range(planes):
        plane = ref[z * extent_x : (z + 1) * extent_x, :]
        packed = jnp.where(lane // 8 == z, roll(plane, 8 * z + 3), packed)
    return packed


def edge_rows(ref, start, planes, extent_x):
    return jnp.concatenate([row_of(ref, start + j, planes, extent_x) for j in range(3)], axis=0)


def upwind(face_rate):
    return jnp.maximum(face_rate, 0.0), jnp.minimum(face_rate, 0.0)


UP = {2: WEIGHTS[0], 1: WEIGHTS[1], 0: WEIGHTS[2], -1: WEIGHTS[3], -2: WEIGHTS[4]}
DOWN = {1: WEIGHTS[4], 0: WEIGHTS[3], -1: WEIGHTS[2], -2: WEIGHTS[1], -3: WEIGHTS[0]}


def combine(up_part, down_part, k):
    total = 0.0
    if k in UP:
        total = total + UP[k] * up_part
    if k in DOWN:
        total = total + DOWN[k] * down_part
    return total


def fill_padded(pad_ref, field_ref, rows_a, rows_b, even, planes, extent_x):
    high = 8 + extent_x
    at_a = jnp.where(even, 5, high)
    at_b = jnp.where(even, high, 5)
    for z in range(planes):
        pad_ref[z * PAD + 8 : z * PAD + high, :] = field_ref[z * extent_x : (z + 1) * extent_x, :]
    for j in range(3):
        part = slice(j * planes, (j + 1) * planes)
        pad_ref[pl.ds(at_a + j, planes, PAD), :] = rows_a[part]
        pad_ref[pl.ds(at_b + j, planes, PAD), :] = rows_b[part]


def edge_join(from_a, from_b, even):
    low = jnp.where(even, from_a, from_b)
    high = jnp.where(even, from_b, from_a)
    return jnp.where(lanes(low.shape) % 8 < 3, low, high)


def adjoint_edges(own, halo, own_rate, halo_rate):
    lane = lanes(own.shape) % 8
    after = roll(jnp.where(lane == 3, own, halo), -1)
    before = roll(jnp.where(lane == 2, own, halo), 1)
    jump = jnp.where(lane < 3, after - halo, halo - before)
    rate = jnp.where(lane < 3, halo_rate, roll(jnp.where(lane == 2, own_rate, halo_rate), 1))
    rate_up, rate_down = upwind(rate)
    up_part, down_part = rate_up * jump, rate_down * jump
    low_side = 0.0
    high_side = 0.0
    for k in (-1, -2, -3):
        part = jnp.where(lane < 3, combine(up_part, down_part, k), 0.0)
        low_side = low_side + roll(part, -k)
    for k in (0, 1, 2):
        part = jnp.where((lane >= 3) & (lane < 6), combine(up_part, down_part, k), 0.0)
        high_side = high_side + roll(part, -(k + 1))
    return jnp.where(lane < 3, high_side, jnp.where(lane < 6, low_side, 0.0))


def adjoint_x(z, pad_ref, pad_rate_ref, up_ref, down_ref, extent_x):
    base = z * PAD
    here = pad_ref[pl.ds(base, PAD), :]
    jump = pad_ref[pl.ds(base + 1, PAD), :] - here
    rate_up, rate_down = upwind(pad_rate_ref[pl.ds(base, PAD), :])
    up_ref[pl.ds(base, PAD), :] = rate_up * jump
    down_ref[pl.ds(base, PAD), :] = rate_down * jump
    total = 0.0
    for k in range(-3, 3):
        if k in UP:
            total = total + UP[k] * up_ref[pl.ds(base + 8 + k, extent_x), :]
        if k in DOWN:
            total = total + DOWN[k] * down_ref[pl.ds(base + 8 + k, extent_x), :]
    return total


def band(weights, first_lost):
    row = lax.broadcasted_iota(jnp.int32, (128, 128), 0)
    gap = row - lax.broadcasted_iota(jnp.int32, (128, 128), 1)
    matrix = jnp.zeros((128, 128), jnp.float32)
    for k, weight in weights.items():
        matrix = jnp.where(gap == k, float(round(60.0 * weight)), matrix)
    return jnp.where(row >= first_lost, 0.0, matrix).astype(jnp.bfloat16)


def mix(left, matrix):
    return lax.dot_general(left, matrix, (((1,), (0,)), ((), ())), preferred_element_type=jnp.float32)


def adjoint_y(field_ref, rate_y_ref, planes, extent_x):
    up_matrix, down_matrix = band(UP, 127), band(DOWN, 127)
    matrix = jnp.concatenate([up_matrix, up_matrix, down_matrix, down_matrix], axis=0)
    rows = 4 * extent_x
    results = []
    for chunk in range(planes // 4):
        field = field_ref[chunk * rows : (chunk + 1) * rows, :]
        jump = roll(field, -1) - field
        rate_up, rate_down = upwind(rate_y_ref[chunk * rows : (chunk + 1) * rows, :])
        left = jnp.concatenate(split(rate_up * jump) + split(rate_down * jump), axis=1)
        results.append(mix(left, matrix))
    return results


LABELS = [(lx, ly, half) for ly in range(3) for lx in range(3) for half in range(2)]


def parities():
    return lax.rem(lax.axis_index("gx"), 2), lax.rem(lax.axis_index("gy"), 2)


def alive_lanes(value, order, number, total):
    lane = lanes(value.shape)
    return jnp.where(jnp.where(lane < TILE, order[0, 2 * number], order[0, 2 * number + 1]) < total, value, 0.0)


def part(ref, number, extent_x):
    return ref[number * extent_x : (number + 1) * extent_x]


def begin_body(
    heading, target, source, field, cotan, rate_x, rate_y, blocks, count,
    order, send_a, send_b, value_s, late_a, late_b, pairs, picked, field_out, cotan_out, rate_y_out,
    rate_x_out, blocks_in, flat, square, heading_in, target_in, source_in, used, sems, *, planes, extent_x,
):
    moves = (
        (heading, heading_in), (target, target_in), (source, source_in),
        (blocks, blocks_in), (field, field_out), (cotan, cotan_out), (rate_x, rate_x_out), (rate_y, rate_y_out),
    )
    copies = [pltpu.make_async_copy(a, b, sems.at[number]) for number, (a, b) in enumerate(moves)]
    for copy in copies:
        copy.start()
    parity_x, parity_y = parities()
    for label in range(9):
        used[label] = 0
    lane = lanes((8, 128))
    for copy in copies[:3]:
        copy.wait()
    asked = jnp.zeros((8, 128), jnp.int32)
    slots = heading.shape[0]
    for slot in range(slots):
        toward = heading_in[slot]
        across = (toward >= 3).astype(jnp.int32) + (toward >= 6).astype(jnp.int32)
        ex = (across - 1) * (1 - 2 * parity_x)
        ey = (toward - 3 * across - 1) * (1 - 2 * parity_y)
        lx = jnp.where(ex == 0, 2, (ex + 1) // 2)
        ly = jnp.where(ey == 0, 2, (ey + 1) // 2)
        label = ly * 3 + lx
        spot = label * ROUTE_MOST + used[label]
        used[label] = used[label] + 1
        order[0, spot] = slot
        order[1, spot] = source_in[slot]
        asked = jnp.where(lane == spot, target_in[slot], asked)
    for out in (send_a, send_b):
        out[0:8, :] = asked.astype(jnp.float32)
    copies[3].wait()
    half = TILE // 2
    for row in range(half):
        flat[pl.ds(row, slots, half), :] = blocks_in[:, row * 128 : (row + 1) * 128].astype(jnp.float32)
    copies[4].wait()
    total = count[0, 0]
    size = 3 * planes
    first_half = lanes((half, 128)) < TILE
    for number, (lx, ly, side) in enumerate(LABELS):
        one = flat[pl.ds(pl.multiple_of(order[0, 2 * number] * half, 8), half), :]
        two = flat[pl.ds(pl.multiple_of(order[0, 2 * number + 1] * half, 8), half), :]
        square[number, pl.ds(0, half, 2), :] = jnp.where(first_half, one, 0.0)
        square[number, pl.ds(1, half, 2), :] = jnp.where(first_half, roll(one, TILE), 0.0)
        square[number, pl.ds(TILE, half, 2), :] = jnp.where(first_half, 0.0, roll(two, TILE))
        square[number, pl.ds(TILE + 1, half, 2), :] = jnp.where(first_half, 0.0, two)
        joined = square[number].astype(jnp.bfloat16)
        pairs[number] = joined
        tiles = tile_pair(field_out, order[1, 2 * number], order[1, 2 * number + 1], planes, extent_x)
        picked[number] = tiles
        value = pair_dot(alive_lanes(tiles, order, number, total), joined, 1)
        first = (0 if lx == S else 8 + 2 * size) + (ly * 2 + side) * planes
        (send_a, send_b, value_s)[lx][first : first + planes, :] = value
    even = parity_x == 0
    high = extent_x - 3
    for number, ref in enumerate((cotan_out, rate_x_out, field_out)):
        if number < 2:
            copies[5 + number].wait()
        to_a = edge_rows(ref, jnp.where(even, 0, high), planes, extent_x)
        to_b = edge_rows(ref, jnp.where(even, high, 0), planes, extent_x)
        if number < 2:
            spot = slice(8 + number * size, 8 + (number + 1) * size)
            send_a[spot, :], send_b[spot, :] = to_a, to_b
        else:
            late_a[...], late_b[...] = to_a, to_b
    copies[7].wait()


def edges_body(field, cotan, rate_y, packs, *, planes, extent_x):
    for number, ref in enumerate((rate_y, field, cotan)):
        packs[number * extent_x : (number + 1) * extent_x, :] = edge_pack(ref, planes, extent_x)


def merge_lists(a, b, s):
    group = lax.rem(lanes((8, 128)), 12) // ROUTE_MOST
    return jnp.where(group == 0, a, jnp.where(group == 1, b, s)).astype(jnp.int32)


def to_scalars(value, list_ref, asked, sem):
    list_ref[...] = value
    copy = pltpu.make_async_copy(list_ref, asked, sem)
    copy.start()
    copy.wait()


def serve_body(request, got_b, got_a, cotan_a, cotan_b, cotan, out_a, out_b, out_s, list_ref, asked, sem, *, planes, extent_x):
    to_scalars(merge_lists(got_a[0:8], got_b[0:8], request[0:8]), list_ref, asked, sem)
    for lx, ly, half in LABELS:
        at = ly * 12 + lx * ROUTE_MOST + 2 * half
        tiles = tile_pair((cotan_a, cotan_b, cotan)[ly], asked[0, at], asked[0, at + 1], planes, extent_x)
        first = (ly * 2 + half) * planes
        (out_a, out_b, out_s)[lx][first : first + planes, :] = tiles


def gather_tiles(asked, field, outs, first, planes, extent_x):
    for ly in range(3):
        for inner in range(6):
            at = ly * 12 + 2 * inner
            tiles = tile_pair(field, asked[ly, at], asked[ly, at + 1], planes, extent_x)
            outs[ly][first + inner * planes : first + (inner + 1) * planes, :] = tiles


def rows_at(ref, first, planes):
    return ref[first : first + planes, :]


def pull_y_body(
    cotan, cotan_a, cotan_b, rate_y, packs, request, got_a, got_b, from_a, from_b, grad, edge_rate, asked, list_ref, joined, sem,
    *, planes, extent_x,
):
    row = lax.broadcasted_iota(jnp.int32, (8, 128), 0)
    spread = [
        jnp.broadcast_to(merge_lists(a, b, c)[0:1], (8, 128))
        for a, b, c in (
            (from_a[8:16], from_a[16:24], from_a[0:8]),
            (from_b[8:16], from_b[16:24], from_b[0:8]),
            (got_a[0:8], got_b[0:8], request[0:8]),
        )
    ]
    list_ref[...] = jnp.where(row == 0, spread[0], jnp.where(row == 1, spread[1], spread[2]))
    copy = pltpu.make_async_copy(list_ref, asked, sem)
    copy.start()
    even_y = parities()[1] == 0
    lane = lanes((extent_x, 128))
    upper = jnp.where(even_y, lane, 127 - lane) >= TILE
    for z in range(planes):
        plane = slice(z * extent_x, (z + 1) * extent_x)
        joined[plane, :] = jnp.where(upper, cotan_a[plane, :], cotan_b[plane, :])
    halo = edge_pack(joined, planes, extent_x)
    halo_rate = edge_join(from_a[24 : 24 + extent_x], from_b[24 : 24 + extent_x], even_y)
    edge_rate[...] = halo_rate
    edges = adjoint_edges(part(packs, 2, extent_x), halo, part(packs, 0, extent_x), halo_rate)
    pulled = adjoint_y(cotan, rate_y, planes, extent_x)
    for z in range(planes):
        spot = pl.ds(z * extent_x, extent_x)
        rim = roll(edges, 125 - 8 * z)
        rim = jnp.where((lane < 3) | (lane >= 125), rim, 0.0)
        main = pulled[z // 4][z % 4 * extent_x : (z % 4 + 1) * extent_x]
        grad[spot, :] = 0.5 * cotan[spot, :] + (0.5 * TIME_STEP) * (main * (1.0 / 60.0) + rim)
    copy.wait()


def pull_x_body(early, cotan, rate_x, rows_a, rows_b, grad, pad_rate, pad, up_ref, down_ref, *, planes, extent_x):
    even_x = parities()[0] == 0
    size = 3 * planes
    fill_padded(pad, cotan, rows_a[8 : 8 + size], rows_b[8 : 8 + size], even_x, planes, extent_x)
    fill_padded(pad_rate, rate_x, rows_a[8 + size : 8 + 2 * size], rows_b[8 + size : 8 + 2 * size], even_x, planes, extent_x)
    for z in range(planes):
        spot = pl.ds(z * extent_x, extent_x)
        grad[spot, :] = early[spot, :] + (0.5 * TIME_STEP) * adjoint_x(z, pad, pad_rate, up_ref, down_ref, extent_x)


def push_body(field, pad_rate, rate_y, edge_rate, rows_a, rows_b, packs, packs_a, packs_b, section, pad, flux_ref, *, planes, extent_x):
    parity_x, parity_y = parities()
    even_x, even_y = parity_x == 0, parity_y == 0
    first = 6 * planes
    fill_padded(pad, field, rows_a[first : first + 3 * planes], rows_b[first : first + 3 * planes], even_x, planes, extent_x)
    second = slice(24 + extent_x, 24 + 2 * extent_x)
    halo = edge_join(packs_a[second], packs_b[second], even_y)
    own_rate = part(packs, 0, extent_x)
    lane8 = lanes(halo.shape) % 8

    def shifted_by(value, k):
        return roll(value, -k) if k else value

    def stencils(value):
        up_part = sum(WEIGHTS[j] * shifted_by(value, j - 2) for j in range(5))
        down_part = sum(WEIGHTS[j] * shifted_by(value, 3 - j) for j in range(5))
        return up_part, down_part

    up_part, down_part = stencils(jnp.where(lane8 < 3, halo, jnp.where(lane8 < 6, part(packs, 1, extent_x), 0.0)))
    rate_up, rate_down = upwind(edge_rate[...])
    flux_low = roll(rate_up * up_part + rate_down * down_part, 1)
    rate_up, rate_down = upwind(own_rate)
    up_part, down_part = stencils(jnp.where((lane8 >= 3) & (lane8 < 6), halo, 0.0))
    flux_high = jnp.where(lane8 < 3, rate_up * up_part + rate_down * down_part, 0.0)
    up_part, down_part = stencils(jnp.where(lane8 < 3, halo, 0.0))
    flux_first = jnp.where((lane8 >= 3) & (lane8 < 5), rate_up * up_part + rate_down * down_part, 0.0)
    change_edge = roll(flux_high, 1) - flux_high
    before = jnp.where(lane8 == 3, flux_low, roll(flux_first, 1))
    change_edge = jnp.where(lane8 < 3, change_edge, jnp.where(lane8 < 6, before - flux_first, 0.0))
    both = jnp.concatenate([band({k: WEIGHTS[k + 2] for k in range(-2, 3)}, 128), band({k: WEIGHTS[3 - k] for k in range(-1, 4)}, 128)], axis=1)
    both = jnp.concatenate([both, both], axis=0)
    chunk_rows = 4 * extent_x
    fluxes = []
    for chunk in range(planes // 4):
        rows = slice(chunk * chunk_rows, (chunk + 1) * chunk_rows)
        parts = mix(jnp.concatenate(split(field[rows, :]), axis=1), both) * (1.0 / 60.0)
        rate_up, rate_down = upwind(rate_y[rows, :])
        fluxes.append(rate_up * parts[:, :128] + rate_down * parts[:, 128:])
    for z in range(planes):
        base = z * PAD
        spot = pl.ds(z * extent_x, extent_x)
        window = extent_x + 8
        near = {k: pad[pl.ds(base + 7 + k, window), :] for k in range(-2, 4)}
        rate_up, rate_down = upwind(pad_rate[pl.ds(base + 7, window), :])
        flux_ref[pl.ds(base, window), :] = rate_up * sum(WEIGHTS[j] * near[j - 2] for j in range(5)) + rate_down * sum(
            WEIGHTS[j] * near[3 - j] for j in range(5)
        )
        change = flux_ref[pl.ds(base, extent_x), :] - flux_ref[pl.ds(base + 1, extent_x), :]
        flux = fluxes[z // 4][z % 4 * extent_x : (z % 4 + 1) * extent_x]
        lane = lanes(flux.shape)
        rim = roll(change_edge, 125 - 8 * z)
        rim = jnp.where((lane < 3) | (lane >= 125), rim, 0.0)
        change = change + jnp.where(lane == 0, 0.0, roll(flux, 1)) - flux + rim
        section[spot, :] = field[spot, :] + TIME_STEP * change


def middle_body(order, asked, count, early, pairs, x_a, x_b, own, grad, returned, send_a, send_b, send_s, rows_a, rows_b, *, planes, extent_x):
    even_x = parities()[0] == 0
    alive = count[0, 0]
    for number, (lx, ly, half) in enumerate(LABELS):
        back = rows_at((x_a, x_b, own)[lx], (ly * 2 + half) * planes, planes)
        back = alive_lanes(back, order, number, alive)
        returned[number] = back
        pulled = (0.5 * TIME_STEP) * pair_dot(back, pairs[number], 0)
        add_tile_pair(grad, order[1, 2 * number], order[1, 2 * number + 1], pulled, planes, extent_x)
    packed = edge_pack(grad, planes, extent_x)
    for out in (send_a, send_b, send_s):
        out[0:extent_x, :] = packed
    gather_tiles(asked, grad, (send_a, send_b, send_s), extent_x, planes, extent_x)
    high = extent_x - 3
    rows_a[...] = edge_rows(grad, jnp.where(even_x, 0, high), planes, extent_x)
    rows_b[...] = edge_rows(grad, jnp.where(even_x, high, 0), planes, extent_x)


def inner_body(cotan, grad, pad_rate, rate_y, out, pad, up_ref, down_ref, *, planes, extent_x):
    high = 8 + extent_x
    for z in range(planes):
        pad[z * PAD + 8 : z * PAD + high, :] = grad[z * extent_x : (z + 1) * extent_x, :]
    for j in range(3):
        pad[pl.ds(5 + j, planes, PAD), :] = row_of(grad, 0, planes, extent_x)
        pad[pl.ds(high + j, planes, PAD), :] = row_of(grad, extent_x - 1, planes, extent_x)

    along_y = adjoint_y(grad, rate_y, planes, extent_x)
    for z in range(planes):
        spot = pl.ds(z * extent_x, extent_x)
        pulled = along_y[z // 4][z % 4 * extent_x : (z % 4 + 1) * extent_x] * (1.0 / 60.0)
        pulled = pulled + adjoint_x(z, pad, pad_rate, up_ref, down_ref, extent_x)
        out[spot, :] = 0.5 * cotan[spot, :] + grad[spot, :] + TIME_STEP * pulled


def outer(left, right):
    left_high, left_low = split(left)
    right_high, right_low = split(right)
    return lax.dot_general(
        jnp.concatenate([left_high, left_high, left_low], axis=0),
        jnp.concatenate([right_high, right_low, right_high], axis=0),
        (((0,), (0,)), ((), ())),
        preferred_element_type=jnp.float32,
    )


def section_body(order, asked, early, returned, x_a, x_b, y_a, y_b, own, section, first_outer, *, planes, extent_x):
    for number, (lx, ly, half) in enumerate(LABELS):
        if ly == S:
            came = rows_at((x_a, x_b, own)[lx], (0 if lx == S else 8 + 6 * planes) + (S * 2 + half) * planes, planes)
        else:
            came = rows_at((y_a, y_b)[ly], 24 + 2 * extent_x + ((1, 2, 0)[lx] * 2 + half) * planes, planes)
        came = TIME_STEP * came
        at = ly * 12 + lx * ROUTE_MOST + 2 * half
        add_tile_pair(section, asked[ly, at], asked[ly, at + 1], came, planes, extent_x)

    for number in range(first_outer.shape[0]):
        picked = tile_pair(section, order[1, 2 * number], order[1, 2 * number + 1], planes, extent_x)
        first_outer[number] = outer((0.5 * TIME_STEP) * returned[number], picked)


def finish(number, back, order, pairs, first_outer, picked, total, work, blocks, planes, extent_x):
    pulled = TIME_STEP * pair_dot(back, pairs[number], 0)
    add_tile_pair(total, order[1, 2 * number], order[1, 2 * number + 1], pulled, planes, extent_x)
    work[number] = first_outer[number] + outer(TIME_STEP * back, picked[number])
    half_lane = lanes((TILE // 2, 128)) < TILE
    for which in range(2):
        slot = order[0, 2 * number + which]
        even_rows = work[number, pl.ds(which * TILE, TILE // 2, 2), :]
        odd_rows = work[number, pl.ds(which * TILE + 1, TILE // 2, 2), :]
        if which == 0:
            merged = jnp.where(half_lane, even_rows, roll(odd_rows, TILE))
        else:
            merged = jnp.where(half_lane, roll(even_rows, TILE), odd_rows)
        blocks[pl.ds(pl.multiple_of(slot * (TILE // 2), 8), TILE // 2), :] = merged


def rest_body(
    order, count, early, rate_edge, packs, own, y_a, y_b, pairs, first_outer, picked, total, blocks, work, *, planes, extent_x,
):
    even_y = parities()[1] == 0
    halo = edge_join(y_a[0:extent_x], y_b[0:extent_x], even_y)
    edges = adjoint_edges(own[0:extent_x], halo, part(packs, 0, extent_x), rate_edge[...])
    lane = lanes((extent_x, 128))
    for z in range(planes):
        spot = pl.ds(z * extent_x, extent_x)
        rim = roll(edges, 125 - 8 * z)
        total[spot, :] = total[spot, :] + TIME_STEP * jnp.where((lane < 3) | (lane >= 125), rim, 0.0)
    for number, (lx, ly, half) in enumerate(LABELS):
        if lx == S:
            back = rows_at((y_a, y_b, own)[ly], extent_x + (S * 2 + half) * planes, planes)
            back = alive_lanes(back, order, number, count[0, 0])
            finish(number, back, order, pairs, first_outer, picked, total, work, blocks, planes, extent_x)


def last_body(
    order, count, early, blocks_early, grad, pad_rate, x_b, x_a, pairs, first_outer, picked, out, out_blocks, total, blocks, work, sems,
    *, planes, extent_x,
):
    even_x = parities()[0] == 0
    size = 3 * planes
    low_rows = [jnp.where(even_x, x_a[j * planes : (j + 1) * planes], x_b[j * planes : (j + 1) * planes]) for j in range(3)]
    high_rows = [jnp.where(even_x, x_b[j * planes : (j + 1) * planes], x_a[j * planes : (j + 1) * planes]) for j in range(3)]
    first_cell = row_of(grad, 0, planes, extent_x)
    last_cell = row_of(grad, extent_x - 1, planes, extent_x)
    for line, low_face in ((low_rows + [first_cell], -3), ([last_cell] + high_rows, extent_x - 1)):
        faces = []
        for j in range(3):
            rate_up, rate_down = upwind(row_of(pad_rate, 8 + low_face + j, planes, PAD))
            jump = line[j + 1] - line[j]
            faces.append((rate_up * jump, rate_down * jump))
        cells = range(0, 3) if low_face < 0 else range(extent_x - 3, extent_x)
        for cell in cells:
            added = 0.0
            for j in range(3):
                k = low_face + j - cell
                if -3 <= k <= 2:
                    added = added + combine(*faces[j], k)
            spot = pl.ds(cell, planes, extent_x)
            total[spot, :] = total[spot, :] + TIME_STEP * added
    for number, (lx, ly, half) in enumerate(LABELS):
        if lx != S:
            back = rows_at((x_a, x_b)[lx], size + ((1, 2, 0)[ly] * 2 + half) * planes, planes)
            back = alive_lanes(back, order, number, count[0, 0])
            finish(number, back, order, pairs, first_outer, picked, total, work, blocks, planes, extent_x)
    copies = [pltpu.make_async_copy(total, out, sems.at[0]), pltpu.make_async_copy(blocks, out_blocks, sems.at[1])]
    for copy in copies:
        copy.start()
    for copy in copies:
        copy.wait()


SPACE = {"v": pltpu.VMEM, "s": pltpu.SMEM, "h": pltpu.HBM}


def call(body, ins, outs, scratch=(), alias=None, **sizes):
    values, specs, shapes, out_specs = [], [], [], []
    for kind, group in ins:
        for value in group:
            values.append(value if kind == "r" else pltpu.with_memory_space_constraint(value, SPACE[kind]))
            specs.append(pl.BlockSpec(memory_space=SPACE["s" if kind == "r" else kind]))
    for shape, dtype, kind in outs:
        shapes.append(SPACE[kind](shape, dtype))
        out_specs.append(pl.BlockSpec(memory_space=SPACE[kind]))
    return pl.pallas_call(
        functools.partial(body, **sizes),
        out_shape=tuple(shapes),
        in_specs=specs,
        out_specs=tuple(out_specs),
        scratch_shapes=list(scratch),
        input_output_aliases=alias or {},
        compiler_params=pltpu.CompilerParams(vmem_limit_bytes=VMEM_LIMIT),
        name=body.__name__,
    )(*values)


def shards(
    level_set, speed_x, speed_y, cotangent, blocks, tile_count, source_tile, dest_offset, dest_tile
):
    planes, extent_x, extent_y = level_set.shape
    slots = source_tile.shape[2]
    cells = planes * extent_x
    f32, i32 = jnp.float32, jnp.int32
    field, rate_x, rate_y, cotan = (v.reshape(cells, extent_y) for v in (level_set, speed_x, speed_y, cotangent))
    sizes = dict(planes=planes, extent_x=extent_x)
    size = 3 * planes
    pair_total = slots // 2
    box = ((2 * size, 128), f32, "v")
    padded = ((planes * PAD + 8, extent_y), f32)
    pad_scratch = pltpu.VMEM(*padded)
    whole = ((cells, 128), f32, "v")

    cotan_a = exchange(cotan, "gy", A)
    cotan_b = exchange(cotan, "gy", B)
    head = 8 + 2 * size
    head = 8 + 2 * size
    sent = ((head + 2 * size, 128), f32, "v")
    tall = ((slots * TILE // 2, 128), f32)
    order, send_a, send_b, value_s, late_a, late_b, pairs, picked, field, cotan, rate_y = call(
        begin_body,
        [("h", [v.reshape(slots) for v in (dest_offset, dest_tile, source_tile)] + [field, cotan, rate_x, rate_y, blocks.reshape(slots, TILE * TILE)]),
         ("r", [tile_count])],
        [((2, slots), i32, "s"), sent, sent, box] + [((size, 128), f32, "v")] * 2
        + [((pair_total, 128, 128), jnp.bfloat16, "v"), ((pair_total, planes, 128), f32, "v")] + [whole] * 3,
        scratch=[pltpu.VMEM((cells, 128), f32), pltpu.VMEM((slots, TILE * TILE), jnp.bfloat16), pltpu.VMEM(*tall), pltpu.VMEM((pair_total, 128, 128), f32)]
        + [pltpu.SMEM((slots,), i32)] * 3 + [pltpu.SMEM((9,), i32), pltpu.SemaphoreType.DMA((8,))],
        **sizes,
    )
    request = send_a
    rows_a = exchange(send_a, "gx", A)
    rows_b = exchange(send_b, "gx", B)
    (packs,) = call(edges_body, [("v", [field, cotan, rate_y])], [((3 * extent_x, 128), f32, "v")], **sizes)

    def onward(own, a, b, own_first, first, m):
        cut = lambda v, start: v[start + m * 2 * planes : start + (m + 1) * 2 * planes]
        return [cut(own, own_first), cut(a, first), cut(b, first)]

    wide = lambda m: jnp.concatenate(
        [request[:8], rows_a[:8], rows_b[:8], packs[: 2 * extent_x]] + onward(value_s, rows_a, rows_b, 0, head, m), axis=0
    )
    packs_b = exchange(wide(B), "gy", B)
    packs_a = exchange(wide(A), "gy", A)
    tiles_a, tiles_b, tiles_s = call(
        serve_body, [("v", [request, rows_b, rows_a, cotan_a, cotan_b, cotan])], [box, box, box],
        scratch=(pltpu.VMEM((8, 128), i32), pltpu.SMEM((8, 128), i32), pltpu.SemaphoreType.DMA(())), **sizes,
    )
    x_b = exchange(jnp.concatenate([tiles_b, late_b], axis=0), "gx", B)
    x_a = exchange(jnp.concatenate([tiles_a, late_a], axis=0), "gx", A)
    early, edge_rate, asked = call(
        pull_y_body, [("v", [cotan, cotan_a, cotan_b, rate_y, packs, request, rows_a, rows_b, packs_a, packs_b])],
        [whole, ((extent_x, 128), f32, "v"), ((8, 128), i32, "s")],
        scratch=(pltpu.VMEM((8, 128), i32), pltpu.VMEM((cells, 128), f32), pltpu.SemaphoreType.DMA(())), **sizes,
    )
    early, pad_rate = call(
        pull_x_body, [("v", [early, cotan, rate_x, rows_a, rows_b])], [whole, padded + ("v",)],
        scratch=(pad_scratch,) * 3, alias={0: 0}, **sizes,
    )
    grad, returned, send_a, send_b, send_s, edge_a, edge_b = call(
        middle_body, [("s", [order, asked]), ("r", [tile_count]), ("v", [early, pairs, x_a, x_b, tiles_s])],
        [whole, ((pair_total, planes, 128), f32, "v")] + [((extent_x + 2 * size, 128), f32, "v")] * 3 + [((size, 128), f32, "v")] * 2,
        alias={3: 0}, **sizes,
    )

    send_a, send_b, field = lax.optimization_barrier((send_a, send_b, field))
    last_y_b = exchange(send_b, "gy", B)
    last_y_a = exchange(send_a, "gy", A)
    (pushed,) = call(
        push_body, [("v", [field, pad_rate, rate_y, edge_rate, x_a, x_b, packs, packs_a, packs_b])],
        [whole], scratch=(pad_scratch,) * 2, **sizes,
    )
    last_y_a, last_y_b, pushed = lax.optimization_barrier((last_y_a, last_y_b, pushed))
    last_x_a = exchange(jnp.concatenate([edge_a] + onward(send_s, last_y_a, last_y_b, extent_x, extent_x, A), axis=0), "gx", A)
    last_x_b = exchange(jnp.concatenate([edge_b] + onward(send_s, last_y_a, last_y_b, extent_x, extent_x, B), axis=0), "gx", B)
    (inner,) = call(
        inner_body, [("v", [cotan, grad, pad_rate, rate_y])], [whole], scratch=(pad_scratch,) * 3, **sizes,
    )
    section, first_outer = call(
        section_body, [("s", [order, asked]), ("v", [pushed, returned, rows_a, rows_b, packs_a, packs_b, value_s])],
        [whole, ((pair_total, 128, 128), f32, "v")], alias={2: 0}, **sizes,
    )
    work = pltpu.VMEM((pair_total, 128, 128), f32)
    flat = ((slots * TILE // 2, 128), f32)
    total, early_blocks = call(
        rest_body,
        [("s", [order]), ("r", [tile_count]), ("v", [inner, edge_rate, packs, send_s, last_y_a, last_y_b, pairs, first_outer, picked])],
        [whole, flat + ("v",)], scratch=(work,), alias={2: 0}, **sizes,
    )
    grad_level_set, grad_blocks, _, _ = call(
        last_body,
        [("s", [order]), ("r", [tile_count]), ("v", [total, early_blocks, grad, pad_rate, last_x_b, last_x_a, pairs, first_outer, picked])],
        [((cells, 128), f32, "h"), flat + ("h",), whole, flat + ("v",)],
        scratch=(work, pltpu.SemaphoreType.DMA((2,))), alias={2: 2, 3: 3}, **sizes,
    )
    return (grad_level_set.reshape(planes, extent_x, extent_y), grad_blocks.reshape(1, 1, slots, TILE * TILE))


def solution(mesh):
    return jax.shard_map(
        shards,
        mesh=mesh,
        in_specs=(
            P(None, "gx", "gy"),
            P(None, "gx", "gy"),
            P(None, "gx", "gy"),
            P(None, "gx", "gy"),
            P("gx", "gy", None, None),
            P("gx", "gy"),
            P("gx", "gy", None),
            P("gx", "gy", None),
            P("gx", "gy", None),
        ),
        out_specs=(P(None, "gx", "gy"), P("gx", "gy", None, None)),
        check_vma=False,
    )
```

```python
import functools

import jax
import jax.numpy as jnp
from jax import lax
from jax.experimental import pallas as pl
from jax.experimental.pallas import tpu as pltpu
from jax.sharding import PartitionSpec as P

TILE = 64
ROUTE_MOST = 4
TIME_STEP = 0.3
WEIGHTS = (2.0 / 60.0, -13.0 / 60.0, 47.0 / 60.0, 27.0 / 60.0, -3.0 / 60.0)
PAD = 80
FLAT = 40
VMEM_LIMIT = 16 << 20

A, B, S = 0, 1, 2


def matching(count, which):
    return [(i, (i + (1 if (i % 2 == 0) == (which == B) else -1)) % count) for i in range(count)]


def exchange(block, axis, which):
    return lax.ppermute(block, axis, matching(lax.axis_size(axis), which))


def lanes(shape):
    return lax.broadcasted_iota(jnp.int32, shape, len(shape) - 1)


def roll(value, shift):
    return pltpu.roll(value, shift % 128 if isinstance(shift, int) else shift, axis=value.ndim - 1)


def split(value):
    high = value.astype(jnp.bfloat16)
    return high, (value - high.astype(jnp.float32)).astype(jnp.bfloat16)


def pair_dot(value, matrix, over):
    high, low = split(value)
    both = lax.dot_general(
        jnp.concatenate([high, low], axis=0),
        matrix,
        (((1,), (over,)), ((), ())),
        preferred_element_type=jnp.float32,
    )
    rows = value.shape[0]
    return both[:rows] + both[rows:]


def row_of(ref, x, planes, stride):
    return ref[pl.ds(x, planes, stride), :]


def tile_pair(ref, first, second, planes, extent_x):
    one = row_of(ref, first // 2, planes, extent_x)
    two = row_of(ref, second // 2, planes, extent_x)
    left = lanes(one.shape) < TILE
    turned = roll(jnp.where(left, two, one), TILE)
    return jnp.where(left, jnp.where(first % 2 == 0, one, turned), jnp.where(second % 2 == 1, two, turned))


def add_tile_pair(ref, first, second, value, planes, extent_x):
    lane = lanes(value.shape)
    turned = roll(value, TILE)
    for tile, half in ((first, 0), (second, 1)):
        spot = pl.ds(tile // 2, planes, extent_x)
        placed = jnp.where(tile % 2 == half, value, turned)
        keep = (lane // TILE) == tile % 2
        ref[spot, :] = ref[spot, :] + jnp.where(keep, placed, 0.0)


def edge_pack(ref, planes, extent_x):
    lane = lanes((extent_x, 128))
    packed = jnp.zeros((extent_x, 128), jnp.float32)
    for z in range(planes):
        plane = ref[z * extent_x : (z + 1) * extent_x, :]
        packed = jnp.where(lane // 8 == z, roll(plane, 8 * z + 3), packed)
    return packed


def edge_rows(ref, start, planes, extent_x):
    return jnp.concatenate([row_of(ref, start + j, planes, extent_x) for j in range(3)], axis=0)


def upwind(face_rate):
    return jnp.maximum(face_rate, 0.0), jnp.minimum(face_rate, 0.0)


UP = {2: WEIGHTS[0], 1: WEIGHTS[1], 0: WEIGHTS[2], -1: WEIGHTS[3], -2: WEIGHTS[4]}
DOWN = {1: WEIGHTS[4], 0: WEIGHTS[3], -1: WEIGHTS[2], -2: WEIGHTS[1], -3: WEIGHTS[0]}


def combine(up_part, down_part, k):
    total = 0.0
    if k in UP:
        total = total + UP[k] * up_part
    if k in DOWN:
        total = total + DOWN[k] * down_part
    return total


def fill_padded(pad_ref, field_ref, rows_a, rows_b, even, planes, extent_x):
    high = 8 + extent_x
    at_a = jnp.where(even, 5, high)
    at_b = jnp.where(even, high, 5)
    for z in range(planes):
        pad_ref[z * PAD + 8 : z * PAD + high, :] = field_ref[z * extent_x : (z + 1) * extent_x, :]
    for j in range(3):
        part = slice(j * planes, (j + 1) * planes)
        pad_ref[pl.ds(at_a + j, planes, PAD), :] = rows_a[part]
        pad_ref[pl.ds(at_b + j, planes, PAD), :] = rows_b[part]


def edge_join(from_a, from_b, even):
    low = jnp.where(even, from_a, from_b)
    high = jnp.where(even, from_b, from_a)
    return jnp.where(lanes(low.shape) % 8 < 3, low, high)


def adjoint_edges(own, halo, own_rate, halo_rate):
    lane = lanes(own.shape) % 8
    after = roll(jnp.where(lane == 3, own, halo), -1)
    before = roll(jnp.where(lane == 2, own, halo), 1)
    jump = jnp.where(lane < 3, after - halo, halo - before)
    rate = jnp.where(lane < 3, halo_rate, roll(jnp.where(lane == 2, own_rate, halo_rate), 1))
    rate_up, rate_down = upwind(rate)
    up_part, down_part = rate_up * jump, rate_down * jump
    low_side = 0.0
    high_side = 0.0
    for k in (-1, -2, -3):
        part = jnp.where(lane < 3, combine(up_part, down_part, k), 0.0)
        low_side = low_side + roll(part, -k)
    for k in (0, 1, 2):
        part = jnp.where((lane >= 3) & (lane < 6), combine(up_part, down_part, k), 0.0)
        high_side = high_side + roll(part, -(k + 1))
    return jnp.where(lane < 3, high_side, jnp.where(lane < 6, low_side, 0.0))


def adjoint_x(z, pad_ref, pad_rate_ref, up_ref, down_ref, extent_x):
    base = z * PAD
    here = pad_ref[pl.ds(base, PAD), :]
    jump = pad_ref[pl.ds(base + 1, PAD), :] - here
    rate_up, rate_down = upwind(pad_rate_ref[pl.ds(base, PAD), :])
    up_ref[pl.ds(base, PAD), :] = rate_up * jump
    down_ref[pl.ds(base, PAD), :] = rate_down * jump
    total = 0.0
    for k in range(-3, 3):
        if k in UP:
            total = total + UP[k] * up_ref[pl.ds(base + 8 + k, extent_x), :]
        if k in DOWN:
            total = total + DOWN[k] * down_ref[pl.ds(base + 8 + k, extent_x), :]
    return total


def band(weights, first_lost):
    row = lax.broadcasted_iota(jnp.int32, (128, 128), 0)
    gap = row - lax.broadcasted_iota(jnp.int32, (128, 128), 1)
    matrix = jnp.zeros((128, 128), jnp.float32)
    for k, weight in weights.items():
        matrix = jnp.where(gap == k, float(round(60.0 * weight)), matrix)
    return jnp.where(row >= first_lost, 0.0, matrix).astype(jnp.bfloat16)


def mix(left, matrix):
    return lax.dot_general(left, matrix, (((1,), (0,)), ((), ())), preferred_element_type=jnp.float32)


def adjoint_y(field_ref, rate_y_ref, planes, extent_x):
    up_matrix, down_matrix = band(UP, 127), band(DOWN, 127)
    matrix = jnp.concatenate([up_matrix, up_matrix, down_matrix, down_matrix], axis=0)
    rows = 4 * extent_x
    results = []
    for chunk in range(planes // 4):
        field = field_ref[chunk * rows : (chunk + 1) * rows, :]
        jump = roll(field, -1) - field
        rate_up, rate_down = upwind(rate_y_ref[chunk * rows : (chunk + 1) * rows, :])
        left = jnp.concatenate(split(rate_up * jump) + split(rate_down * jump), axis=1)
        results.append(mix(left, matrix))
    return results


LABELS = [(lx, ly, half) for ly in range(3) for lx in range(3) for half in range(2)]


def parities():
    return lax.rem(lax.axis_index("gx"), 2), lax.rem(lax.axis_index("gy"), 2)


def alive_lanes(value, order, number, total):
    lane = lanes(value.shape)
    return jnp.where(jnp.where(lane < TILE, order[0, 2 * number], order[0, 2 * number + 1]) < total, value, 0.0)


def part(ref, number, extent_x):
    return ref[number * extent_x : (number + 1) * extent_x]


def begin_body(
    heading, target, source, field, cotan, rate_y, blocks, cotan_cube, rate_cube, count,
    order, send_a, send_b, value_s, late_a, late_b, pairs, picked, field_out, cotan_out, rate_y_out,
    low_c, high_c, low_s, high_s, blocks_in, flat, square, heading_in, target_in, source_in, used, sems, *, planes, extent_x,
):
    moves = (
        (heading, heading_in), (target, target_in), (source, source_in),
        (blocks, blocks_in), (field, field_out),
        (cotan_cube.at[:, 0:8, :], low_c), (cotan_cube.at[:, extent_x - 8 : extent_x, :], high_c),
        (rate_cube.at[:, 0:8, :], low_s), (rate_cube.at[:, extent_x - 8 : extent_x, :], high_s),
        (cotan, cotan_out), (rate_y, rate_y_out),
    )
    copies = [pltpu.make_async_copy(a, b, sems.at[number]) for number, (a, b) in enumerate(moves)]
    for copy in copies:
        copy.start()
    parity_x, parity_y = parities()
    for label in range(9):
        used[label] = 0
    lane = lanes((8, 128))
    for copy in copies[:4]:
        copy.wait()
    asked = jnp.zeros((8, 128), jnp.int32)
    slots = heading.shape[0]
    for slot in range(slots):
        toward = heading_in[slot]
        across = (toward >= 3).astype(jnp.int32) + (toward >= 6).astype(jnp.int32)
        ex = (across - 1) * (1 - 2 * parity_x)
        ey = (toward - 3 * across - 1) * (1 - 2 * parity_y)
        lx = jnp.where(ex == 0, 2, (ex + 1) // 2)
        ly = jnp.where(ey == 0, 2, (ey + 1) // 2)
        label = ly * 3 + lx
        spot = label * ROUTE_MOST + used[label]
        used[label] = used[label] + 1
        order[0, spot] = slot
        order[1, spot] = source_in[slot]
        asked = jnp.where(lane == spot, target_in[slot], asked)
    for out in (send_a, send_b):
        out[0:8, :] = asked.astype(jnp.float32)
    half = TILE // 2
    for row in range(half):
        flat[pl.ds(row, slots, FLAT), :] = blocks_in[:, row * 128 : (row + 1) * 128].astype(jnp.float32)
    copies[4].wait()
    total = count[0, 0]
    size = 3 * planes
    first_half = lanes((half, 128)) < TILE
    for number, (lx, ly, side) in enumerate(LABELS):
        one = flat[pl.ds(pl.multiple_of(order[0, 2 * number] * FLAT, 8), half), :]
        two = flat[pl.ds(pl.multiple_of(order[0, 2 * number + 1] * FLAT, 8), half), :]
        turned = roll(jnp.where(first_half, two, one), TILE)
        square[number, pl.ds(0, half, 2), :] = jnp.where(first_half, one, 0.0)
        square[number, pl.ds(1, half, 2), :] = jnp.where(first_half, turned, 0.0)
        square[number, pl.ds(TILE, half, 2), :] = jnp.where(first_half, 0.0, turned)
        square[number, pl.ds(TILE + 1, half, 2), :] = jnp.where(first_half, 0.0, two)
        joined = square[number].astype(jnp.bfloat16)
        pairs[number] = joined
        tiles = tile_pair(field_out, order[1, 2 * number], order[1, 2 * number + 1], planes, extent_x)
        picked[number] = tiles
        value = pair_dot(alive_lanes(tiles, order, number, total), joined, 1)
        first = (0 if lx == S else 8 + 2 * size) + (ly * 2 + side) * planes
        (send_a, send_b, value_s)[lx][first : first + planes, :] = value
    even = parity_x == 0
    for copy in copies[5:9]:
        copy.wait()
    for number, (low, high) in enumerate(((low_c, high_c), (low_s, high_s))):
        low = jnp.concatenate([low[:, j, :] for j in range(3)], axis=0)
        high = jnp.concatenate([high[:, 5 + j, :] for j in range(3)], axis=0)
        spot = slice(8 + number * size, 8 + (number + 1) * size)
        send_a[spot, :] = jnp.where(even, low, high)
        send_b[spot, :] = jnp.where(even, high, low)
    high = extent_x - 3
    late_a[...] = edge_rows(field_out, jnp.where(even, 0, high), planes, extent_x)
    late_b[...] = edge_rows(field_out, jnp.where(even, high, 0), planes, extent_x)
    copies[9].wait()
    copies[10].wait()


def local_body(field, cotan, rate_y, packs, early, section, *, planes, extent_x):
    for number, ref in enumerate((rate_y, field, cotan)):
        packs[number * extent_x : (number + 1) * extent_x, :] = edge_pack(ref, planes, extent_x)
    rows = 4 * extent_x
    for chunk, pulled in enumerate(adjoint_y(cotan, rate_y, planes, extent_x)):
        spot = slice(chunk * rows, (chunk + 1) * rows)
        early[spot, :] = 0.5 * cotan[spot, :] + (0.5 * TIME_STEP / 60.0) * pulled
    both = jnp.concatenate(
        [band({k: WEIGHTS[k + 2] for k in range(-2, 3)}, 128), band({k: WEIGHTS[3 - k] for k in range(-1, 4)}, 128)], axis=1
    )
    both = jnp.concatenate([both, both], axis=0)
    first_lane = lanes((rows, 128)) == 0
    for chunk in range(planes // 4):
        spot = slice(chunk * rows, (chunk + 1) * rows)
        parts = mix(jnp.concatenate(split(field[spot, :]), axis=1), both)
        rate_up, rate_down = upwind(rate_y[spot, :])
        flux = rate_up * parts[:, :128] + rate_down * parts[:, 128:]
        change = jnp.where(first_lane, 0.0, roll(flux, 1)) - flux
        section[spot, :] = field[spot, :] + (TIME_STEP / 60.0) * change


def merge_lists(a, b, s):
    group = lax.rem(lanes((8, 128)), 12) // ROUTE_MOST
    return jnp.where(group == 0, a, jnp.where(group == 1, b, s)).astype(jnp.int32)


def to_scalars(value, list_ref, asked, sem):
    list_ref[...] = value
    copy = pltpu.make_async_copy(list_ref, asked, sem)
    copy.start()
    copy.wait()


def serve_body(request, got_b, got_a, cotan_a, cotan_b, cotan, out_a, out_b, out_s, list_ref, asked, sem, *, planes, extent_x):
    to_scalars(merge_lists(got_a[0:8], got_b[0:8], request[0:8]), list_ref, asked, sem)
    for lx, ly, half in LABELS:
        at = ly * 12 + lx * ROUTE_MOST + 2 * half
        tiles = tile_pair((cotan_a, cotan_b, cotan)[ly], asked[0, at], asked[0, at + 1], planes, extent_x)
        first = (ly * 2 + half) * planes
        (out_a, out_b, out_s)[lx][first : first + planes, :] = tiles


def rows_at(ref, first, planes):
    return ref[first : first + planes, :]


def give_back(back, number, scale, order, pairs, field, planes, extent_x):
    pulled = scale * pair_dot(back, pairs[number], 0)
    add_tile_pair(field, order[1, 2 * number], order[1, 2 * number + 1], pulled, planes, extent_x)


def pull_body(
    order, count, early, cotan, cotan_a, cotan_b, rate_x, packs, request, rows_a, rows_b, from_a, from_b, own, pairs,
    grad, edge_rate, asked, pad_rate, returned, list_ref, joined, pad, up_ref, down_ref, sem, *, planes, extent_x,
):
    row = lax.broadcasted_iota(jnp.int32, (8, 128), 0)
    spread = [
        jnp.broadcast_to(merge_lists(a, b, c)[0:1], (8, 128))
        for a, b, c in (
            (from_a[8:16], from_a[16:24], from_a[0:8]),
            (from_b[8:16], from_b[16:24], from_b[0:8]),
            (rows_a[0:8], rows_b[0:8], request[0:8]),
        )
    ]
    list_ref[...] = jnp.where(row == 0, spread[0], jnp.where(row == 1, spread[1], spread[2]))
    copy = pltpu.make_async_copy(list_ref, asked, sem)
    copy.start()
    parity_x, parity_y = parities()
    even_x, even_y = parity_x == 0, parity_y == 0
    size = 3 * planes
    fill_padded(pad, cotan, rows_a[8 : 8 + size], rows_b[8 : 8 + size], even_x, planes, extent_x)
    fill_padded(pad_rate, rate_x, rows_a[8 + size : 8 + 2 * size], rows_b[8 + size : 8 + 2 * size], even_x, planes, extent_x)
    lane = lanes((extent_x, 128))
    upper = jnp.where(even_y, lane, 127 - lane) >= TILE
    for z in range(planes):
        plane = slice(z * extent_x, (z + 1) * extent_x)
        joined[plane, :] = jnp.where(upper, cotan_a[plane, :], cotan_b[plane, :])
    halo = edge_pack(joined, planes, extent_x)
    halo_rate = edge_join(from_a[24 : 24 + extent_x], from_b[24 : 24 + extent_x], even_y)
    edge_rate[...] = halo_rate
    edges = adjoint_edges(part(packs, 2, extent_x), halo, part(packs, 0, extent_x), halo_rate)
    for z in range(planes):
        spot = pl.ds(z * extent_x, extent_x)
        rim = roll(edges, 125 - 8 * z)
        rim = jnp.where((lane < 3) | (lane >= 125), rim, 0.0)
        along_x = adjoint_x(z, pad, pad_rate, up_ref, down_ref, extent_x)
        grad[spot, :] = early[spot, :] + (0.5 * TIME_STEP) * (along_x + rim)
    for number, (lx, ly, half) in enumerate(LABELS):
        if lx == S:
            back = alive_lanes(rows_at(own, (ly * 2 + half) * planes, planes), order, number, count[0, 0])
            returned[number] = back
            give_back(back, number, 0.5 * TIME_STEP, order, pairs, grad, planes, extent_x)
    copy.wait()


def push_body(early, field, pad_rate, edge_rate, rows_a, rows_b, packs, packs_a, packs_b, section, pad, flux_ref, *, planes, extent_x):
    parity_x, parity_y = parities()
    even_x, even_y = parity_x == 0, parity_y == 0
    first = 6 * planes
    fill_padded(pad, field, rows_a[first : first + 3 * planes], rows_b[first : first + 3 * planes], even_x, planes, extent_x)
    second = slice(24 + extent_x, 24 + 2 * extent_x)
    halo = edge_join(packs_a[second], packs_b[second], even_y)
    own_rate = part(packs, 0, extent_x)
    lane8 = lanes(halo.shape) % 8

    def shifted_by(value, k):
        return roll(value, -k) if k else value

    def stencils(value):
        up_part = sum(WEIGHTS[j] * shifted_by(value, j - 2) for j in range(5))
        down_part = sum(WEIGHTS[j] * shifted_by(value, 3 - j) for j in range(5))
        return up_part, down_part

    up_part, down_part = stencils(jnp.where(lane8 < 3, halo, jnp.where(lane8 < 6, part(packs, 1, extent_x), 0.0)))
    rate_up, rate_down = upwind(edge_rate[...])
    flux_low = roll(rate_up * up_part + rate_down * down_part, 1)
    rate_up, rate_down = upwind(own_rate)
    up_part, down_part = stencils(jnp.where((lane8 >= 3) & (lane8 < 6), halo, 0.0))
    flux_high = jnp.where(lane8 < 3, rate_up * up_part + rate_down * down_part, 0.0)
    up_part, down_part = stencils(jnp.where(lane8 < 3, halo, 0.0))
    flux_first = jnp.where((lane8 >= 3) & (lane8 < 5), rate_up * up_part + rate_down * down_part, 0.0)
    change_edge = roll(flux_high, 1) - flux_high
    before = jnp.where(lane8 == 3, flux_low, roll(flux_first, 1))
    change_edge = jnp.where(lane8 < 3, change_edge, jnp.where(lane8 < 6, before - flux_first, 0.0))
    for z in range(planes):
        base = z * PAD
        spot = pl.ds(z * extent_x, extent_x)
        window = extent_x + 8
        near = {k: pad[pl.ds(base + 7 + k, window), :] for k in range(-2, 4)}
        rate_up, rate_down = upwind(pad_rate[pl.ds(base + 7, window), :])
        flux_ref[pl.ds(base, window), :] = rate_up * sum(WEIGHTS[j] * near[j - 2] for j in range(5)) + rate_down * sum(
            WEIGHTS[j] * near[3 - j] for j in range(5)
        )
        change = flux_ref[pl.ds(base, extent_x), :] - flux_ref[pl.ds(base + 1, extent_x), :]
        lane = lanes(change.shape)
        rim = roll(change_edge, 125 - 8 * z)
        rim = jnp.where((lane < 3) | (lane >= 125), rim, 0.0)
        section[spot, :] = early[spot, :] + TIME_STEP * (change + rim)


def compact(packed, low):
    chosen = jnp.where(low, roll(packed, -3), packed)
    half = packed.shape[0] // 2
    return jnp.where(lanes((half, 128)) % 8 < 4, chosen[:half], roll(chosen[half:], 4))


def expand_join(from_a, from_b, even):
    from_a, from_b = (jnp.concatenate([v, roll(v, -4)], axis=0) for v in (from_a, from_b))
    low = jnp.where(even, from_a, from_b)
    high = jnp.where(even, from_b, from_a)
    return jnp.where(lanes(low.shape) % 8 < 3, low, roll(high, 3))


def gather_pair(asked, field, out, first, lx, ly, half, planes, extent_x):
    at = ly * 12 + lx * ROUTE_MOST + 2 * half
    out[first : first + planes, :] = tile_pair(field, asked[ly, at], asked[ly, at + 1], planes, extent_x)


def middle_body(order, asked, count, early, returned_early, pairs, x_a, x_b, grad, returned, send_a, send_b, *, planes, extent_x):
    for number, (lx, ly, half) in enumerate(LABELS):
        if lx != S:
            back = rows_at((x_a, x_b)[lx], (ly * 2 + half) * planes, planes)
            back = alive_lanes(back, order, number, count[0, 0])
            returned[number] = back
            give_back(back, number, 0.5 * TIME_STEP, order, pairs, grad, planes, extent_x)
    for lx, ly, half in LABELS:
        if ly != S:
            gather_pair(asked, grad, (send_a, send_b)[ly], (lx * 2 + half) * planes, lx, ly, half, planes, extent_x)
    packed = edge_pack(grad, planes, extent_x)
    even_y = parities()[1] == 0
    send_a[6 * planes :, :] = compact(packed, even_y)
    send_b[6 * planes :, :] = compact(packed, jnp.logical_not(even_y))


def after_body(asked, grad, own, pack, rows_a, rows_b, *, planes, extent_x):
    pack[...] = edge_pack(grad, planes, extent_x)
    for lx, ly, half in LABELS:
        if ly == S:
            gather_pair(asked, grad, own, (lx * 2 + half) * planes, lx, ly, half, planes, extent_x)
    even_x = parities()[0] == 0
    high = extent_x - 3
    rows_a[...] = edge_rows(grad, jnp.where(even_x, 0, high), planes, extent_x)
    rows_b[...] = edge_rows(grad, jnp.where(even_x, high, 0), planes, extent_x)


def row_back(ly, half, y_a, y_b, own, planes, extent_x):
    if ly == S:
        return rows_at(own, (S * 2 + half) * planes, planes)
    return rows_at((y_a, y_b)[ly], (S * 2 + half) * planes, planes)


def inner_body(
    cotan, grad, pad_rate, rate_y, out, pad, up_ref, down_ref, *, planes, extent_x,
):
    high = 8 + extent_x
    for z in range(planes):
        pad[z * PAD + 8 : z * PAD + high, :] = grad[z * extent_x : (z + 1) * extent_x, :]
    for j in range(3):
        pad[pl.ds(5 + j, planes, PAD), :] = row_of(grad, 0, planes, extent_x)
        pad[pl.ds(high + j, planes, PAD), :] = row_of(grad, extent_x - 1, planes, extent_x)
    along_y = adjoint_y(grad, rate_y, planes, extent_x)
    for z in range(planes):
        spot = pl.ds(z * extent_x, extent_x)
        pulled = along_y[z // 4][z % 4 * extent_x : (z % 4 + 1) * extent_x] * (1.0 / 60.0)
        pulled = pulled + adjoint_x(z, pad, pad_rate, up_ref, down_ref, extent_x)
        out[spot, :] = 0.5 * cotan[spot, :] + grad[spot, :] + TIME_STEP * pulled


def outer(left, right):
    left_high, left_low = split(left)
    right_high, right_low = split(right)
    return lax.dot_general(
        jnp.concatenate([left_high, left_high, left_low], axis=0),
        jnp.concatenate([right_high, right_low, right_high], axis=0),
        (((0,), (0,)), ((), ())),
        preferred_element_type=jnp.float32,
    )


def merge_blocks(value, number, work, blocks):
    work[number] = value
    half = TILE // 2
    half_lane = lanes((half, 128)) < TILE
    even_one, odd_one, even_two, odd_two = (work[number, pl.ds(first, half, 2), :] for first in (0, 1, TILE, TILE + 1))
    turned = roll(jnp.where(half_lane, odd_one, even_two), TILE)
    blocks[2 * number] = jnp.where(half_lane, even_one, turned)
    blocks[2 * number + 1] = jnp.where(half_lane, turned, odd_two)


def start_blocks(number, order, blocks, out_blocks, sems):
    half = TILE // 2
    copies = []
    for which in range(2):
        spot = pl.ds(pl.multiple_of(order[0, 2 * number + which] * half, 8), half)
        copies.append(pltpu.make_async_copy(blocks.at[2 * number + which], out_blocks.at[spot, :], sems.at[2 * number + which]))
        copies[-1].start()
    return copies


def section_body(
    order, asked, early, returned, x_a, x_b, y_a, y_b, value_s, section, first_outer, *, planes, extent_x,
):
    for lx, ly, half in LABELS:
        if ly == S:
            came = rows_at((x_a, x_b, value_s)[lx], (0 if lx == S else 8 + 6 * planes) + (S * 2 + half) * planes, planes)
        else:
            came = rows_at((y_a, y_b)[ly], 24 + 2 * extent_x + ((1, 2, 0)[lx] * 2 + half) * planes, planes)
        at = ly * 12 + lx * ROUTE_MOST + 2 * half
        add_tile_pair(section, asked[ly, at], asked[ly, at + 1], TIME_STEP * came, planes, extent_x)
    for number in range(first_outer.shape[0]):
        found = tile_pair(section, order[1, 2 * number], order[1, 2 * number + 1], planes, extent_x)
        first_outer[number] = outer((0.5 * TIME_STEP) * returned[number], found)


def rest_body(
    order, count, early, edge_rate, packs, pack, y_a, y_b, own, pairs, first_outer, picked, total, blocks, work, *, planes, extent_x,
):
    halo = expand_join(y_a[6 * planes :], y_b[6 * planes :], parities()[1] == 0)
    edges = adjoint_edges(pack[...], halo, part(packs, 0, extent_x), edge_rate[...])
    lane = lanes((extent_x, 128))
    backs = {}
    for number, (lx, ly, half) in enumerate(LABELS):
        if lx == S:
            backs[number] = alive_lanes(row_back(ly, half, y_a, y_b, own, planes, extent_x), order, number, count[0, 0])
            value = first_outer[number] + outer(TIME_STEP * backs[number], picked[number])
            merge_blocks(value, number, work, blocks)
    for z in range(planes):
        spot = pl.ds(z * extent_x, extent_x)
        rim = roll(edges, 125 - 8 * z)
        total[spot, :] = total[spot, :] + TIME_STEP * jnp.where((lane < 3) | (lane >= 125), rim, 0.0)
    for number, back in backs.items():
        give_back(back, number, TIME_STEP, order, pairs, total, planes, extent_x)


def last_body(
    order, count, early, blocks_early, grad, pad_rate, x_b, x_a, pairs, first_outer, picked, out, out_blocks, total, work, blocks, sems,
    *, planes, extent_x,
):
    copies = []
    for number, (lx, _, _) in enumerate(LABELS):
        if lx == S:
            copies += start_blocks(number, order, blocks_early, out_blocks, sems)
    even_x = parities()[0] == 0
    size = 3 * planes
    low_rows = [jnp.where(even_x, x_a[j * planes : (j + 1) * planes], x_b[j * planes : (j + 1) * planes]) for j in range(3)]
    high_rows = [jnp.where(even_x, x_b[j * planes : (j + 1) * planes], x_a[j * planes : (j + 1) * planes]) for j in range(3)]
    first_cell = row_of(grad, 0, planes, extent_x)
    last_cell = row_of(grad, extent_x - 1, planes, extent_x)
    for line, low_face in ((low_rows + [first_cell], -3), ([last_cell] + high_rows, extent_x - 1)):
        faces = []
        for j in range(3):
            rate_up, rate_down = upwind(row_of(pad_rate, 8 + low_face + j, planes, PAD))
            jump = line[j + 1] - line[j]
            faces.append((rate_up * jump, rate_down * jump))
        cells = range(0, 3) if low_face < 0 else range(extent_x - 3, extent_x)
        for cell in cells:
            added = 0.0
            for j in range(3):
                k = low_face + j - cell
                if -3 <= k <= 2:
                    added = added + combine(*faces[j], k)
            spot = pl.ds(cell, planes, extent_x)
            total[spot, :] = total[spot, :] + TIME_STEP * added
    backs = {}
    for number, (lx, ly, half) in enumerate(LABELS):
        if lx != S:
            back = rows_at((x_a, x_b)[lx], size + ((1, 2, 0)[ly] * 2 + half) * planes, planes)
            backs[number] = alive_lanes(back, order, number, count[0, 0])
            give_back(backs[number], number, TIME_STEP, order, pairs, total, planes, extent_x)
    copies.append(pltpu.make_async_copy(total, out, sems.at[2 * len(LABELS)]))
    copies[-1].start()
    for number, back in backs.items():
        merge_blocks(first_outer[number] + outer(TIME_STEP * back, picked[number]), number, work, blocks)
        copies += start_blocks(number, order, blocks, out_blocks, sems)
    for copy in copies:
        copy.wait()


SPACE = {"v": pltpu.VMEM, "s": pltpu.SMEM, "h": pltpu.HBM}


def call(body, ins, outs, scratch=(), alias=None, **sizes):
    values, specs, shapes, out_specs = [], [], [], []
    for kind, group in ins:
        for value in group:
            values.append(value if kind == "r" else pltpu.with_memory_space_constraint(value, SPACE[kind]))
            specs.append(pl.BlockSpec(memory_space=SPACE["s" if kind == "r" else kind]))
    for shape, dtype, kind in outs:
        shapes.append(SPACE[kind](shape, dtype))
        out_specs.append(pl.BlockSpec(memory_space=SPACE[kind]))
    return pl.pallas_call(
        functools.partial(body, **sizes),
        out_shape=tuple(shapes),
        in_specs=specs,
        out_specs=tuple(out_specs),
        scratch_shapes=list(scratch),
        input_output_aliases=alias or {},
        compiler_params=pltpu.CompilerParams(vmem_limit_bytes=VMEM_LIMIT),
        name=body.__name__,
    )(*values)


def shards(
    level_set, speed_x, speed_y, cotangent, blocks, tile_count, source_tile, dest_offset, dest_tile
):
    planes, extent_x, extent_y = level_set.shape
    slots = source_tile.shape[2]
    cells = planes * extent_x
    f32, i32 = jnp.float32, jnp.int32
    field, rate_x, rate_y, cotan = (v.reshape(cells, extent_y) for v in (level_set, speed_x, speed_y, cotangent))
    sizes = dict(planes=planes, extent_x=extent_x)
    size = 3 * planes
    pair_total = slots // 2
    box = ((2 * size, 128), f32, "v")
    padded = ((planes * PAD + 8, extent_y), f32)
    pad_scratch = pltpu.VMEM(*padded)
    whole = ((cells, 128), f32, "v")

    cotan_a = exchange(cotan, "gy", A)
    cotan_b = exchange(cotan, "gy", B)
    head = 8 + 2 * size
    head = 8 + 2 * size
    sent = ((head + 2 * size, 128), f32, "v")
    tall = ((slots * TILE // 2, 128), f32)
    order, send_a, send_b, value_s, late_a, late_b, pairs, picked, field, cotan, rate_y = call(
        begin_body,
        [("h", [v.reshape(slots) for v in (dest_offset, dest_tile, source_tile)] + [field, cotan, rate_y, blocks.reshape(slots, TILE * TILE), cotangent, speed_x]),
         ("r", [tile_count])],
        [((2, slots), i32, "s"), sent, sent, box] + [((size, 128), f32, "v")] * 2
        + [((pair_total, 128, 128), jnp.bfloat16, "v"), ((pair_total, planes, 128), f32, "v")] + [whole] * 3,
        scratch=[pltpu.VMEM((planes, 8, 128), f32)] * 4 + [pltpu.VMEM((slots, TILE * TILE), jnp.bfloat16), pltpu.VMEM((slots * FLAT, 128), f32), pltpu.VMEM((pair_total, 128, 128), f32)]
        + [pltpu.SMEM((slots,), i32)] * 3 + [pltpu.SMEM((9,), i32), pltpu.SemaphoreType.DMA((11,))],
        **sizes,
    )
    request = send_a
    rows_a = exchange(send_a, "gx", A)
    rows_b = exchange(send_b, "gx", B)
    packs, early, pushed = call(
        local_body, [("v", [field, cotan, rate_y])], [((3 * extent_x, 128), f32, "v"), whole, whole], **sizes
    )

    def onward(own, a, b, own_first, first, m):
        cut = lambda v, start: v[start + m * 2 * planes : start + (m + 1) * 2 * planes]
        return [cut(own, own_first), cut(a, first), cut(b, first)]

    wide = lambda m: jnp.concatenate(
        [request[:8], rows_a[:8], rows_b[:8], packs[: 2 * extent_x]] + onward(value_s, rows_a, rows_b, 0, head, m), axis=0
    )
    packs_b = exchange(wide(B), "gy", B)
    packs_a = exchange(wide(A), "gy", A)
    tiles_a, tiles_b, tiles_s = call(
        serve_body, [("v", [request, rows_b, rows_a, cotan_a, cotan_b, cotan])], [box, box, box],
        scratch=(pltpu.VMEM((8, 128), i32), pltpu.SMEM((8, 128), i32), pltpu.SemaphoreType.DMA(())), **sizes,
    )
    x_b = exchange(jnp.concatenate([tiles_b, late_b], axis=0), "gx", B)
    x_a = exchange(jnp.concatenate([tiles_a, late_a], axis=0), "gx", A)
    small = ((extent_x, 128), f32, "v")
    eighteen = ((pair_total, planes, 128), f32, "v")
    early, edge_rate, asked, pad_rate, returned = call(
        pull_body,
        [("s", [order]), ("r", [tile_count]),
         ("v", [early, cotan, cotan_a, cotan_b, rate_x, packs, request, rows_a, rows_b, packs_a, packs_b, tiles_s, pairs])],
        [whole, small, ((8, 128), i32, "s"), padded + ("v",), eighteen],
        scratch=(pltpu.VMEM((8, 128), i32), pltpu.VMEM((cells, 128), f32), pad_scratch, pad_scratch, pad_scratch, pltpu.SemaphoreType.DMA(())),
        alias={2: 0}, **sizes,
    )
    grad, returned, send_a, send_b = call(
        middle_body, [("s", [order, asked]), ("r", [tile_count]), ("v", [early, returned, pairs, x_a, x_b])],
        [whole, eighteen] + [((6 * planes + extent_x // 2, 128), f32, "v")] * 2, alias={3: 0, 4: 1}, **sizes,
    )
    send_a, send_b, pushed, grad = lax.optimization_barrier((send_a, send_b, pushed, grad))
    last_y_b = exchange(send_b, "gy", B)
    last_y_a = exchange(send_a, "gy", A)
    own, pack, edge_a, edge_b = call(
        after_body, [("s", [asked]), ("v", [grad])], [box, small] + [((size, 128), f32, "v")] * 2, **sizes,
    )
    (pushed,) = call(
        push_body, [("v", [pushed, field, pad_rate, edge_rate, x_a, x_b, packs, packs_a, packs_b])],
        [whole], scratch=(pad_scratch,) * 2, alias={0: 0}, **sizes,
    )
    last_y_a, last_y_b, pushed = lax.optimization_barrier((last_y_a, last_y_b, pushed))
    last_x_a = exchange(jnp.concatenate([edge_a] + onward(own, last_y_a, last_y_b, 0, 0, A), axis=0), "gx", A)
    last_x_b = exchange(jnp.concatenate([edge_b] + onward(own, last_y_a, last_y_b, 0, 0, B), axis=0), "gx", B)
    (inner,) = call(inner_body, [("v", [cotan, grad, pad_rate, rate_y])], [whole], scratch=(pad_scratch,) * 3, **sizes)
    section, first_outer = call(
        section_body, [("s", [order, asked]), ("v", [pushed, returned, rows_a, rows_b, packs_a, packs_b, value_s])],
        [whole, ((pair_total, 128, 128), f32, "v")], alias={2: 0}, **sizes,
    )
    work = pltpu.VMEM((pair_total, 128, 128), f32)
    blocks_out = pltpu.VMEM((slots, TILE // 2, 128), f32)
    inner, early_blocks = call(
        rest_body,
        [("s", [order]), ("r", [tile_count]), ("v", [inner, edge_rate, packs, pack, last_y_a, last_y_b, own, pairs, first_outer, picked])],
        [whole, ((slots, TILE // 2, 128), f32, "v")], scratch=(work,), alias={2: 0}, **sizes,
    )
    grad_level_set, grad_blocks, _ = call(
        last_body,
        [("s", [order]), ("r", [tile_count]), ("v", [inner, early_blocks, grad, pad_rate, last_x_b, last_x_a, pairs, first_outer, picked])],
        [((cells, 128), f32, "h"), tall + ("h",), whole],
        scratch=(work, blocks_out, pltpu.SemaphoreType.DMA((slots + 1,))), alias={2: 2}, **sizes,
    )
    return (grad_level_set.reshape(planes, extent_x, extent_y), grad_blocks.reshape(1, 1, slots, TILE * TILE))


def solution(mesh):
    return jax.shard_map(
        shards,
        mesh=mesh,
        in_specs=(
            P(None, "gx", "gy"),
            P(None, "gx", "gy"),
            P(None, "gx", "gy"),
            P(None, "gx", "gy"),
            P("gx", "gy", None, None),
            P("gx", "gy"),
            P("gx", "gy", None),
            P("gx", "gy", None),
            P("gx", "gy", None),
        ),
        out_specs=(P(None, "gx", "gy"), P("gx", "gy", None, None)),
        check_vma=False,
    )
```

```python
import functools

import jax
import jax.numpy as jnp
from jax import lax
from jax.experimental import pallas as pl
from jax.experimental.pallas import tpu as pltpu
from jax.sharding import PartitionSpec as P

TILE = 64
ROUTE_MOST = 4
TIME_STEP = 0.3
WEIGHTS = (2.0 / 60.0, -13.0 / 60.0, 47.0 / 60.0, 27.0 / 60.0, -3.0 / 60.0)
PAD = 80
FLAT = 40
VMEM_LIMIT = 16 << 20

A, B, S = 0, 1, 2


def matching(count, which):
    return [(i, (i + (1 if (i % 2 == 0) == (which == B) else -1)) % count) for i in range(count)]


def exchange(block, axis, which):
    return lax.ppermute(block, axis, matching(lax.axis_size(axis), which))


def lanes(shape):
    return lax.broadcasted_iota(jnp.int32, shape, len(shape) - 1)


def roll(value, shift):
    return pltpu.roll(value, shift % 128 if isinstance(shift, int) else shift, axis=value.ndim - 1)


def split(value):
    high = value.astype(jnp.bfloat16)
    return high, (value - high.astype(jnp.float32)).astype(jnp.bfloat16)


def pair_dot(value, matrix, over):
    high, low = split(value)
    both = lax.dot_general(
        jnp.concatenate([high, low], axis=0),
        matrix,
        (((1,), (over,)), ((), ())),
        preferred_element_type=jnp.float32,
    )
    rows = value.shape[0]
    return both[:rows] + both[rows:]


def row_of(ref, x, planes, stride):
    return ref[pl.ds(x, planes, stride), :]


def tile_pair(ref, first, second, planes, extent_x):
    one = row_of(ref, first // 2, planes, extent_x)
    two = row_of(ref, second // 2, planes, extent_x)
    left = lanes(one.shape) < TILE
    turned = roll(jnp.where(left, two, one), TILE)
    return jnp.where(left, jnp.where(first % 2 == 0, one, turned), jnp.where(second % 2 == 1, two, turned))


def add_tile_pair(ref, first, second, value, planes, extent_x):
    lane = lanes(value.shape)
    turned = roll(value, TILE)
    for tile, half in ((first, 0), (second, 1)):
        spot = pl.ds(tile // 2, planes, extent_x)
        placed = jnp.where(tile % 2 == half, value, turned)
        keep = (lane // TILE) == tile % 2
        ref[spot, :] = ref[spot, :] + jnp.where(keep, placed, 0.0)


def edge_pack(ref, planes, extent_x):
    lane = lanes((extent_x, 128))
    packed = jnp.zeros((extent_x, 128), jnp.float32)
    for z in range(planes):
        plane = ref[z * extent_x : (z + 1) * extent_x, :]
        packed = jnp.where(lane // 8 == z, roll(plane, 8 * z + 3), packed)
    return packed


def edge_rows(ref, start, planes, extent_x):
    return jnp.concatenate([row_of(ref, start + j, planes, extent_x) for j in range(3)], axis=0)


def upwind(face_rate):
    return jnp.maximum(face_rate, 0.0), jnp.minimum(face_rate, 0.0)


UP = {2: WEIGHTS[0], 1: WEIGHTS[1], 0: WEIGHTS[2], -1: WEIGHTS[3], -2: WEIGHTS[4]}
DOWN = {1: WEIGHTS[4], 0: WEIGHTS[3], -1: WEIGHTS[2], -2: WEIGHTS[1], -3: WEIGHTS[0]}


def combine(up_part, down_part, k):
    total = 0.0
    if k in UP:
        total = total + UP[k] * up_part
    if k in DOWN:
        total = total + DOWN[k] * down_part
    return total


def fill_padded(pad_ref, field_ref, rows_a, rows_b, even, planes, extent_x):
    high = 8 + extent_x
    at_a = jnp.where(even, 5, high)
    at_b = jnp.where(even, high, 5)
    for z in range(planes):
        pad_ref[z * PAD + 8 : z * PAD + high, :] = field_ref[z * extent_x : (z + 1) * extent_x, :]
    for j in range(3):
        part = slice(j * planes, (j + 1) * planes)
        pad_ref[pl.ds(at_a + j, planes, PAD), :] = rows_a[part]
        pad_ref[pl.ds(at_b + j, planes, PAD), :] = rows_b[part]


def edge_join(from_a, from_b, even):
    low = jnp.where(even, from_a, from_b)
    high = jnp.where(even, from_b, from_a)
    return jnp.where(lanes(low.shape) % 8 < 3, low, high)


def adjoint_edges(own, halo, own_rate, halo_rate):
    lane = lanes(own.shape) % 8
    after = roll(jnp.where(lane == 3, own, halo), -1)
    before = roll(jnp.where(lane == 2, own, halo), 1)
    jump = jnp.where(lane < 3, after - halo, halo - before)
    rate = jnp.where(lane < 3, halo_rate, roll(jnp.where(lane == 2, own_rate, halo_rate), 1))
    rate_up, rate_down = upwind(rate)
    up_part, down_part = rate_up * jump, rate_down * jump
    low_side = 0.0
    high_side = 0.0
    for k in (-1, -2, -3):
        part = jnp.where(lane < 3, combine(up_part, down_part, k), 0.0)
        low_side = low_side + roll(part, -k)
    for k in (0, 1, 2):
        part = jnp.where((lane >= 3) & (lane < 6), combine(up_part, down_part, k), 0.0)
        high_side = high_side + roll(part, -(k + 1))
    return jnp.where(lane < 3, high_side, jnp.where(lane < 6, low_side, 0.0))


def adjoint_x(z, pad_ref, pad_rate_ref, up_ref, down_ref, extent_x):
    base = z * PAD
    here = pad_ref[pl.ds(base, PAD), :]
    jump = pad_ref[pl.ds(base + 1, PAD), :] - here
    rate_up, rate_down = upwind(pad_rate_ref[pl.ds(base, PAD), :])
    up_ref[pl.ds(base, PAD), :] = rate_up * jump
    down_ref[pl.ds(base, PAD), :] = rate_down * jump
    total = 0.0
    for k in range(-3, 3):
        if k in UP:
            total = total + UP[k] * up_ref[pl.ds(base + 8 + k, extent_x), :]
        if k in DOWN:
            total = total + DOWN[k] * down_ref[pl.ds(base + 8 + k, extent_x), :]
    return total


def band(weights, first_lost):
    row = lax.broadcasted_iota(jnp.int32, (128, 128), 0)
    gap = row - lax.broadcasted_iota(jnp.int32, (128, 128), 1)
    matrix = jnp.zeros((128, 128), jnp.float32)
    for k, weight in weights.items():
        matrix = jnp.where(gap == k, float(round(60.0 * weight)), matrix)
    return jnp.where(row >= first_lost, 0.0, matrix).astype(jnp.bfloat16)


def mix(left, matrix):
    return lax.dot_general(left, matrix, (((1,), (0,)), ((), ())), preferred_element_type=jnp.float32)


def adjoint_y(field_ref, rate_y_ref, planes, extent_x):
    up_matrix, down_matrix = band(UP, 127), band(DOWN, 127)
    matrix = jnp.concatenate([up_matrix, up_matrix, down_matrix, down_matrix], axis=0)
    rows = 4 * extent_x
    results = []
    for chunk in range(planes // 4):
        field = field_ref[chunk * rows : (chunk + 1) * rows, :]
        jump = roll(field, -1) - field
        rate_up, rate_down = upwind(rate_y_ref[chunk * rows : (chunk + 1) * rows, :])
        left = jnp.concatenate(split(rate_up * jump) + split(rate_down * jump), axis=1)
        results.append(mix(left, matrix))
    return results


LABELS = [(lx, ly, half) for ly in range(3) for lx in range(3) for half in range(2)]


def parities():
    return lax.rem(lax.axis_index("gx"), 2), lax.rem(lax.axis_index("gy"), 2)


def alive_lanes(value, order, number, total):
    lane = lanes(value.shape)
    return jnp.where(jnp.where(lane < TILE, order[0, 2 * number], order[0, 2 * number + 1]) < total, value, 0.0)


def part(ref, number, extent_x):
    return ref[number * extent_x : (number + 1) * extent_x]


def begin_body(
    heading, target, source, field, cotan, rate_y, blocks, cotan_cube, rate_cube, count,
    order, send_a, send_b, value_s, late_a, late_b, pairs, picked, field_out, cotan_out, rate_y_out,
    low_c, high_c, low_s, high_s, blocks_in, flat, square, heading_in, target_in, source_in, sems, *, planes, extent_x,
):
    moves = (
        (heading, heading_in), (target, target_in), (source, source_in),
        (blocks, blocks_in), (field, field_out),
        (cotan_cube.at[:, 0:8, :], low_c), (cotan_cube.at[:, extent_x - 8 : extent_x, :], high_c),
        (rate_cube.at[:, 0:8, :], low_s), (rate_cube.at[:, extent_x - 8 : extent_x, :], high_s),
        (cotan, cotan_out), (rate_y, rate_y_out),
    )
    copies = [pltpu.make_async_copy(a, b, sems.at[number]) for number, (a, b) in enumerate(moves)]
    for copy in copies:
        copy.start()
    parity_x, parity_y = parities()
    used = jnp.int32(0)
    lane = lanes((8, 128))
    for copy in copies[:4]:
        copy.wait()
    asked = jnp.zeros((8, 128), jnp.int32)
    slots = heading.shape[0]
    for slot in range(slots):
        toward = heading_in[slot]
        across = (toward >= 3).astype(jnp.int32) + (toward >= 6).astype(jnp.int32)
        ex = (across - 1) * (1 - 2 * parity_x)
        ey = (toward - 3 * across - 1) * (1 - 2 * parity_y)
        lx = jnp.where(ex == 0, 2, (ex == 1).astype(jnp.int32))
        ly = jnp.where(ey == 0, 2, (ey == 1).astype(jnp.int32))
        label = ly * 3 + lx
        spot = label * ROUTE_MOST + ((used >> (3 * label)) & 7)
        used = used + (jnp.int32(1) << (3 * label))
        order[0, spot] = slot
        order[1, spot] = source_in[slot]
        asked = jnp.where(lane == spot, target_in[slot], asked)
    for out in (send_a, send_b):
        out[0:8, :] = asked.astype(jnp.float32)
    half = TILE // 2
    for row in range(half):
        flat[pl.ds(row, slots, FLAT), :] = blocks_in[:, row * 128 : (row + 1) * 128].astype(jnp.float32)
    copies[4].wait()
    total = count[0, 0]
    size = 3 * planes
    first_half = lanes((half, 128)) < TILE
    for number, (lx, ly, side) in enumerate(LABELS):
        one = flat[pl.ds(pl.multiple_of(order[0, 2 * number] * FLAT, 8), half), :]
        two = flat[pl.ds(pl.multiple_of(order[0, 2 * number + 1] * FLAT, 8), half), :]
        turned = roll(jnp.where(first_half, two, one), TILE)
        square[number, pl.ds(0, half, 2), :] = jnp.where(first_half, one, 0.0)
        square[number, pl.ds(1, half, 2), :] = jnp.where(first_half, turned, 0.0)
        square[number, pl.ds(TILE, half, 2), :] = jnp.where(first_half, 0.0, turned)
        square[number, pl.ds(TILE + 1, half, 2), :] = jnp.where(first_half, 0.0, two)
        joined = square[number].astype(jnp.bfloat16)
        pairs[number] = joined
        tiles = tile_pair(field_out, order[1, 2 * number], order[1, 2 * number + 1], planes, extent_x)
        picked[number] = tiles
        value = pair_dot(alive_lanes(tiles, order, number, total), joined, 1)
        first = (0 if lx == S else 8 + 2 * size) + (ly * 2 + side) * planes
        (send_a, send_b, value_s)[lx][first : first + planes, :] = value
    even = parity_x == 0
    for copy in copies[5:9]:
        copy.wait()
    for number, (low, high) in enumerate(((low_c, high_c), (low_s, high_s))):
        low = jnp.concatenate([low[:, j, :] for j in range(3)], axis=0)
        high = jnp.concatenate([high[:, 5 + j, :] for j in range(3)], axis=0)
        spot = slice(8 + number * size, 8 + (number + 1) * size)
        send_a[spot, :] = jnp.where(even, low, high)
        send_b[spot, :] = jnp.where(even, high, low)
    high = extent_x - 3
    late_a[...] = edge_rows(field_out, jnp.where(even, 0, high), planes, extent_x)
    late_b[...] = edge_rows(field_out, jnp.where(even, high, 0), planes, extent_x)
    copies[9].wait()
    copies[10].wait()


def local_body(field, cotan, rate_y, packs, early, section, *, planes, extent_x):
    for number, ref in enumerate((rate_y, field, cotan)):
        packs[number * extent_x : (number + 1) * extent_x, :] = edge_pack(ref, planes, extent_x)
    rows = 4 * extent_x
    for chunk, pulled in enumerate(adjoint_y(cotan, rate_y, planes, extent_x)):
        spot = slice(chunk * rows, (chunk + 1) * rows)
        early[spot, :] = 0.5 * cotan[spot, :] + (0.5 * TIME_STEP / 60.0) * pulled
    both = jnp.concatenate(
        [band({k: WEIGHTS[k + 2] for k in range(-2, 3)}, 128), band({k: WEIGHTS[3 - k] for k in range(-1, 4)}, 128)], axis=1
    )
    both = jnp.concatenate([both, both], axis=0)
    first_lane = lanes((rows, 128)) == 0
    for chunk in range(planes // 4):
        spot = slice(chunk * rows, (chunk + 1) * rows)
        parts = mix(jnp.concatenate(split(field[spot, :]), axis=1), both)
        rate_up, rate_down = upwind(rate_y[spot, :])
        flux = rate_up * parts[:, :128] + rate_down * parts[:, 128:]
        change = jnp.where(first_lane, 0.0, roll(flux, 1)) - flux
        section[spot, :] = field[spot, :] + (TIME_STEP / 60.0) * change


def merge_lists(a, b, s):
    group = lax.rem(lanes((8, 128)), 12) // ROUTE_MOST
    return jnp.where(group == 0, a, jnp.where(group == 1, b, s)).astype(jnp.int32)


def to_scalars(value, list_ref, asked, sem):
    list_ref[...] = value
    copy = pltpu.make_async_copy(list_ref, asked, sem)
    copy.start()
    copy.wait()


def serve_body(request, got_b, got_a, cotan_b, cotan, asked, out_a, out_b, out_s, list_ref, sem, *, planes, extent_x):
    to_scalars(merge_lists(got_a[0:8], got_b[0:8], request[0:8]), list_ref, asked, sem)
    serve_tiles(asked, (None, cotan_b, cotan), (out_a, out_b, out_s), planes, extent_x)


def serve_tiles(asked, fields, outs, planes, extent_x):
    for lx, ly, half in LABELS:
        if fields[ly] is not None:
            at = ly * 12 + lx * ROUTE_MOST + 2 * half
            tiles = tile_pair(fields[ly], asked[0, at], asked[0, at + 1], planes, extent_x)
            first = (ly * 2 + half) * planes
            outs[lx][first : first + planes, :] = tiles


def serve_late_body(asked, early_a, early_b, early_s, cotan_a, out_a, out_b, out_s, *, planes, extent_x):
    serve_tiles(asked, (cotan_a, None, None), (out_a, out_b, out_s), planes, extent_x)


def rows_at(ref, first, planes):
    return ref[first : first + planes, :]


def give_back(back, number, scale, order, pairs, field, planes, extent_x):
    pulled = scale * pair_dot(back, pairs[number], 0)
    add_tile_pair(field, order[1, 2 * number], order[1, 2 * number + 1], pulled, planes, extent_x)


def pull_body(
    order, count, early, cotan, cotan_a, cotan_b, rate_x, packs, request, rows_a, rows_b, from_a, from_b, own, pairs,
    grad, edge_rate, asked, pad_rate, returned, list_ref, joined, pad, up_ref, down_ref, sem, *, planes, extent_x,
):
    row = lax.broadcasted_iota(jnp.int32, (8, 128), 0)
    spread = [
        jnp.broadcast_to(merge_lists(a, b, c)[0:1], (8, 128))
        for a, b, c in (
            (from_a[8:16], from_a[16:24], from_a[0:8]),
            (from_b[8:16], from_b[16:24], from_b[0:8]),
            (rows_a[0:8], rows_b[0:8], request[0:8]),
        )
    ]
    list_ref[...] = jnp.where(row == 0, spread[0], jnp.where(row == 1, spread[1], spread[2]))
    copy = pltpu.make_async_copy(list_ref, asked, sem)
    copy.start()
    parity_x, parity_y = parities()
    even_x, even_y = parity_x == 0, parity_y == 0
    size = 3 * planes
    fill_padded(pad, cotan, rows_a[8 : 8 + size], rows_b[8 : 8 + size], even_x, planes, extent_x)
    fill_padded(pad_rate, rate_x, rows_a[8 + size : 8 + 2 * size], rows_b[8 + size : 8 + 2 * size], even_x, planes, extent_x)
    lane = lanes((extent_x, 128))
    upper = jnp.where(even_y, lane, 127 - lane) >= TILE
    for z in range(planes):
        plane = slice(z * extent_x, (z + 1) * extent_x)
        joined[plane, :] = jnp.where(upper, cotan_a[plane, :], cotan_b[plane, :])
    halo = edge_pack(joined, planes, extent_x)
    halo_rate = edge_join(from_a[24 : 24 + extent_x], from_b[24 : 24 + extent_x], even_y)
    edge_rate[...] = halo_rate
    edges = adjoint_edges(part(packs, 2, extent_x), halo, part(packs, 0, extent_x), halo_rate)
    for z in range(planes):
        spot = pl.ds(z * extent_x, extent_x)
        rim = roll(edges, 125 - 8 * z)
        rim = jnp.where((lane < 3) | (lane >= 125), rim, 0.0)
        along_x = adjoint_x(z, pad, pad_rate, up_ref, down_ref, extent_x)
        grad[spot, :] = early[spot, :] + (0.5 * TIME_STEP) * (along_x + rim)
    for number, (lx, ly, half) in enumerate(LABELS):
        if lx == S:
            back = alive_lanes(rows_at(own, (ly * 2 + half) * planes, planes), order, number, count[0, 0])
            returned[number] = back
            give_back(back, number, 0.5 * TIME_STEP, order, pairs, grad, planes, extent_x)
    copy.wait()


def push_body(early, field, pad_rate, edge_rate, rows_a, rows_b, packs, packs_a, packs_b, section, pad, flux_ref, *, planes, extent_x):
    parity_x, parity_y = parities()
    even_x, even_y = parity_x == 0, parity_y == 0
    first = 6 * planes
    fill_padded(pad, field, rows_a[first : first + 3 * planes], rows_b[first : first + 3 * planes], even_x, planes, extent_x)
    second = slice(24 + extent_x, 24 + 2 * extent_x)
    halo = edge_join(packs_a[second], packs_b[second], even_y)
    own_rate = part(packs, 0, extent_x)
    lane8 = lanes(halo.shape) % 8

    def shifted_by(value, k):
        return roll(value, -k) if k else value

    def stencils(value):
        up_part = sum(WEIGHTS[j] * shifted_by(value, j - 2) for j in range(5))
        down_part = sum(WEIGHTS[j] * shifted_by(value, 3 - j) for j in range(5))
        return up_part, down_part

    up_part, down_part = stencils(jnp.where(lane8 < 3, halo, jnp.where(lane8 < 6, part(packs, 1, extent_x), 0.0)))
    rate_up, rate_down = upwind(edge_rate[...])
    flux_low = roll(rate_up * up_part + rate_down * down_part, 1)
    rate_up, rate_down = upwind(own_rate)
    up_part, down_part = stencils(jnp.where((lane8 >= 3) & (lane8 < 6), halo, 0.0))
    flux_high = jnp.where(lane8 < 3, rate_up * up_part + rate_down * down_part, 0.0)
    up_part, down_part = stencils(jnp.where(lane8 < 3, halo, 0.0))
    flux_first = jnp.where((lane8 >= 3) & (lane8 < 5), rate_up * up_part + rate_down * down_part, 0.0)
    change_edge = roll(flux_high, 1) - flux_high
    before = jnp.where(lane8 == 3, flux_low, roll(flux_first, 1))
    change_edge = jnp.where(lane8 < 3, change_edge, jnp.where(lane8 < 6, before - flux_first, 0.0))
    for z in range(planes):
        base = z * PAD
        spot = pl.ds(z * extent_x, extent_x)
        window = extent_x + 8
        near = {k: pad[pl.ds(base + 7 + k, window), :] for k in range(-2, 4)}
        rate_up, rate_down = upwind(pad_rate[pl.ds(base + 7, window), :])
        flux_ref[pl.ds(base, window), :] = rate_up * sum(WEIGHTS[j] * near[j - 2] for j in range(5)) + rate_down * sum(
            WEIGHTS[j] * near[3 - j] for j in range(5)
        )
        change = flux_ref[pl.ds(base, extent_x), :] - flux_ref[pl.ds(base + 1, extent_x), :]
        lane = lanes(change.shape)
        rim = roll(change_edge, 125 - 8 * z)
        rim = jnp.where((lane < 3) | (lane >= 125), rim, 0.0)
        section[spot, :] = early[spot, :] + TIME_STEP * (change + rim)


def compact(packed, low):
    chosen = jnp.where(low, roll(packed, -3), packed)
    half = packed.shape[0] // 2
    return jnp.where(lanes((half, 128)) % 8 < 4, chosen[:half], roll(chosen[half:], 4))


def expand_join(from_a, from_b, even):
    from_a, from_b = (jnp.concatenate([v, roll(v, -4)], axis=0) for v in (from_a, from_b))
    low = jnp.where(even, from_a, from_b)
    high = jnp.where(even, from_b, from_a)
    return jnp.where(lanes(low.shape) % 8 < 3, low, roll(high, 3))


def gather_pair(asked, field, out, first, lx, ly, half, planes, extent_x):
    at = ly * 12 + lx * ROUTE_MOST + 2 * half
    out[first : first + planes, :] = tile_pair(field, asked[ly, at], asked[ly, at + 1], planes, extent_x)


def middle_body(order, asked, count, early, returned_early, pairs, x_a, x_b, grad, returned, send_a, send_b, *, planes, extent_x):
    for number, (lx, ly, half) in enumerate(LABELS):
        if lx != S:
            back = rows_at((x_a, x_b)[lx], (ly * 2 + half) * planes, planes)
            back = alive_lanes(back, order, number, count[0, 0])
            returned[number] = back
            give_back(back, number, 0.5 * TIME_STEP, order, pairs, grad, planes, extent_x)
    for lx, ly, half in LABELS:
        if ly != S:
            gather_pair(asked, grad, (send_a, send_b)[ly], (lx * 2 + half) * planes, lx, ly, half, planes, extent_x)
    packed = edge_pack(grad, planes, extent_x)
    even_y = parities()[1] == 0
    send_a[6 * planes :, :] = compact(packed, even_y)
    send_b[6 * planes :, :] = compact(packed, jnp.logical_not(even_y))


def after_body(asked, grad, own, pack, rows_a, rows_b, *, planes, extent_x):
    pack[...] = edge_pack(grad, planes, extent_x)
    for lx, ly, half in LABELS:
        if ly == S:
            gather_pair(asked, grad, own, (lx * 2 + half) * planes, lx, ly, half, planes, extent_x)
    even_x = parities()[0] == 0
    high = extent_x - 3
    rows_a[...] = edge_rows(grad, jnp.where(even_x, 0, high), planes, extent_x)
    rows_b[...] = edge_rows(grad, jnp.where(even_x, high, 0), planes, extent_x)


def row_back(ly, half, y_a, y_b, own, planes, extent_x):
    if ly == S:
        return rows_at(own, (S * 2 + half) * planes, planes)
    return rows_at((y_a, y_b)[ly], (S * 2 + half) * planes, planes)


def inner_body(
    cotan, grad, pad_rate, rate_y, out, pad, up_ref, down_ref, *, planes, extent_x,
):
    high = 8 + extent_x
    for z in range(planes):
        pad[z * PAD + 8 : z * PAD + high, :] = grad[z * extent_x : (z + 1) * extent_x, :]
    for j in range(3):
        pad[pl.ds(5 + j, planes, PAD), :] = row_of(grad, 0, planes, extent_x)
        pad[pl.ds(high + j, planes, PAD), :] = row_of(grad, extent_x - 1, planes, extent_x)
    along_y = adjoint_y(grad, rate_y, planes, extent_x)
    for z in range(planes):
        spot = pl.ds(z * extent_x, extent_x)
        pulled = along_y[z // 4][z % 4 * extent_x : (z % 4 + 1) * extent_x] * (1.0 / 60.0)
        pulled = pulled + adjoint_x(z, pad, pad_rate, up_ref, down_ref, extent_x)
        out[spot, :] = 0.5 * cotan[spot, :] + grad[spot, :] + TIME_STEP * pulled


def outer(left, right):
    left_high, left_low = split(left)
    right_high, right_low = split(right)
    return lax.dot_general(
        jnp.concatenate([left_high, left_high, left_low], axis=0),
        jnp.concatenate([right_high, right_low, right_high], axis=0),
        (((0,), (0,)), ((), ())),
        preferred_element_type=jnp.float32,
    )


def merge_blocks(value, number, work, blocks):
    work[number] = value
    half = TILE // 2
    half_lane = lanes((half, 128)) < TILE
    even_one, odd_one, even_two, odd_two = (work[number, pl.ds(first, half, 2), :] for first in (0, 1, TILE, TILE + 1))
    turned = roll(jnp.where(half_lane, odd_one, even_two), TILE)
    blocks[2 * number] = jnp.where(half_lane, even_one, turned)
    blocks[2 * number + 1] = jnp.where(half_lane, turned, odd_two)


def start_blocks(number, order, blocks, out_blocks, sems):
    half = TILE // 2
    copies = []
    for which in range(2):
        spot = pl.ds(pl.multiple_of(order[0, 2 * number + which] * half, 8), half)
        copies.append(pltpu.make_async_copy(blocks.at[2 * number + which], out_blocks.at[spot, :], sems.at[2 * number + which]))
        copies[-1].start()
    return copies


def section_body(
    order, asked, early, returned, x_a, x_b, y_a, y_b, value_s, section, first_outer, *, planes, extent_x,
):
    for lx, ly, half in LABELS:
        if ly == S:
            came = rows_at((x_a, x_b, value_s)[lx], (0 if lx == S else 8 + 6 * planes) + (S * 2 + half) * planes, planes)
        else:
            came = rows_at((y_a, y_b)[ly], 24 + 2 * extent_x + ((1, 2, 0)[lx] * 2 + half) * planes, planes)
        at = ly * 12 + lx * ROUTE_MOST + 2 * half
        add_tile_pair(section, asked[ly, at], asked[ly, at + 1], TIME_STEP * came, planes, extent_x)
    for number in range(first_outer.shape[0]):
        found = tile_pair(section, order[1, 2 * number], order[1, 2 * number + 1], planes, extent_x)
        first_outer[number] = outer((0.5 * TIME_STEP) * returned[number], found)


def rest_body(
    order, count, early, edge_rate, packs, pack, y_a, y_b, own, pairs, first_outer, picked, total, blocks, work, *, planes, extent_x,
):
    halo = expand_join(y_a[6 * planes :], y_b[6 * planes :], parities()[1] == 0)
    edges = adjoint_edges(pack[...], halo, part(packs, 0, extent_x), edge_rate[...])
    lane = lanes((extent_x, 128))
    backs = {}
    for number, (lx, ly, half) in enumerate(LABELS):
        if lx == S:
            backs[number] = alive_lanes(row_back(ly, half, y_a, y_b, own, planes, extent_x), order, number, count[0, 0])
            value = first_outer[number] + outer(TIME_STEP * backs[number], picked[number])
            merge_blocks(value, number, work, blocks)
    for z in range(planes):
        spot = pl.ds(z * extent_x, extent_x)
        rim = roll(edges, 125 - 8 * z)
        total[spot, :] = total[spot, :] + TIME_STEP * jnp.where((lane < 3) | (lane >= 125), rim, 0.0)
    for number, back in backs.items():
        give_back(back, number, TIME_STEP, order, pairs, total, planes, extent_x)


def last_body(
    order, count, early, blocks_early, grad, pad_rate, x_b, x_a, pairs, first_outer, picked, out, out_blocks, total, work, blocks, sems,
    *, planes, extent_x,
):
    copies = []
    for number, (lx, _, _) in enumerate(LABELS):
        if lx == S:
            copies += start_blocks(number, order, blocks_early, out_blocks, sems)
    even_x = parities()[0] == 0
    size = 3 * planes
    low_rows = [jnp.where(even_x, x_a[j * planes : (j + 1) * planes], x_b[j * planes : (j + 1) * planes]) for j in range(3)]
    high_rows = [jnp.where(even_x, x_b[j * planes : (j + 1) * planes], x_a[j * planes : (j + 1) * planes]) for j in range(3)]
    first_cell = row_of(grad, 0, planes, extent_x)
    last_cell = row_of(grad, extent_x - 1, planes, extent_x)
    for line, low_face in ((low_rows + [first_cell], -3), ([last_cell] + high_rows, extent_x - 1)):
        faces = []
        for j in range(3):
            rate_up, rate_down = upwind(row_of(pad_rate, 8 + low_face + j, planes, PAD))
            jump = line[j + 1] - line[j]
            faces.append((rate_up * jump, rate_down * jump))
        cells = range(0, 3) if low_face < 0 else range(extent_x - 3, extent_x)
        for cell in cells:
            added = 0.0
            for j in range(3):
                k = low_face + j - cell
                if -3 <= k <= 2:
                    added = added + combine(*faces[j], k)
            spot = pl.ds(cell, planes, extent_x)
            total[spot, :] = total[spot, :] + TIME_STEP * added
    backs = {}
    for number, (lx, ly, half) in enumerate(LABELS):
        if lx != S:
            back = rows_at((x_a, x_b)[lx], size + ((1, 2, 0)[ly] * 2 + half) * planes, planes)
            backs[number] = alive_lanes(back, order, number, count[0, 0])
            give_back(backs[number], number, TIME_STEP, order, pairs, total, planes, extent_x)
    copies.append(pltpu.make_async_copy(total, out, sems.at[2 * len(LABELS)]))
    copies[-1].start()
    for number, back in backs.items():
        merge_blocks(first_outer[number] + outer(TIME_STEP * back, picked[number]), number, work, blocks)
        copies += start_blocks(number, order, blocks, out_blocks, sems)
    for copy in copies:
        copy.wait()


SPACE = {"v": pltpu.VMEM, "s": pltpu.SMEM, "h": pltpu.HBM}


def call(body, ins, outs, scratch=(), alias=None, **sizes):
    values, specs, shapes, out_specs = [], [], [], []
    for kind, group in ins:
        for value in group:
            values.append(value if kind == "r" else pltpu.with_memory_space_constraint(value, SPACE[kind]))
            specs.append(pl.BlockSpec(memory_space=SPACE["s" if kind == "r" else kind]))
    for shape, dtype, kind in outs:
        shapes.append(SPACE[kind](shape, dtype))
        out_specs.append(pl.BlockSpec(memory_space=SPACE[kind]))
    return pl.pallas_call(
        functools.partial(body, **sizes),
        out_shape=tuple(shapes),
        in_specs=specs,
        out_specs=tuple(out_specs),
        scratch_shapes=list(scratch),
        input_output_aliases=alias or {},
        compiler_params=pltpu.CompilerParams(vmem_limit_bytes=VMEM_LIMIT),
        name=body.__name__,
    )(*values)


def shards(
    level_set, speed_x, speed_y, cotangent, blocks, tile_count, source_tile, dest_offset, dest_tile
):
    planes, extent_x, extent_y = level_set.shape
    slots = source_tile.shape[2]
    cells = planes * extent_x
    f32, i32 = jnp.float32, jnp.int32
    field, rate_x, rate_y, cotan = (v.reshape(cells, extent_y) for v in (level_set, speed_x, speed_y, cotangent))
    sizes = dict(planes=planes, extent_x=extent_x)
    size = 3 * planes
    pair_total = slots // 2
    box = ((2 * size, 128), f32, "v")
    padded = ((planes * PAD + 8, extent_y), f32)
    pad_scratch = pltpu.VMEM(*padded)
    whole = ((cells, 128), f32, "v")

    cotan_a = exchange(cotan, "gy", A)
    cotan_b = exchange(cotan, "gy", B)
    head = 8 + 2 * size
    head = 8 + 2 * size
    sent = ((head + 2 * size, 128), f32, "v")
    tall = ((slots * TILE // 2, 128), f32)
    order, send_a, send_b, value_s, late_a, late_b, pairs, picked, field, cotan, rate_y = call(
        begin_body,
        [("h", [v.reshape(slots) for v in (dest_offset, dest_tile, source_tile)] + [field, cotan, rate_y, blocks.reshape(slots, TILE * TILE), cotangent, speed_x]),
         ("r", [tile_count])],
        [((2, slots), i32, "s"), sent, sent, box] + [((size, 128), f32, "v")] * 2
        + [((pair_total, 128, 128), jnp.bfloat16, "v"), ((pair_total, planes, 128), f32, "v")] + [whole] * 3,
        scratch=[pltpu.VMEM((planes, 8, 128), f32)] * 4 + [pltpu.VMEM((slots, TILE * TILE), jnp.bfloat16), pltpu.VMEM((slots * FLAT, 128), f32), pltpu.VMEM((pair_total, 128, 128), f32)]
        + [pltpu.SMEM((slots,), i32)] * 3 + [pltpu.SemaphoreType.DMA((11,))],
        **sizes,
    )
    request = send_a
    rows_a = exchange(send_a, "gx", A)
    rows_b = exchange(send_b, "gx", B)
    packs, early, pushed = call(
        local_body, [("v", [field, cotan, rate_y])], [((3 * extent_x, 128), f32, "v"), whole, whole], **sizes
    )

    def onward(own, a, b, own_first, first, m):
        cut = lambda v, start: v[start + m * 2 * planes : start + (m + 1) * 2 * planes]
        return [cut(own, own_first), cut(a, first), cut(b, first)]

    wide = lambda m: jnp.concatenate(
        [request[:8], rows_a[:8], rows_b[:8], packs[: 2 * extent_x]] + onward(value_s, rows_a, rows_b, 0, head, m), axis=0
    )
    packs_b = exchange(wide(B), "gy", B)
    packs_a = exchange(wide(A), "gy", A)
    column, tiles_a, tiles_b, tiles_s = call(
        serve_body, [("v", [request, rows_b, rows_a, cotan_b, cotan])], [((8, 128), i32, "s"), box, box, box],
        scratch=(pltpu.VMEM((8, 128), i32), pltpu.SemaphoreType.DMA(())), **sizes,
    )
    tiles_a, tiles_b, tiles_s = call(
        serve_late_body, [("s", [column]), ("v", [tiles_a, tiles_b, tiles_s, cotan_a])], [box, box, box], alias={1: 0, 2: 1, 3: 2}, **sizes,
    )
    x_b = exchange(jnp.concatenate([tiles_b, late_b], axis=0), "gx", B)
    x_a = exchange(jnp.concatenate([tiles_a, late_a], axis=0), "gx", A)
    small = ((extent_x, 128), f32, "v")
    eighteen = ((pair_total, planes, 128), f32, "v")
    early, edge_rate, asked, pad_rate, returned = call(
        pull_body,
        [("s", [order]), ("r", [tile_count]),
         ("v", [early, cotan, cotan_a, cotan_b, rate_x, packs, request, rows_a, rows_b, packs_a, packs_b, tiles_s, pairs])],
        [whole, small, ((8, 128), i32, "s"), padded + ("v",), eighteen],
        scratch=(pltpu.VMEM((8, 128), i32), pltpu.VMEM((cells, 128), f32), pad_scratch, pad_scratch, pad_scratch, pltpu.SemaphoreType.DMA(())),
        alias={2: 0}, **sizes,
    )
    grad, returned, send_a, send_b = call(
        middle_body, [("s", [order, asked]), ("r", [tile_count]), ("v", [early, returned, pairs, x_a, x_b])],
        [whole, eighteen] + [((6 * planes + extent_x // 2, 128), f32, "v")] * 2, alias={3: 0, 4: 1}, **sizes,
    )
    send_a, send_b, pushed, grad = lax.optimization_barrier((send_a, send_b, pushed, grad))
    last_y_b = exchange(send_b, "gy", B)
    last_y_a = exchange(send_a, "gy", A)
    own, pack, edge_a, edge_b = call(
        after_body, [("s", [asked]), ("v", [grad])], [box, small] + [((size, 128), f32, "v")] * 2, **sizes,
    )
    (pushed,) = call(
        push_body, [("v", [pushed, field, pad_rate, edge_rate, x_a, x_b, packs, packs_a, packs_b])],
        [whole], scratch=(pad_scratch,) * 2, alias={0: 0}, **sizes,
    )
    last_y_a, last_y_b, pushed = lax.optimization_barrier((last_y_a, last_y_b, pushed))
    last_x_a = exchange(jnp.concatenate([edge_a] + onward(own, last_y_a, last_y_b, 0, 0, A), axis=0), "gx", A)
    last_x_b = exchange(jnp.concatenate([edge_b] + onward(own, last_y_a, last_y_b, 0, 0, B), axis=0), "gx", B)
    (inner,) = call(inner_body, [("v", [cotan, grad, pad_rate, rate_y])], [whole], scratch=(pad_scratch,) * 3, **sizes)
    section, first_outer = call(
        section_body, [("s", [order, asked]), ("v", [pushed, returned, rows_a, rows_b, packs_a, packs_b, value_s])],
        [whole, ((pair_total, 128, 128), f32, "v")], alias={2: 0}, **sizes,
    )
    work = pltpu.VMEM((pair_total, 128, 128), f32)
    blocks_out = pltpu.VMEM((slots, TILE // 2, 128), f32)
    inner, early_blocks = call(
        rest_body,
        [("s", [order]), ("r", [tile_count]), ("v", [inner, edge_rate, packs, pack, last_y_a, last_y_b, own, pairs, first_outer, picked])],
        [whole, ((slots, TILE // 2, 128), f32, "v")], scratch=(work,), alias={2: 0}, **sizes,
    )
    grad_level_set, grad_blocks, _ = call(
        last_body,
        [("s", [order]), ("r", [tile_count]), ("v", [inner, early_blocks, grad, pad_rate, last_x_b, last_x_a, pairs, first_outer, picked])],
        [((cells, 128), f32, "h"), tall + ("h",), whole],
        scratch=(work, blocks_out, pltpu.SemaphoreType.DMA((slots + 1,))), alias={2: 2}, **sizes,
    )
    return (grad_level_set.reshape(planes, extent_x, extent_y), grad_blocks.reshape(1, 1, slots, TILE * TILE))


def solution(mesh):
    return jax.shard_map(
        shards,
        mesh=mesh,
        in_specs=(
            P(None, "gx", "gy"),
            P(None, "gx", "gy"),
            P(None, "gx", "gy"),
            P(None, "gx", "gy"),
            P("gx", "gy", None, None),
            P("gx", "gy"),
            P("gx", "gy", None),
            P("gx", "gy", None),
            P("gx", "gy", None),
        ),
        out_specs=(P(None, "gx", "gy"), P("gx", "gy", None, None)),
        check_vma=False,
    )
```

```python
import functools

import jax
import jax.numpy as jnp
from jax import lax
from jax.experimental import pallas as pl
from jax.experimental.pallas import tpu as pltpu
from jax.sharding import PartitionSpec as P

TILE = 64
ROUTE_MOST = 4
TIME_STEP = 0.3
WEIGHTS = (2.0 / 60.0, -13.0 / 60.0, 47.0 / 60.0, 27.0 / 60.0, -3.0 / 60.0)
PAD = 80
FLAT = 40
VMEM_LIMIT = 16 << 20

A, B, S = 0, 1, 2


def matching(count, which):
    return [(i, (i + (1 if (i % 2 == 0) == (which == B) else -1)) % count) for i in range(count)]


def exchange(block, axis, which):
    return lax.ppermute(block, axis, matching(lax.axis_size(axis), which))


def lanes(shape):
    return lax.broadcasted_iota(jnp.int32, shape, len(shape) - 1)


def roll(value, shift):
    return pltpu.roll(value, shift % 128 if isinstance(shift, int) else shift, axis=value.ndim - 1)


def split(value):
    high = value.astype(jnp.bfloat16)
    return high, (value - high.astype(jnp.float32)).astype(jnp.bfloat16)


def pair_dot(value, matrix, over):
    high, low = split(value)
    both = lax.dot_general(
        jnp.concatenate([high, low], axis=0),
        matrix,
        (((1,), (over,)), ((), ())),
        preferred_element_type=jnp.float32,
    )
    rows = value.shape[0]
    return both[:rows] + both[rows:]


def row_of(ref, x, planes, stride):
    return ref[pl.ds(x, planes, stride), :]


def tile_pair(ref, first, second, planes, extent_x):
    one = row_of(ref, first // 2, planes, extent_x)
    two = row_of(ref, second // 2, planes, extent_x)
    left = lanes(one.shape) < TILE
    turned = roll(jnp.where(left, two, one), TILE)
    return jnp.where(left, jnp.where(first % 2 == 0, one, turned), jnp.where(second % 2 == 1, two, turned))


def add_tile_pair(ref, first, second, value, planes, extent_x):
    lane = lanes(value.shape)
    turned = roll(value, TILE)
    for tile, half in ((first, 0), (second, 1)):
        spot = pl.ds(tile // 2, planes, extent_x)
        placed = jnp.where(tile % 2 == half, value, turned)
        keep = (lane // TILE) == tile % 2
        ref[spot, :] = ref[spot, :] + jnp.where(keep, placed, 0.0)


def edge_pack(ref, planes, extent_x):
    lane = lanes((extent_x, 128))
    packed = jnp.zeros((extent_x, 128), jnp.float32)
    for z in range(planes):
        plane = ref[z * extent_x : (z + 1) * extent_x, :]
        packed = jnp.where(lane // 8 == z, roll(plane, 8 * z + 3), packed)
    return packed


def edge_rows(ref, start, planes, extent_x):
    return jnp.concatenate([row_of(ref, start + j, planes, extent_x) for j in range(3)], axis=0)


def upwind(face_rate):
    return jnp.maximum(face_rate, 0.0), jnp.minimum(face_rate, 0.0)


UP = {2: WEIGHTS[0], 1: WEIGHTS[1], 0: WEIGHTS[2], -1: WEIGHTS[3], -2: WEIGHTS[4]}
DOWN = {1: WEIGHTS[4], 0: WEIGHTS[3], -1: WEIGHTS[2], -2: WEIGHTS[1], -3: WEIGHTS[0]}


def combine(up_part, down_part, k):
    total = 0.0
    if k in UP:
        total = total + UP[k] * up_part
    if k in DOWN:
        total = total + DOWN[k] * down_part
    return total


def fill_padded(pad_ref, field_ref, rows_a, rows_b, even, planes, extent_x):
    high = 8 + extent_x
    at_a = jnp.where(even, 5, high)
    at_b = jnp.where(even, high, 5)
    for z in range(planes):
        pad_ref[z * PAD + 8 : z * PAD + high, :] = field_ref[z * extent_x : (z + 1) * extent_x, :]
    for j in range(3):
        part = slice(j * planes, (j + 1) * planes)
        pad_ref[pl.ds(at_a + j, planes, PAD), :] = rows_a[part]
        pad_ref[pl.ds(at_b + j, planes, PAD), :] = rows_b[part]


def edge_join(from_a, from_b, even):
    low = jnp.where(even, from_a, from_b)
    high = jnp.where(even, from_b, from_a)
    return jnp.where(lanes(low.shape) % 8 < 3, low, high)


def adjoint_edges(own, halo, own_rate, halo_rate):
    lane = lanes(own.shape) % 8
    after = roll(jnp.where(lane == 3, own, halo), -1)
    before = roll(jnp.where(lane == 2, own, halo), 1)
    jump = jnp.where(lane < 3, after - halo, halo - before)
    rate = jnp.where(lane < 3, halo_rate, roll(jnp.where(lane == 2, own_rate, halo_rate), 1))
    rate_up, rate_down = upwind(rate)
    up_part, down_part = rate_up * jump, rate_down * jump
    low_side = 0.0
    high_side = 0.0
    for k in (-1, -2, -3):
        part = jnp.where(lane < 3, combine(up_part, down_part, k), 0.0)
        low_side = low_side + roll(part, -k)
    for k in (0, 1, 2):
        part = jnp.where((lane >= 3) & (lane < 6), combine(up_part, down_part, k), 0.0)
        high_side = high_side + roll(part, -(k + 1))
    return jnp.where(lane < 3, high_side, jnp.where(lane < 6, low_side, 0.0))


def adjoint_x(z, pad_ref, pad_rate_ref, up_ref, down_ref, extent_x):
    base = z * PAD
    here = pad_ref[pl.ds(base, PAD), :]
    jump = pad_ref[pl.ds(base + 1, PAD), :] - here
    rate_up, rate_down = upwind(pad_rate_ref[pl.ds(base, PAD), :])
    up_ref[pl.ds(base, PAD), :] = rate_up * jump
    down_ref[pl.ds(base, PAD), :] = rate_down * jump
    total = 0.0
    for k in range(-3, 3):
        if k in UP:
            total = total + UP[k] * up_ref[pl.ds(base + 8 + k, extent_x), :]
        if k in DOWN:
            total = total + DOWN[k] * down_ref[pl.ds(base + 8 + k, extent_x), :]
    return total


def band(weights, first_lost):
    row = lax.broadcasted_iota(jnp.int32, (128, 128), 0)
    gap = row - lax.broadcasted_iota(jnp.int32, (128, 128), 1)
    matrix = jnp.zeros((128, 128), jnp.float32)
    for k, weight in weights.items():
        matrix = jnp.where(gap == k, float(round(60.0 * weight)), matrix)
    return jnp.where(row >= first_lost, 0.0, matrix).astype(jnp.bfloat16)


def mix(left, matrix):
    return lax.dot_general(left, matrix, (((1,), (0,)), ((), ())), preferred_element_type=jnp.float32)


def adjoint_y(field_ref, rate_y_ref, planes, extent_x):
    up_matrix, down_matrix = band(UP, 127), band(DOWN, 127)
    matrix = jnp.concatenate([up_matrix, up_matrix, down_matrix, down_matrix], axis=0)
    rows = 4 * extent_x
    results = []
    for chunk in range(planes // 4):
        field = field_ref[chunk * rows : (chunk + 1) * rows, :]
        jump = roll(field, -1) - field
        rate_up, rate_down = upwind(rate_y_ref[chunk * rows : (chunk + 1) * rows, :])
        left = jnp.concatenate(split(rate_up * jump) + split(rate_down * jump), axis=1)
        results.append(mix(left, matrix))
    return results


LABELS = [(lx, ly, half) for ly in range(3) for lx in range(3) for half in range(2)]


def parities():
    return lax.rem(lax.axis_index("gx"), 2), lax.rem(lax.axis_index("gy"), 2)


def alive_lanes(value, order, number, total):
    lane = lanes(value.shape)
    return jnp.where(jnp.where(lane < TILE, order[0, 2 * number], order[0, 2 * number + 1]) < total, value, 0.0)


def part(ref, number, extent_x):
    return ref[number * extent_x : (number + 1) * extent_x]


def begin_body(
    heading, target, source, field, cotan, rate_y, blocks, cotan_cube, rate_cube, count,
    order, send_a, send_b, value_s, late_a, late_b, pairs, picked, field_out, cotan_out, rate_y_out,
    low_c, high_c, low_s, high_s, blocks_in, flat, square, heading_in, target_in, source_in, sems, *, planes, extent_x,
):
    moves = (
        (heading, heading_in), (target, target_in), (source, source_in),
        (blocks, blocks_in), (field, field_out),
        (cotan_cube.at[:, 0:8, :], low_c), (cotan_cube.at[:, extent_x - 8 : extent_x, :], high_c),
        (rate_cube.at[:, 0:8, :], low_s), (rate_cube.at[:, extent_x - 8 : extent_x, :], high_s),
        (cotan, cotan_out), (rate_y, rate_y_out),
    )
    copies = [pltpu.make_async_copy(a, b, sems.at[number]) for number, (a, b) in enumerate(moves)]
    for copy in copies:
        copy.start()
    parity_x, parity_y = parities()
    used = jnp.int32(0)
    lane = lanes((8, 128))
    for copy in copies[:4]:
        copy.wait()
    asked = jnp.zeros((8, 128), jnp.int32)
    slots = heading.shape[0]
    for slot in range(slots):
        toward = heading_in[slot]
        across = (toward >= 3).astype(jnp.int32) + (toward >= 6).astype(jnp.int32)
        ex = (across - 1) * (1 - 2 * parity_x)
        ey = (toward - 3 * across - 1) * (1 - 2 * parity_y)
        lx = jnp.where(ex == 0, 2, (ex == 1).astype(jnp.int32))
        ly = jnp.where(ey == 0, 2, (ey == 1).astype(jnp.int32))
        label = ly * 3 + lx
        spot = label * ROUTE_MOST + ((used >> (3 * label)) & 7)
        used = used + (jnp.int32(1) << (3 * label))
        order[0, spot] = slot
        order[1, spot] = source_in[slot]
        asked = jnp.where(lane == spot, target_in[slot], asked)
    for out in (send_a, send_b):
        out[0:8, :] = asked.astype(jnp.float32)
    half = TILE // 2
    for row in range(half):
        flat[pl.ds(row, slots, FLAT), :] = blocks_in[:, row * 128 : (row + 1) * 128].astype(jnp.float32)
    copies[4].wait()
    total = count[0, 0]
    size = 3 * planes
    first_half = lanes((half, 128)) < TILE
    for number, (lx, ly, side) in enumerate(LABELS):
        one = flat[pl.ds(pl.multiple_of(order[0, 2 * number] * FLAT, 8), half), :]
        two = flat[pl.ds(pl.multiple_of(order[0, 2 * number + 1] * FLAT, 8), half), :]
        turned = roll(jnp.where(first_half, two, one), TILE)
        square[number, pl.ds(0, half, 2), :] = jnp.where(first_half, one, 0.0)
        square[number, pl.ds(1, half, 2), :] = jnp.where(first_half, turned, 0.0)
        square[number, pl.ds(TILE, half, 2), :] = jnp.where(first_half, 0.0, turned)
        square[number, pl.ds(TILE + 1, half, 2), :] = jnp.where(first_half, 0.0, two)
        joined = square[number].astype(jnp.bfloat16)
        pairs[number] = joined
        tiles = tile_pair(field_out, order[1, 2 * number], order[1, 2 * number + 1], planes, extent_x)
        picked[number] = tiles
        value = pair_dot(alive_lanes(tiles, order, number, total), joined, 1)
        first = (0 if lx == S else 8 + 2 * size) + (ly * 2 + side) * planes
        (send_a, send_b, value_s)[lx][first : first + planes, :] = value
    even = parity_x == 0
    for copy in copies[5:9]:
        copy.wait()
    for number, (low, high) in enumerate(((low_c, high_c), (low_s, high_s))):
        low = jnp.concatenate([low[:, j, :] for j in range(3)], axis=0)
        high = jnp.concatenate([high[:, 5 + j, :] for j in range(3)], axis=0)
        spot = slice(8 + number * size, 8 + (number + 1) * size)
        send_a[spot, :] = jnp.where(even, low, high)
        send_b[spot, :] = jnp.where(even, high, low)
    high = extent_x - 3
    late_a[...] = edge_rows(field_out, jnp.where(even, 0, high), planes, extent_x)
    late_b[...] = edge_rows(field_out, jnp.where(even, high, 0), planes, extent_x)
    copies[9].wait()
    copies[10].wait()


def local_body(field, cotan, rate_y, packs, early, section, *, planes, extent_x):
    for number, ref in enumerate((rate_y, field, cotan)):
        packs[number * extent_x : (number + 1) * extent_x, :] = edge_pack(ref, planes, extent_x)
    rows = 4 * extent_x
    for chunk, pulled in enumerate(adjoint_y(cotan, rate_y, planes, extent_x)):
        spot = slice(chunk * rows, (chunk + 1) * rows)
        early[spot, :] = 0.5 * cotan[spot, :] + (0.5 * TIME_STEP / 60.0) * pulled
    both = jnp.concatenate(
        [band({k: WEIGHTS[k + 2] for k in range(-2, 3)}, 128), band({k: WEIGHTS[3 - k] for k in range(-1, 4)}, 128)], axis=1
    )
    both = jnp.concatenate([both, both], axis=0)
    first_lane = lanes((rows, 128)) == 0
    for chunk in range(planes // 4):
        spot = slice(chunk * rows, (chunk + 1) * rows)
        parts = mix(jnp.concatenate(split(field[spot, :]), axis=1), both)
        rate_up, rate_down = upwind(rate_y[spot, :])
        flux = rate_up * parts[:, :128] + rate_down * parts[:, 128:]
        change = jnp.where(first_lane, 0.0, roll(flux, 1)) - flux
        section[spot, :] = field[spot, :] + (TIME_STEP / 60.0) * change


def merge_lists(a, b, s):
    group = lax.rem(lanes((8, 128)), 12) // ROUTE_MOST
    return jnp.where(group == 0, a, jnp.where(group == 1, b, s)).astype(jnp.int32)


def to_scalars(value, list_ref, asked, sem):
    list_ref[...] = value
    copy = pltpu.make_async_copy(list_ref, asked, sem)
    copy.start()
    copy.wait()


def serve_body(request, got_b, got_a, cotan_b, cotan, asked, out_a, out_b, out_s, list_ref, sem, *, planes, extent_x):
    to_scalars(merge_lists(got_a[0:8], got_b[0:8], request[0:8]), list_ref, asked, sem)
    serve_tiles(asked, (None, cotan_b, cotan), (out_a, out_b, out_s), planes, extent_x)


def serve_tiles(asked, fields, outs, planes, extent_x):
    for lx, ly, half in LABELS:
        if fields[ly] is not None:
            at = ly * 12 + lx * ROUTE_MOST + 2 * half
            tiles = tile_pair(fields[ly], asked[0, at], asked[0, at + 1], planes, extent_x)
            first = (ly * 2 + half) * planes
            outs[lx][first : first + planes, :] = tiles


def serve_late_body(asked, early_a, early_b, early_s, cotan_a, out_a, out_b, out_s, *, planes, extent_x):
    serve_tiles(asked, (cotan_a, None, None), (out_a, out_b, out_s), planes, extent_x)


def rows_at(ref, first, planes):
    return ref[first : first + planes, :]


def give_back(back, number, scale, order, pairs, field, planes, extent_x):
    pulled = scale * pair_dot(back, pairs[number], 0)
    add_tile_pair(field, order[1, 2 * number], order[1, 2 * number + 1], pulled, planes, extent_x)


def pull_body(
    order, count, early, cotan, cotan_a, cotan_b, rate_x, packs, request, rows_a, rows_b, from_a, from_b, own, pairs,
    grad, edge_rate, asked, pad_rate, returned, list_ref, joined, pad, up_ref, down_ref, sem, *, planes, extent_x,
):
    row = lax.broadcasted_iota(jnp.int32, (8, 128), 0)
    spread = [
        jnp.broadcast_to(merge_lists(a, b, c)[0:1], (8, 128))
        for a, b, c in (
            (from_a[8:16], from_a[16:24], from_a[0:8]),
            (from_b[8:16], from_b[16:24], from_b[0:8]),
            (rows_a[0:8], rows_b[0:8], request[0:8]),
        )
    ]
    list_ref[...] = jnp.where(row == 0, spread[0], jnp.where(row == 1, spread[1], spread[2]))
    copy = pltpu.make_async_copy(list_ref, asked, sem)
    copy.start()
    parity_x, parity_y = parities()
    even_x, even_y = parity_x == 0, parity_y == 0
    size = 3 * planes
    fill_padded(pad, cotan, rows_a[8 : 8 + size], rows_b[8 : 8 + size], even_x, planes, extent_x)
    fill_padded(pad_rate, rate_x, rows_a[8 + size : 8 + 2 * size], rows_b[8 + size : 8 + 2 * size], even_x, planes, extent_x)
    lane = lanes((extent_x, 128))
    upper = jnp.where(even_y, lane, 127 - lane) >= TILE
    for z in range(planes):
        plane = slice(z * extent_x, (z + 1) * extent_x)
        joined[plane, :] = jnp.where(upper, cotan_a[plane, :], cotan_b[plane, :])
    halo = edge_pack(joined, planes, extent_x)
    halo_rate = edge_join(from_a[24 : 24 + extent_x], from_b[24 : 24 + extent_x], even_y)
    edge_rate[...] = halo_rate
    edges = adjoint_edges(part(packs, 2, extent_x), halo, part(packs, 0, extent_x), halo_rate)
    for z in range(planes):
        spot = pl.ds(z * extent_x, extent_x)
        rim = roll(edges, 125 - 8 * z)
        rim = jnp.where((lane < 3) | (lane >= 125), rim, 0.0)
        along_x = adjoint_x(z, pad, pad_rate, up_ref, down_ref, extent_x)
        grad[spot, :] = early[spot, :] + (0.5 * TIME_STEP) * (along_x + rim)
    for number, (lx, ly, half) in enumerate(LABELS):
        if lx == S:
            back = alive_lanes(rows_at(own, (ly * 2 + half) * planes, planes), order, number, count[0, 0])
            returned[number] = back
            give_back(back, number, 0.5 * TIME_STEP, order, pairs, grad, planes, extent_x)
    copy.wait()


def push_body(early, field, pad_rate, edge_rate, rows_a, rows_b, packs, packs_a, packs_b, section, pad, flux_ref, *, planes, extent_x):
    parity_x, parity_y = parities()
    even_x, even_y = parity_x == 0, parity_y == 0
    first = 6 * planes
    fill_padded(pad, field, rows_a[first : first + 3 * planes], rows_b[first : first + 3 * planes], even_x, planes, extent_x)
    second = slice(24 + extent_x, 24 + 2 * extent_x)
    halo = edge_join(packs_a[second], packs_b[second], even_y)
    own_rate = part(packs, 0, extent_x)
    lane8 = lanes(halo.shape) % 8

    def shifted_by(value, k):
        return roll(value, -k) if k else value

    def stencils(value):
        up_part = sum(WEIGHTS[j] * shifted_by(value, j - 2) for j in range(5))
        down_part = sum(WEIGHTS[j] * shifted_by(value, 3 - j) for j in range(5))
        return up_part, down_part

    up_part, down_part = stencils(jnp.where(lane8 < 3, halo, jnp.where(lane8 < 6, part(packs, 1, extent_x), 0.0)))
    rate_up, rate_down = upwind(edge_rate[...])
    flux_low = roll(rate_up * up_part + rate_down * down_part, 1)
    rate_up, rate_down = upwind(own_rate)
    up_part, down_part = stencils(jnp.where((lane8 >= 3) & (lane8 < 6), halo, 0.0))
    flux_high = jnp.where(lane8 < 3, rate_up * up_part + rate_down * down_part, 0.0)
    up_part, down_part = stencils(jnp.where(lane8 < 3, halo, 0.0))
    flux_first = jnp.where((lane8 >= 3) & (lane8 < 5), rate_up * up_part + rate_down * down_part, 0.0)
    change_edge = roll(flux_high, 1) - flux_high
    before = jnp.where(lane8 == 3, flux_low, roll(flux_first, 1))
    change_edge = jnp.where(lane8 < 3, change_edge, jnp.where(lane8 < 6, before - flux_first, 0.0))
    for z in range(planes):
        base = z * PAD
        spot = pl.ds(z * extent_x, extent_x)
        window = extent_x + 8
        near = {k: pad[pl.ds(base + 7 + k, window), :] for k in range(-2, 4)}
        rate_up, rate_down = upwind(pad_rate[pl.ds(base + 7, window), :])
        flux_ref[pl.ds(base, window), :] = rate_up * sum(WEIGHTS[j] * near[j - 2] for j in range(5)) + rate_down * sum(
            WEIGHTS[j] * near[3 - j] for j in range(5)
        )
        change = flux_ref[pl.ds(base, extent_x), :] - flux_ref[pl.ds(base + 1, extent_x), :]
        lane = lanes(change.shape)
        rim = roll(change_edge, 125 - 8 * z)
        rim = jnp.where((lane < 3) | (lane >= 125), rim, 0.0)
        section[spot, :] = early[spot, :] + TIME_STEP * (change + rim)


def compact(packed, low):
    chosen = jnp.where(low, roll(packed, -3), packed)
    half = packed.shape[0] // 2
    return jnp.where(lanes((half, 128)) % 8 < 4, chosen[:half], roll(chosen[half:], 4))


def expand_join(from_a, from_b, even):
    from_a, from_b = (jnp.concatenate([v, roll(v, -4)], axis=0) for v in (from_a, from_b))
    low = jnp.where(even, from_a, from_b)
    high = jnp.where(even, from_b, from_a)
    return jnp.where(lanes(low.shape) % 8 < 3, low, roll(high, 3))


def gather_pair(asked, field, out, first, lx, ly, half, planes, extent_x):
    at = ly * 12 + lx * ROUTE_MOST + 2 * half
    out[first : first + planes, :] = tile_pair(field, asked[ly, at], asked[ly, at + 1], planes, extent_x)


def middle_body(order, asked, count, early, returned_early, pairs, x_a, x_b, grad, returned, send_a, send_b, *, planes, extent_x):
    for number, (lx, ly, half) in enumerate(LABELS):
        if lx != S:
            back = rows_at((x_a, x_b)[lx], (ly * 2 + half) * planes, planes)
            back = alive_lanes(back, order, number, count[0, 0])
            returned[number] = back
            give_back(back, number, 0.5 * TIME_STEP, order, pairs, grad, planes, extent_x)
    for lx, ly, half in LABELS:
        if ly != S:
            gather_pair(asked, grad, (send_a, send_b)[ly], (lx * 2 + half) * planes, lx, ly, half, planes, extent_x)
    packed = edge_pack(grad, planes, extent_x)
    even_y = parities()[1] == 0
    send_a[6 * planes :, :] = compact(packed, even_y)
    send_b[6 * planes :, :] = compact(packed, jnp.logical_not(even_y))


def after_body(asked, grad, own, pack, rows_a, rows_b, *, planes, extent_x):
    pack[...] = edge_pack(grad, planes, extent_x)
    for lx, ly, half in LABELS:
        if ly == S:
            gather_pair(asked, grad, own, (lx * 2 + half) * planes, lx, ly, half, planes, extent_x)
    even_x = parities()[0] == 0
    high = extent_x - 3
    rows_a[...] = edge_rows(grad, jnp.where(even_x, 0, high), planes, extent_x)
    rows_b[...] = edge_rows(grad, jnp.where(even_x, high, 0), planes, extent_x)


def row_back(ly, half, y_a, y_b, own, planes, extent_x):
    if ly == S:
        return rows_at(own, (S * 2 + half) * planes, planes)
    return rows_at((y_a, y_b)[ly], (S * 2 + half) * planes, planes)


def inner_body(
    cotan, grad, pad_rate, rate_y, out, pad, up_ref, down_ref, *, planes, extent_x,
):
    high = 8 + extent_x
    for z in range(planes):
        pad[z * PAD + 8 : z * PAD + high, :] = grad[z * extent_x : (z + 1) * extent_x, :]
    for j in range(3):
        pad[pl.ds(5 + j, planes, PAD), :] = row_of(grad, 0, planes, extent_x)
        pad[pl.ds(high + j, planes, PAD), :] = row_of(grad, extent_x - 1, planes, extent_x)
    along_y = adjoint_y(grad, rate_y, planes, extent_x)
    for z in range(planes):
        spot = pl.ds(z * extent_x, extent_x)
        pulled = along_y[z // 4][z % 4 * extent_x : (z % 4 + 1) * extent_x] * (1.0 / 60.0)
        pulled = pulled + adjoint_x(z, pad, pad_rate, up_ref, down_ref, extent_x)
        out[spot, :] = 0.5 * cotan[spot, :] + grad[spot, :] + TIME_STEP * pulled


def outer(left, right):
    left_high, left_low = split(left)
    right_high, right_low = split(right)
    return lax.dot_general(
        jnp.concatenate([left_high, left_high, left_low], axis=0),
        jnp.concatenate([right_high, right_low, right_high], axis=0),
        (((0,), (0,)), ((), ())),
        preferred_element_type=jnp.float32,
    )


def merge_blocks(value, number, order, work, blocks):
    work[number] = value
    half = TILE // 2
    half_lane = lanes((half, 128)) < TILE
    even_one, odd_one, even_two, odd_two = (work[number, pl.ds(first, half, 2), :] for first in (0, 1, TILE, TILE + 1))
    turned = roll(jnp.where(half_lane, odd_one, even_two), TILE)
    for which, rows in enumerate((jnp.where(half_lane, even_one, turned), jnp.where(half_lane, turned, odd_two))):
        blocks[pl.ds(pl.multiple_of(order[0, 2 * number + which] * half, 8), half), :] = rows


def section_body(
    order, asked, early, returned, x_a, x_b, y_a, y_b, value_s, section, first_outer, *, planes, extent_x,
):
    for lx, ly, half in LABELS:
        if ly == S:
            came = rows_at((x_a, x_b, value_s)[lx], (0 if lx == S else 8 + 6 * planes) + (S * 2 + half) * planes, planes)
        else:
            came = rows_at((y_a, y_b)[ly], 24 + 2 * extent_x + ((1, 2, 0)[lx] * 2 + half) * planes, planes)
        at = ly * 12 + lx * ROUTE_MOST + 2 * half
        add_tile_pair(section, asked[ly, at], asked[ly, at + 1], TIME_STEP * came, planes, extent_x)
    for number in range(first_outer.shape[0]):
        found = tile_pair(section, order[1, 2 * number], order[1, 2 * number + 1], planes, extent_x)
        first_outer[number] = outer((0.5 * TIME_STEP) * returned[number], found)


def rest_body(
    order, count, early, edge_rate, packs, pack, y_a, y_b, own, pairs, first_outer, picked, total, blocks, work, *, planes, extent_x,
):
    halo = expand_join(y_a[6 * planes :], y_b[6 * planes :], parities()[1] == 0)
    edges = adjoint_edges(pack[...], halo, part(packs, 0, extent_x), edge_rate[...])
    lane = lanes((extent_x, 128))
    backs = {}
    for number, (lx, ly, half) in enumerate(LABELS):
        if lx == S:
            backs[number] = alive_lanes(row_back(ly, half, y_a, y_b, own, planes, extent_x), order, number, count[0, 0])
            value = first_outer[number] + outer(TIME_STEP * backs[number], picked[number])
            merge_blocks(value, number, order, work, blocks)
    for z in range(planes):
        spot = pl.ds(z * extent_x, extent_x)
        rim = roll(edges, 125 - 8 * z)
        total[spot, :] = total[spot, :] + TIME_STEP * jnp.where((lane < 3) | (lane >= 125), rim, 0.0)
    for number, back in backs.items():
        give_back(back, number, TIME_STEP, order, pairs, total, planes, extent_x)


def last_body(
    order, count, early, blocks_early, grad, pad_rate, x_b, x_a, pairs, first_outer, picked, out, out_blocks, total, blocks, work, sems,
    *, planes, extent_x,
):
    even_x = parities()[0] == 0
    size = 3 * planes
    low_rows = [jnp.where(even_x, x_a[j * planes : (j + 1) * planes], x_b[j * planes : (j + 1) * planes]) for j in range(3)]
    high_rows = [jnp.where(even_x, x_b[j * planes : (j + 1) * planes], x_a[j * planes : (j + 1) * planes]) for j in range(3)]
    first_cell = row_of(grad, 0, planes, extent_x)
    last_cell = row_of(grad, extent_x - 1, planes, extent_x)
    for line, low_face in ((low_rows + [first_cell], -3), ([last_cell] + high_rows, extent_x - 1)):
        faces = []
        for j in range(3):
            rate_up, rate_down = upwind(row_of(pad_rate, 8 + low_face + j, planes, PAD))
            jump = line[j + 1] - line[j]
            faces.append((rate_up * jump, rate_down * jump))
        cells = range(0, 3) if low_face < 0 else range(extent_x - 3, extent_x)
        for cell in cells:
            added = 0.0
            for j in range(3):
                k = low_face + j - cell
                if -3 <= k <= 2:
                    added = added + combine(*faces[j], k)
            spot = pl.ds(cell, planes, extent_x)
            total[spot, :] = total[spot, :] + TIME_STEP * added
    backs = {}
    for number, (lx, ly, half) in enumerate(LABELS):
        if lx != S:
            back = rows_at((x_a, x_b)[lx], size + ((1, 2, 0)[ly] * 2 + half) * planes, planes)
            backs[number] = alive_lanes(back, order, number, count[0, 0])
            give_back(backs[number], number, TIME_STEP, order, pairs, total, planes, extent_x)
    copies = (pltpu.make_async_copy(total, out, sems.at[0]), pltpu.make_async_copy(blocks, out_blocks, sems.at[1]))
    copies[0].start()
    for number, back in backs.items():
        merge_blocks(first_outer[number] + outer(TIME_STEP * back, picked[number]), number, order, work, blocks)
    copies[1].start()
    for copy in copies:
        copy.wait()


SPACE = {"v": pltpu.VMEM, "s": pltpu.SMEM, "h": pltpu.HBM}


def call(body, ins, outs, scratch=(), alias=None, **sizes):
    values, specs, shapes, out_specs = [], [], [], []
    for kind, group in ins:
        for value in group:
            values.append(value if kind == "r" else pltpu.with_memory_space_constraint(value, SPACE[kind]))
            specs.append(pl.BlockSpec(memory_space=SPACE["s" if kind == "r" else kind]))
    for shape, dtype, kind in outs:
        shapes.append(SPACE[kind](shape, dtype))
        out_specs.append(pl.BlockSpec(memory_space=SPACE[kind]))
    return pl.pallas_call(
        functools.partial(body, **sizes),
        out_shape=tuple(shapes),
        in_specs=specs,
        out_specs=tuple(out_specs),
        scratch_shapes=list(scratch),
        input_output_aliases=alias or {},
        compiler_params=pltpu.CompilerParams(vmem_limit_bytes=VMEM_LIMIT),
        name=body.__name__,
    )(*values)


def shards(
    level_set, speed_x, speed_y, cotangent, blocks, tile_count, source_tile, dest_offset, dest_tile
):
    planes, extent_x, extent_y = level_set.shape
    slots = source_tile.shape[2]
    cells = planes * extent_x
    f32, i32 = jnp.float32, jnp.int32
    field, rate_x, rate_y, cotan = (v.reshape(cells, extent_y) for v in (level_set, speed_x, speed_y, cotangent))
    sizes = dict(planes=planes, extent_x=extent_x)
    size = 3 * planes
    pair_total = slots // 2
    box = ((2 * size, 128), f32, "v")
    padded = ((planes * PAD + 8, extent_y), f32)
    pad_scratch = pltpu.VMEM(*padded)
    whole = ((cells, 128), f32, "v")

    cotan_a = exchange(cotan, "gy", A)
    cotan_b = exchange(cotan, "gy", B)
    head = 8 + 2 * size
    head = 8 + 2 * size
    sent = ((head + 2 * size, 128), f32, "v")
    tall = ((slots * TILE // 2, 128), f32)
    order, send_a, send_b, value_s, late_a, late_b, pairs, picked, field, cotan, rate_y = call(
        begin_body,
        [("h", [v.reshape(slots) for v in (dest_offset, dest_tile, source_tile)] + [field, cotan, rate_y, blocks.reshape(slots, TILE * TILE), cotangent, speed_x]),
         ("r", [tile_count])],
        [((2, slots), i32, "s"), sent, sent, box] + [((size, 128), f32, "v")] * 2
        + [((pair_total, 128, 128), jnp.bfloat16, "v"), ((pair_total, planes, 128), f32, "v")] + [whole] * 3,
        scratch=[pltpu.VMEM((planes, 8, 128), f32)] * 4 + [pltpu.VMEM((slots, TILE * TILE), jnp.bfloat16), pltpu.VMEM((slots * FLAT, 128), f32), pltpu.VMEM((pair_total, 128, 128), f32)]
        + [pltpu.SMEM((slots,), i32)] * 3 + [pltpu.SemaphoreType.DMA((11,))],
        **sizes,
    )
    request = send_a
    rows_a = exchange(send_a, "gx", A)
    rows_b = exchange(send_b, "gx", B)
    packs, early, pushed = call(
        local_body, [("v", [field, cotan, rate_y])], [((3 * extent_x, 128), f32, "v"), whole, whole], **sizes
    )

    def onward(own, a, b, own_first, first, m):
        cut = lambda v, start: v[start + m * 2 * planes : start + (m + 1) * 2 * planes]
        return [cut(own, own_first), cut(a, first), cut(b, first)]

    wide = lambda m: jnp.concatenate(
        [request[:8], rows_a[:8], rows_b[:8], packs[: 2 * extent_x]] + onward(value_s, rows_a, rows_b, 0, head, m), axis=0
    )
    packs_b = exchange(wide(B), "gy", B)
    packs_a = exchange(wide(A), "gy", A)
    column, tiles_a, tiles_b, tiles_s = call(
        serve_body, [("v", [request, rows_b, rows_a, cotan_b, cotan])], [((8, 128), i32, "s"), box, box, box],
        scratch=(pltpu.VMEM((8, 128), i32), pltpu.SemaphoreType.DMA(())), **sizes,
    )
    tiles_a, tiles_b, tiles_s = call(
        serve_late_body, [("s", [column]), ("v", [tiles_a, tiles_b, tiles_s, cotan_a])], [box, box, box], alias={1: 0, 2: 1, 3: 2}, **sizes,
    )
    x_b = exchange(jnp.concatenate([tiles_b, late_b], axis=0), "gx", B)
    x_a = exchange(jnp.concatenate([tiles_a, late_a], axis=0), "gx", A)
    small = ((extent_x, 128), f32, "v")
    eighteen = ((pair_total, planes, 128), f32, "v")
    early, edge_rate, asked, pad_rate, returned = call(
        pull_body,
        [("s", [order]), ("r", [tile_count]),
         ("v", [early, cotan, cotan_a, cotan_b, rate_x, packs, request, rows_a, rows_b, packs_a, packs_b, tiles_s, pairs])],
        [whole, small, ((8, 128), i32, "s"), padded + ("v",), eighteen],
        scratch=(pltpu.VMEM((8, 128), i32), pltpu.VMEM((cells, 128), f32), pad_scratch, pad_scratch, pad_scratch, pltpu.SemaphoreType.DMA(())),
        alias={2: 0}, **sizes,
    )
    grad, returned, send_a, send_b = call(
        middle_body, [("s", [order, asked]), ("r", [tile_count]), ("v", [early, returned, pairs, x_a, x_b])],
        [whole, eighteen] + [((6 * planes + extent_x // 2, 128), f32, "v")] * 2, alias={3: 0, 4: 1}, **sizes,
    )
    send_a, send_b, pushed, grad = lax.optimization_barrier((send_a, send_b, pushed, grad))
    last_y_b = exchange(send_b, "gy", B)
    last_y_a = exchange(send_a, "gy", A)
    own, pack, edge_a, edge_b = call(
        after_body, [("s", [asked]), ("v", [grad])], [box, small] + [((size, 128), f32, "v")] * 2, **sizes,
    )
    (pushed,) = call(
        push_body, [("v", [pushed, field, pad_rate, edge_rate, x_a, x_b, packs, packs_a, packs_b])],
        [whole], scratch=(pad_scratch,) * 2, alias={0: 0}, **sizes,
    )
    last_y_a, last_y_b, pushed = lax.optimization_barrier((last_y_a, last_y_b, pushed))
    last_x_a = exchange(jnp.concatenate([edge_a] + onward(own, last_y_a, last_y_b, 0, 0, A), axis=0), "gx", A)
    last_x_b = exchange(jnp.concatenate([edge_b] + onward(own, last_y_a, last_y_b, 0, 0, B), axis=0), "gx", B)
    (inner,) = call(inner_body, [("v", [cotan, grad, pad_rate, rate_y])], [whole], scratch=(pad_scratch,) * 3, **sizes)
    section, first_outer = call(
        section_body, [("s", [order, asked]), ("v", [pushed, returned, rows_a, rows_b, packs_a, packs_b, value_s])],
        [whole, ((pair_total, 128, 128), f32, "v")], alias={2: 0}, **sizes,
    )
    work = pltpu.VMEM((pair_total, 128, 128), f32)
    inner, early_blocks = call(
        rest_body,
        [("s", [order]), ("r", [tile_count]), ("v", [inner, edge_rate, packs, pack, last_y_a, last_y_b, own, pairs, first_outer, picked])],
        [whole, tall + ("v",)], scratch=(work,), alias={2: 0}, **sizes,
    )
    grad_level_set, grad_blocks, _, _ = call(
        last_body,
        [("s", [order]), ("r", [tile_count]), ("v", [inner, early_blocks, grad, pad_rate, last_x_b, last_x_a, pairs, first_outer, picked])],
        [((cells, 128), f32, "h"), tall + ("h",), whole, tall + ("v",)],
        scratch=(work, pltpu.SemaphoreType.DMA((2,))), alias={2: 2, 3: 3}, **sizes,
    )
    return (grad_level_set.reshape(planes, extent_x, extent_y), grad_blocks.reshape(1, 1, slots, TILE * TILE))


def solution(mesh):
    return jax.shard_map(
        shards,
        mesh=mesh,
        in_specs=(
            P(None, "gx", "gy"),
            P(None, "gx", "gy"),
            P(None, "gx", "gy"),
            P(None, "gx", "gy"),
            P("gx", "gy", None, None),
            P("gx", "gy"),
            P("gx", "gy", None),
            P("gx", "gy", None),
            P("gx", "gy", None),
        ),
        out_specs=(P(None, "gx", "gy"), P("gx", "gy", None, None)),
        check_vma=False,
    )
```
